32 devices in a mesh: dp: 2 (over core), fsdp: 16 (over z, y, x).
Axes of the slice: x: 2, y: 2, z: 4, core: 2. Of those that a mesh axis runs over, the one named last changes fastest.
Arguments:
- features: bfloat16 [128, 784, 320], P(('dp', 'fsdp')), may hold values from -6 to 6
- key_rows: int32 [128], P(('dp', 'fsdp')), may hold values from 7 to 14
- key_cols: int32 [128], P(('dp', 'fsdp')), may hold values from 7 to 14
- out_grad: bfloat16 [128, 196, 512], P(('dp', 'fsdp')), may hold values from -12 to 12
- lower_weights: float32 [1658880], P(('dp', 'fsdp')), may hold values from -4 to 4
- lower_mean: float32 [1658880], P(('dp', 'fsdp')), may hold values from -0.0119474626 to 0.0119474626
- lower_square: float32 [1658880], P(('dp', 'fsdp')), may hold values from 3.9650517e-06 to 0.0002537633
- embed_weights: float32 [1478656], P(('dp', 'fsdp')), may hold values from -4 to 4
- embed_mean: float32 [1478656], P(('dp', 'fsdp')), may hold values from -0.0119474626 to 0.0119474626
- embed_square: float32 [1478656], P(('dp', 'fsdp')), may hold values from 3.9650517e-06 to 0.0002537633
- upper_weights: float32 [3174400], P(('dp', 'fsdp')), may hold values from -4 to 4
- upper_mean: float32 [3174400], P(('dp', 'fsdp')), may hold values from -0.0119474626 to 0.0119474626
- upper_square: float32 [3174400], P(('dp', 'fsdp')), may hold values from 3.9650517e-06 to 0.0002537633
- learn_rate: float32 [1], replicated, may hold values from 0.03 to 0.08
Outputs:
- block_out: float32 [128, 196, 512], P(('dp', 'fsdp'))
- input_grad: float32 [128, 784, 320], P(('dp', 'fsdp'))
- grad_norm: float32 [1], replicated
- lower_grad: float32 [1658880], P(('dp', 'fsdp'))
- lower_new: float32 [1658880], P(('dp', 'fsdp'))
- lower_mean_new: float32 [1658880], P(('dp', 'fsdp'))
- lower_square_new: float32 [1658880], P(('dp', 'fsdp'))
- lower_copy: bfloat16 [1658880], P(('dp', 'fsdp'))
- embed_grad: float32 [1478656], P(('dp', 'fsdp'))
- embed_new: float32 [1478656], P(('dp', 'fsdp'))
- embed_mean_new: float32 [1478656], P(('dp', 'fsdp'))
- embed_square_new: float32 [1478656], P(('dp', 'fsdp'))
- embed_copy: bfloat16 [1478656], P(('dp', 'fsdp'))
- upper_grad: float32 [3174400], P(('dp', 'fsdp'))
- upper_new: float32 [3174400], P(('dp', 'fsdp'))
- upper_mean_new: float32 [3174400], P(('dp', 'fsdp'))
- upper_square_new: float32 [3174400], P(('dp', 'fsdp'))
- upper_copy: bfloat16 [3174400], P(('dp', 'fsdp'))
The draws below stay inside these ranges and needn't reach their ends.
Inputs may be any that keep to these rules, and one draw needn't show every extreme that they name: key_rows and key_cols count valid rows and columns of the 14 x 14 key grid.
All inputs are finite; a program needn't handle non-finite values.
Results may differ from the reference program's by a relative error of at most 0.015.
Values may be sent and summed in bfloat16 or wider, within the bound.
No kernel may reach another device: no remote copies, remote signals or barrier semaphores. Data moves between devices by JAX's collectives and lax.ppermute only.
A program may use at most 448 MiB of HBM per device.

```python
import math
import jax
import jax.numpy as jnp
from jax import lax

D3 = 320
D4 = 512
HID3 = 1280
HID4 = 2048
HEAD = 64
GRID = 28
ADAM_STEP = 2
IMG_DEV = 4
KGRID = 14
TOK3 = 784
TOK4 = 196
IMAGES = 128
N3 = 1656000
NE = 1476736
N4 = 3172352
P3 = 1658880
PE = 1478656
P4 = 3174400


def lower_layout_drawn():
    return [('norm_gain', (D3,)), ('norm_bias', (D3,)), ('query_w', (D3, D3)), ('query_b', (D3,)), ('reduce_w', (4 * D3, D3)), ('reduce_b', (D3,)), ('reduce_gain', (D3,)), ('reduce_bias', (D3,)), ('pair_w', (D3, 2 * D3)), ('value_b', (D3,)), ('output_w', (D3, D3)), ('output_b', (D3,)), ('second_gain', (D3,)), ('second_bias', (D3,)), ('expand_w', (D3, HID3)), ('expand_b', (HID3,)), ('depth_w', (9, HID3)), ('depth_b', (HID3,)), ('shrink_w', (HID3, D3)), ('shrink_b', (D3,))]


def embed_layout_drawn():
    return [('final_gain', (D3,)), ('final_bias', (D3,)), ('patch_w', (9 * D3, D4)), ('patch_b', (D4,)), ('patch_gain', (D4,)), ('patch_bias', (D4,))]


def upper_layout_drawn():
    return [('norm_gain', (D4,)), ('norm_bias', (D4,)), ('query_w', (D4, D4)), ('query_b', (D4,)), ('pair_w', (D4, 2 * D4)), ('value_b', (D4,)), ('output_w', (D4, D4)), ('output_b', (D4,)), ('second_gain', (D4,)), ('second_bias', (D4,)), ('expand_w', (D4, HID4)), ('expand_b', (HID4,)), ('depth_w', (9, HID4)), ('depth_b', (HID4,)), ('shrink_w', (HID4, D4)), ('shrink_b', (D4,))]


def draw_flat(key, layout, padded_length):
    segments = []
    used_count = 0
    for position, (entry_name, entry_shape) in enumerate(layout):
        subkey = jax.random.fold_in(key, position)
        amount = math.prod(entry_shape)
        if entry_name[-2:] == '_w':
            fan_in = entry_shape[0] / 32.0 if entry_name == 'output_w' else float(entry_shape[0])
            segment = jax.random.truncated_normal(subkey, -4.0, 4.0, (amount,), jnp.float32) / math.sqrt(fan_in)
        elif entry_name[-4:] == 'gain':
            segment = jax.random.uniform(subkey, (amount,), jnp.float32, 0.6, 1.4)
        else:
            segment = 0.3 * jax.random.truncated_normal(subkey, -4.0, 4.0, (amount,), jnp.float32)
        segments.append(segment)
        used_count = used_count + amount
    segments.append(0.05 * jax.random.truncated_normal(jax.random.fold_in(key, 999), -4.0, 4.0, (padded_length - used_count,), jnp.float32))
    return jnp.concatenate(segments)


def state_segment(subkey, amount, factor, second):
    if second:
        return factor * factor * jnp.exp(jax.random.uniform(subkey, (amount,), jnp.float32, 0.0, math.log(4.0)))
    magnitude = factor * jnp.exp(jax.random.uniform(subkey, (amount,), jnp.float32, math.log(0.5), math.log(1.5)))
    sign_flip = jnp.where(jax.random.bernoulli(jax.random.fold_in(subkey, 7), 0.5, (amount,)), 1.0, -1.0)
    return magnitude * sign_flip


def draw_state(key, layout, padded_length, second):
    base_scale = 5.0 / math.sqrt(N3 + NE + N4)
    segments = []
    used_count = 0
    for position, (entry_name, entry_shape) in enumerate(layout):
        amount = math.prod(entry_shape)
        factor = base_scale * (1.0 if len(entry_shape) == 2 else 4.0)
        segments.append(state_segment(jax.random.fold_in(key, position), amount, factor, second))
        used_count = used_count + amount
    segments.append(state_segment(jax.random.fold_in(key, 999), padded_length - used_count, base_scale, second))
    return jnp.concatenate(segments)


def draw_lower_weights(key, part):
    return draw_flat(key, lower_layout_drawn(), P3)


def draw_embed_weights(key, part):
    return draw_flat(key, embed_layout_drawn(), PE)


def draw_upper_weights(key, part):
    return draw_flat(key, upper_layout_drawn(), P4)


def draw_lower_mean(key, part):
    return draw_state(key, lower_layout_drawn(), P3, False)


def draw_embed_mean(key, part):
    return draw_state(key, embed_layout_drawn(), PE, False)


def draw_upper_mean(key, part):
    return draw_state(key, upper_layout_drawn(), P4, False)


def draw_lower_square(key, part):
    return draw_state(key, lower_layout_drawn(), P3, True)


def draw_embed_square(key, part):
    return draw_state(key, embed_layout_drawn(), PE, True)


def draw_upper_square(key, part):
    return draw_state(key, upper_layout_drawn(), P4, True)


def set_ends(drawn, stream_key, low, largest):
    shape = drawn.shape
    index_at = [jax.random.randint(jax.random.fold_in(stream_key, axis), (), 0, shape[axis]) for axis in range(len(shape))]
    drawn = drawn.at[tuple(index_at)].set(low)
    longest = shape.index(max(shape))
    index_at[longest] = (index_at[longest] + 1) % shape[longest]
    return drawn.at[tuple(index_at)].set(largest)


def steps_of(rng, extent, cuts, smallest, top_value):
    def one(dim, blocks):
        steps = jax.random.uniform(jax.random.fold_in(jax.random.fold_in(rng, 6), dim), (blocks,), jnp.float32, smallest / len(cuts), top_value / len(cuts))
        return jnp.repeat(jnp.exp(steps), extent[dim] // blocks).reshape((-1,) + (1,) * (len(extent) - dim - 1))

    loudness = one(*cuts[0])
    for cut in cuts[1:]:
        loudness = loudness * one(*cut)
    return loudness


def normal_values(key, extent, width, limit, shards=(), held_as=jnp.bfloat16):
    values = jax.random.normal(key, extent, jnp.float32) * width
    if len(shards) > 0:
        values = steps_of(key, extent, shards, -0.22, 0.18) * values
    return jnp.clip(values, min=-limit, max=limit).astype(held_as)


def setup_inputs(seed: int = 0) -> dict:
    key_of = jax.random.split(jax.random.key(seed), 15)
    return {
        "features": normal_values(key_of[0], (IMAGES, TOK3, D3), 1.0, 6.0, ((0, 32),)),
        "key_rows": set_ends(jax.random.randint(key_of[1], (IMAGES,), KGRID // 2, KGRID + 1), jax.random.fold_in(key_of[1], 1), KGRID // 2, KGRID).astype(jnp.int32),
        "key_cols": set_ends(jax.random.randint(key_of[2], (IMAGES,), KGRID // 2, KGRID + 1), jax.random.fold_in(key_of[2], 1), KGRID // 2, KGRID).astype(jnp.int32),
        "out_grad": normal_values(key_of[3], (IMAGES, TOK4, D4), 2.0, 12.0, ((0, 32),)),
        "lower_weights": draw_lower_weights(jax.random.fold_in(key_of[14], 71), 0),
        "lower_mean": draw_lower_mean(jax.random.fold_in(key_of[14], 71), 0),
        "lower_square": draw_lower_square(jax.random.fold_in(key_of[14], 71), 0),
        "embed_weights": draw_embed_weights(jax.random.fold_in(key_of[14], 71), 0),
        "embed_mean": draw_embed_mean(jax.random.fold_in(key_of[14], 71), 0),
        "embed_square": draw_embed_square(jax.random.fold_in(key_of[14], 71), 0),
        "upper_weights": draw_upper_weights(jax.random.fold_in(key_of[14], 71), 0),
        "upper_mean": draw_upper_mean(jax.random.fold_in(key_of[14], 71), 0),
        "upper_square": draw_upper_square(jax.random.fold_in(key_of[14], 71), 0),
        "learn_rate": jnp.clip(jnp.exp(jax.random.uniform(key_of[13], (1,), jnp.float32, math.log(0.03), math.log(0.08))), 0.03, 0.08),
    }


@jax.custom_vjp
def low(v):
    return lax.optimization_barrier(v.astype(jnp.bfloat16)).astype(jnp.float32)

@jax.custom_vjp
def low_back(v):
    return v

def low_keep(v):
    return (low(v), None)

def low_pass(kept, grad):
    return (grad,)

def back_keep(v):
    return (v, None)

def back_low(kept, grad):
    return (low(grad),)
low.defvjp(low_keep, low_pass)
low_back.defvjp(back_keep, back_low)

def lower_layout():
    return [('norm_gain', (D3,)), ('norm_bias', (D3,)), ('query_w', (D3, D3)), ('query_b', (D3,)), ('reduce_w', (4 * D3, D3)), ('reduce_b', (D3,)), ('reduce_gain', (D3,)), ('reduce_bias', (D3,)), ('pair_w', (D3, 2 * D3)), ('value_b', (D3,)), ('output_w', (D3, D3)), ('output_b', (D3,)), ('second_gain', (D3,)), ('second_bias', (D3,)), ('expand_w', (D3, HID3)), ('expand_b', (HID3,)), ('depth_w', (9, HID3)), ('depth_b', (HID3,)), ('shrink_w', (HID3, D3)), ('shrink_b', (D3,))]

def embed_layout():
    return [('final_gain', (D3,)), ('final_bias', (D3,)), ('patch_w', (9 * D3, D4)), ('patch_b', (D4,)), ('patch_gain', (D4,)), ('patch_bias', (D4,))]

def upper_layout():
    return [('norm_gain', (D4,)), ('norm_bias', (D4,)), ('query_w', (D4, D4)), ('query_b', (D4,)), ('pair_w', (D4, 2 * D4)), ('value_b', (D4,)), ('output_w', (D4, D4)), ('output_b', (D4,)), ('second_gain', (D4,)), ('second_bias', (D4,)), ('expand_w', (D4, HID4)), ('expand_b', (HID4,)), ('depth_w', (9, HID4)), ('depth_b', (HID4,)), ('shrink_w', (HID4, D4)), ('shrink_b', (D4,))]

def unpack_params(flat_params, layout):
    collected = {}
    offset = 0
    for entry_name, entry_shape in layout:
        amount = math.prod(entry_shape)
        collected[entry_name] = flat_params[offset:offset + amount].reshape(entry_shape)
        offset = offset + amount
    return collected

def layer_norm(values, gain_row, bias_row):
    centred = values - lax.optimization_barrier(jnp.mean(values, axis=-1, keepdims=True))
    spread = lax.optimization_barrier(jnp.mean(centred * centred, axis=-1, keepdims=True))
    return centred * lax.rsqrt(spread + 1e-06) * gain_row + bias_row

def multiply(operand, matrix):
    return jnp.matmul(operand, matrix, precision=lax.Precision.HIGHEST)

def key_mask(row_counts, col_counts):
    places = jnp.arange(KGRID * KGRID, dtype=jnp.int32)
    return ((places // KGRID)[None, :] < row_counts[:, None]) & ((places % KGRID)[None, :] < col_counts[:, None])

def patch_pairs(values, grid_side):
    images = values.shape[0]
    channels = values.shape[2]
    half_side = grid_side // 2
    tile_grid = values.reshape(images, half_side, 2, half_side, 2, channels).transpose(0, 1, 3, 2, 4, 5)
    return tile_grid.reshape(images, half_side * half_side, 4 * channels)

def patch_taps(values, grid_side):
    images = values.shape[0]
    channels = values.shape[2]
    half_side = grid_side // 2
    padded = jnp.pad(values.reshape(images, grid_side, grid_side, channels), ((0, 0), (1, 1), (1, 1), (0, 0)))
    tap_list = [padded[:, row_tap:row_tap + grid_side:2, col_tap:col_tap + grid_side:2, :] for row_tap in range(3) for col_tap in range(3)]
    return jnp.concatenate(tap_list, axis=-1).reshape(images, half_side * half_side, 9 * channels)

def depthwise(hidden, kernel, bias_row, grid_side):
    images = hidden.shape[0]
    channels = hidden.shape[2]
    padded = jnp.pad(hidden.reshape(images, grid_side, grid_side, channels), ((0, 0), (1, 1), (1, 1), (0, 0)))
    result = jnp.zeros((images, grid_side, grid_side, channels), jnp.float32)
    for row_tap in range(3):
        for col_tap in range(3):
            result = result + kernel[3 * row_tap + col_tap] * padded[:, row_tap:row_tap + grid_side, col_tap:col_tap + grid_side, :]
    return (result + bias_row).reshape(images, grid_side * grid_side, channels)

def conv_gelu(hidden, kernel, bias_row, grid_side):
    return jax.nn.gelu(depthwise(hidden, kernel, bias_row, grid_side), approximate=False)

def attention(query, keys, values, key_valid, head_count):
    images = query.shape[0]
    queries = query.shape[1]
    channels = query.shape[2]
    key_count = keys.shape[1]
    query_heads = query.reshape(images, queries, head_count, HEAD)
    key_heads = keys.reshape(images, key_count, head_count, HEAD)
    value_heads = values.reshape(images, key_count, head_count, HEAD)
    scores = low_back(jnp.einsum('bnhd,bmhd->bhnm', query_heads, key_heads, precision=lax.Precision.HIGHEST) * 0.125)
    scores = jnp.where(key_valid[:, None, None, :], scores, -1e+30)
    biggest = lax.optimization_barrier(jnp.max(scores, axis=-1, keepdims=True))
    expo = jnp.exp(scores - biggest)
    attention_probs = expo / lax.optimization_barrier(jnp.sum(expo, axis=-1, keepdims=True))
    mixed = jnp.einsum('bhnm,bmhd->bnhd', low(attention_probs), value_heads, precision=lax.Precision.HIGHEST)
    return mixed.reshape(images, queries, channels)

def transformer_block(inputs, params, key_valid, channels, grid_side, has_reduction):
    normed_in = low(layer_norm(inputs, params['norm_gain'], params['norm_bias']))
    query = low(low_back(multiply(normed_in, params['query_w']) + params['query_b']))
    if has_reduction:
        reduced = low_back(multiply(patch_pairs(normed_in, grid_side), params['reduce_w']) + params['reduce_b'])
        source = low(layer_norm(reduced, params['reduce_gain'], params['reduce_bias']))
    else:
        source = normed_in
    value_shift = jnp.concatenate([jnp.zeros_like(params['value_b']), params['value_b']])
    pair = low(low_back(multiply(source, params['pair_w']) + value_shift))
    attended = low(low_back(attention(query, pair[..., :channels], pair[..., channels:], key_valid, channels // HEAD)))
    middle = inputs + low_back(multiply(attended, params['output_w']) + params['output_b'])
    normed_mid = low(layer_norm(middle, params['second_gain'], params['second_bias']))
    hidden = low_back(multiply(normed_mid, params['expand_w']) + params['expand_b'])
    mixed = low(conv_gelu(hidden, params['depth_w'], params['depth_b'], grid_side))
    return middle + low_back(multiply(mixed, params['shrink_w']) + params['shrink_b'])

def embed_section(section_three, params):
    normed_in = low(layer_norm(section_three, params['final_gain'], params['final_bias']))
    embedded = low_back(multiply(patch_taps(normed_in, GRID), params['patch_w']) + params['patch_b'])
    return layer_norm(embedded, params['patch_gain'], params['patch_bias'])

def forward_pass(inputs, lower_flat, embed_flat, upper_flat, key_valid):
    section_three = transformer_block(inputs, unpack_params(low(lower_flat), lower_layout()), key_valid, D3, GRID, True)
    section_four = embed_section(section_three, unpack_params(low(embed_flat), embed_layout()))
    return transformer_block(section_four, unpack_params(low(upper_flat), upper_layout()), key_valid, D4, KGRID, False)

def adamw_update(weights, mean_old, square_old, gradient, clip_factor, rate_value, fix_one):
    clipped = gradient * clip_factor
    mean_new = 0.5 * mean_old + 0.5 * clipped
    square_new = 0.5 * square_old + 0.5 * clipped * clipped
    updated = weights * (1.0 - rate_value * 0.05) - rate_value * (mean_new / fix_one) / (jnp.sqrt(square_new / fix_one) + 1e-08)
    return (updated, mean_new, square_new)

def reference(features, key_rows, key_cols, out_grad, lower_weights, lower_mean, lower_square, embed_weights, embed_mean, embed_square, upper_weights, upper_mean, upper_square, learn_rate):
    groups = IMAGES // IMG_DEV
    feature_groups = features.astype(jnp.float32).reshape(groups, IMG_DEV, TOK3, D3)
    row_groups = key_rows.reshape(groups, IMG_DEV)
    col_groups = key_cols.reshape(groups, IMG_DEV)
    cotangents = out_grad.astype(jnp.float32).reshape(groups, IMG_DEV, TOK4, D4)

    def one_group(carry, item):
        feature_block, row_block, col_block, cot_block = item
        key_valid = key_mask(row_block, col_block)

        def run_forward(inputs, lower_flat, embed_flat, upper_flat):
            return forward_pass(inputs, lower_flat, embed_flat, upper_flat, key_valid)
        result, pullback = jax.vjp(run_forward, feature_block, lower_weights, embed_weights, upper_weights)
        gradient = pullback(cot_block)
        summed = (carry[0] + gradient[1], carry[1] + gradient[2], carry[2] + gradient[3])
        return (summed, (result, gradient[0]))
    start = (jnp.zeros_like(lower_weights), jnp.zeros_like(embed_weights), jnp.zeros_like(upper_weights))
    sums, (results, input_grads) = lax.scan(one_group, start, (feature_groups, row_groups, col_groups, cotangents))
    lower_grad, embed_grad, upper_grad = sums
    squares = jnp.sum(lower_grad * lower_grad) + jnp.sum(embed_grad * embed_grad) + jnp.sum(upper_grad * upper_grad)
    grad_norm = jnp.sqrt(squares)
    clip_factor = jnp.minimum(1.0, 5.0 / (grad_norm + 1e-06))
    rate_value = learn_rate[0]
    fix_one = 1.0 - 0.5 ** ADAM_STEP
    lower_new, lower_mean_new, lower_square_new = adamw_update(lower_weights, lower_mean, lower_square, lower_grad, clip_factor, rate_value, fix_one)
    embed_new, embed_mean_new, embed_square_new = adamw_update(embed_weights, embed_mean, embed_square, embed_grad, clip_factor, rate_value, fix_one)
    upper_new, upper_mean_new, upper_square_new = adamw_update(upper_weights, upper_mean, upper_square, upper_grad, clip_factor, rate_value, fix_one)
    return (results.reshape(IMAGES, TOK4, D4), input_grads.reshape(IMAGES, TOK3, D3), grad_norm.reshape(1), lower_grad, lower_new, lower_mean_new, lower_square_new, lower_new.astype(jnp.bfloat16), embed_grad, embed_new, embed_mean_new, embed_square_new, embed_new.astype(jnp.bfloat16), upper_grad, upper_new, upper_mean_new, upper_square_new, upper_new.astype(jnp.bfloat16))
```

```python
import math

import jax
import jax.numpy as jnp
from jax import lax
from jax.experimental import pallas as pl
from jax.experimental.pallas import tpu as pltpu
from jax.sharding import PartitionSpec as P

D3 = 320
D4 = 512
HID3 = 1280
HID4 = 2048
HEAD = 64
GRID = 28
ADAM_STEP = 2


def lower_layout():
    return [
        ("norm_gain", (D3,)),
        ("norm_bias", (D3,)),
        ("query_w", (D3, D3)),
        ("query_b", (D3,)),
        ("reduce_w", (4 * D3, D3)),
        ("reduce_b", (D3,)),
        ("reduce_gain", (D3,)),
        ("reduce_bias", (D3,)),
        ("pair_w", (D3, 2 * D3)),
        ("value_b", (D3,)),
        ("output_w", (D3, D3)),
        ("output_b", (D3,)),
        ("second_gain", (D3,)),
        ("second_bias", (D3,)),
        ("expand_w", (D3, HID3)),
        ("expand_b", (HID3,)),
        ("depth_w", (9, HID3)),
        ("depth_b", (HID3,)),
        ("shrink_w", (HID3, D3)),
        ("shrink_b", (D3,)),
    ]


def embed_layout():
    return [
        ("final_gain", (D3,)),
        ("final_bias", (D3,)),
        ("patch_w", (9 * D3, D4)),
        ("patch_b", (D4,)),
        ("patch_gain", (D4,)),
        ("patch_bias", (D4,)),
    ]


def upper_layout():
    return [
        ("norm_gain", (D4,)),
        ("norm_bias", (D4,)),
        ("query_w", (D4, D4)),
        ("query_b", (D4,)),
        ("pair_w", (D4, 2 * D4)),
        ("value_b", (D4,)),
        ("output_w", (D4, D4)),
        ("output_b", (D4,)),
        ("second_gain", (D4,)),
        ("second_bias", (D4,)),
        ("expand_w", (D4, HID4)),
        ("expand_b", (HID4,)),
        ("depth_w", (9, HID4)),
        ("depth_b", (HID4,)),
        ("shrink_w", (HID4, D4)),
        ("shrink_b", (D4,)),
    ]


LANES = 128
PAIR_CHUNK = 32


def layout_places(layout):
    places = []
    offset = 0
    for entry_name, entry_shape in layout:
        places.append((entry_name, entry_shape, offset))
        offset = offset + math.prod(entry_shape)
    return places


def is_narrow(entry_shape, offset):
    return entry_shape[-1] % LANES != 0 or offset % LANES != 0


def narrow_ranges(layout):
    ranges = []
    for entry_name, entry_shape, offset in layout_places(layout):
        if not is_narrow(entry_shape, offset):
            continue
        first = offset // D3
        last = first + math.prod(entry_shape) // D3
        if ranges and ranges[-1][1] == first:
            ranges[-1] = (ranges[-1][0], last)
        else:
            ranges.append((first, last))
    return [(first // 2, (last + 1) // 2) for first, last in ranges]


def round_up(amount, unit):
    return (amount + unit - 1) // unit * unit


def for_chunks(first, last, chunk, step):
    full = (last - first) // chunk

    def body(index, carry):
        step(first + index * chunk, chunk)
        return carry

    if full > 0:
        lax.fori_loop(0, full, body, 0)
    rest = (last - first) - full * chunk
    if rest > 0:
        step(first + full * chunk, rest)


def unpack_kernel(layout, shard_rows, shard_count, *refs):
    gathered_ref = refs[0]
    out_refs = refs[1 : 1 + len(layout)]
    dense_ref, narrow_ref = refs[1 + len(layout) :]
    padded_rows = gathered_ref.shape[1]

    def spread(index, carry):
        dense_ref[pl.ds(index * shard_rows, padded_rows), :] = gathered_ref[index].astype(
            jnp.float32
        )
        return carry

    lax.fori_loop(0, shard_count, spread, 0)

    def narrow_step(start, amount):
        parts = [
            dense_ref[pl.ds(5 * start + part, amount, stride=5), :] for part in range(5)
        ]
        low_lanes = lax.broadcasted_iota(jnp.int32, (amount, LANES), 1) < LANES // 2
        turned = [pltpu.roll(part, LANES // 2, 1) for part in parts[2:]]
        even_rows = pl.ds(2 * start, amount, stride=2)
        odd_rows = pl.ds(2 * start + 1, amount, stride=2)
        for part in range(3):
            narrow_ref[part, even_rows, :] = parts[part]
        narrow_ref[0, odd_rows, :] = jnp.where(low_lanes, turned[0], turned[1])
        narrow_ref[1, odd_rows, :] = jnp.where(low_lanes, turned[1], turned[2])
        narrow_ref[2, odd_rows, :] = turned[2]

    for first, last in narrow_ranges(layout):
        for_chunks(first, last, PAIR_CHUNK, narrow_step)

    for out_ref, (entry_name, entry_shape, offset) in zip(out_refs, layout_places(layout)):
        rows = math.prod(entry_shape[:-1])
        cols = entry_shape[-1]
        narrow = is_narrow(entry_shape, offset)

        def copy_rows(start, amount):
            for part in range(-(-cols // LANES)):
                lanes = min(LANES, cols - part * LANES)
                if narrow:
                    piece = narrow_ref[part, pl.ds(offset // D3 + start, amount), :]
                else:
                    stride = cols // LANES
                    base = offset // LANES + part + start * stride
                    piece = dense_ref[pl.ds(base, amount, stride=stride), :]
                out_ref[pl.ds(start, amount), part * LANES : part * LANES + lanes] = piece[
                    :, :lanes
                ].astype(out_ref.dtype)

        if rows < 32:
            copy_rows(0, rows)
        else:
            for_chunks(0, rows, 32, copy_rows)


def unpack_weights(flat_shard, layout, shard_count, matrix_names):
    shard_rows = flat_shard.shape[0] // LANES
    padded_rows = round_up(shard_rows, 16)
    local = jnp.pad(
        flat_shard.reshape(shard_rows, LANES).astype(jnp.bfloat16),
        ((0, padded_rows - shard_rows), (0, 0)),
    )
    gathered = lax.all_gather(local, ("dp", "fsdp"), axis=0, tiled=True)
    gathered = gathered.reshape(shard_count, padded_rows, LANES)
    dense_rows = round_up(shard_rows * shard_count + padded_rows, 16)
    narrow_rows = max([16] + [2 * last for first, last in narrow_ranges(layout)])
    out_shapes = []
    for entry_name, entry_shape in layout:
        kind = jnp.bfloat16 if entry_name in matrix_names else jnp.float32
        shape = entry_shape if len(entry_shape) == 2 else (1,) + entry_shape
        out_shapes.append(jax.ShapeDtypeStruct(shape, kind))
    results = pl.pallas_call(
        lambda *refs: unpack_kernel(layout, shard_rows, shard_count, *refs),
        out_shape=out_shapes,
        scratch_shapes=[
            pltpu.VMEM((dense_rows, LANES), jnp.float32),
            pltpu.VMEM((3, round_up(narrow_rows, 16), LANES), jnp.float32),
        ],
        compiler_params=pltpu.CompilerParams(vmem_limit_bytes=60 * 1024 * 1024),
        name="unpack_weights",
    )(gathered)
    return {entry[0]: result for entry, result in zip(layout, results)}


def pack_kernel(layout, shard_rows, shard_count, *refs):
    in_refs = refs[: len(layout)]
    packed_ref = refs[len(layout)]
    dense_ref, narrow_ref = refs[len(layout) + 1 :]
    padded_rows = packed_ref.shape[1]

    places = layout_places(layout)
    used_rows = (places[-1][2] + math.prod(places[-1][1])) // LANES
    tail = dense_ref.shape[0] - used_rows
    dense_ref[pl.ds(used_rows, tail), :] = jnp.zeros((tail, LANES), jnp.float32)

    for in_ref, (entry_name, entry_shape, offset) in zip(in_refs, places):
        rows = math.prod(entry_shape[:-1])
        cols = entry_shape[-1]
        narrow = is_narrow(entry_shape, offset)

        def copy_rows(start, amount):
            for part in range(-(-cols // LANES)):
                lanes = min(LANES, cols - part * LANES)
                piece = in_ref[pl.ds(start, amount), part * LANES : part * LANES + lanes]
                if narrow:
                    narrow_ref[part, pl.ds(offset // D3 + start, amount), 0:lanes] = piece
                else:
                    stride = cols // LANES
                    base = offset // LANES + part + start * stride
                    dense_ref[pl.ds(base, amount, stride=stride), :] = piece

        if rows < 32:
            copy_rows(0, rows)
        else:
            for_chunks(0, rows, 32, copy_rows)

    if narrow and (offset // D3 + rows) % 2 == 1:
        beyond = offset // D3 + rows
        narrow_ref[:, beyond : beyond + 1, :] = jnp.zeros((3, 1, LANES), jnp.float32)

    def narrow_step(start, amount):
        even_rows = pl.ds(2 * start, amount, stride=2)
        odd_rows = pl.ds(2 * start + 1, amount, stride=2)
        low_lanes = lax.broadcasted_iota(jnp.int32, (amount, LANES), 1) < LANES // 2
        even = [narrow_ref[part, even_rows, :] for part in range(3)]
        odd = [pltpu.roll(narrow_ref[part, odd_rows, :], LANES // 2, 1) for part in range(3)]
        joined = [
            even[0],
            even[1],
            jnp.where(low_lanes, even[2], odd[0]),
            jnp.where(low_lanes, odd[0], odd[1]),
            jnp.where(low_lanes, odd[1], odd[2]),
        ]
        for part in range(5):
            dense_ref[pl.ds(5 * start + part, amount, stride=5), :] = joined[part]

    for first, last in narrow_ranges(layout):
        for_chunks(first, last, PAIR_CHUNK, narrow_step)

    def cut(index, carry):
        packed_ref[index] = dense_ref[pl.ds(index * shard_rows, padded_rows), :].astype(
            packed_ref.dtype
        )
        return carry

    lax.fori_loop(0, shard_count, cut, 0)


def reduce_grads(collected, layout, shard_rows, shard_count):
    padded_rows = round_up(shard_rows, 16)
    dense_rows = round_up(shard_rows * shard_count + padded_rows, 16)
    narrow_rows = max([16] + [2 * last for first, last in narrow_ranges(layout)])
    operands = []
    for entry_name, entry_shape in layout:
        shape = entry_shape if len(entry_shape) == 2 else (1,) + entry_shape
        operands.append(collected[entry_name].reshape(shape))
    packed = pl.pallas_call(
        lambda *refs: pack_kernel(layout, shard_rows, shard_count, *refs),
        out_shape=jax.ShapeDtypeStruct((shard_count, padded_rows, LANES), WIRE_TYPE),
        scratch_shapes=[
            pltpu.VMEM((dense_rows, LANES), jnp.float32),
            pltpu.VMEM((3, round_up(narrow_rows, 16), LANES), jnp.float32),
        ],
        compiler_params=pltpu.CompilerParams(vmem_limit_bytes=60 * 1024 * 1024),
        name="pack_grads",
    )(*operands)
    summed = packed.reshape(shard_count * padded_rows, LANES)
    for axis in ("dp", "fsdp"):
        summed = lax.psum_scatter(summed, axis, scatter_dimension=0, tiled=True)
    return summed[:shard_rows].astype(jnp.float32).reshape(-1)


WIRE_TYPE = jnp.bfloat16
MATRIX_NAMES = (
    "query_w",
    "reduce_w",
    "pair_w",
    "output_w",
    "expand_w",
    "shrink_w",
    "patch_w",
)


def to_float(values):
    return values.astype(jnp.float32)


def as_row(values):
    return values.reshape(-1)


def layer_norm(values, gain_row, bias_row):
    centred = values - jnp.mean(values, axis=-1, keepdims=True)
    spread = jnp.mean(centred * centred, axis=-1, keepdims=True)
    return centred * lax.rsqrt(spread + 1e-06) * gain_row + bias_row


def norm_back(values, gain_row, bias_row, gradient):
    result, pullback = jax.vjp(layer_norm, values, gain_row, bias_row)
    return pullback(gradient)


def product(operand, matrix):
    return jnp.einsum("bni,ij->bnj", operand, matrix, preferred_element_type=jnp.float32)


def product_back(gradient, matrix):
    return jnp.einsum("bnj,ij->bni", gradient, matrix, preferred_element_type=jnp.float32)


def weight_grad(operand, gradient):
    return jnp.einsum("bni,bnj->ij", operand, gradient, preferred_element_type=jnp.float32)


def column_sum(gradient):
    return jnp.sum(gradient.astype(jnp.float32), axis=(0, 1))


def key_mask(row_counts, col_counts):
    side_keys = GRID // 2
    places = jnp.arange(side_keys * side_keys, dtype=jnp.int32)
    return ((places // side_keys)[None, :] < row_counts[:, None]) & (
        (places % side_keys)[None, :] < col_counts[:, None]
    )


def patch_pairs(values, grid_side):
    images = values.shape[0]
    channels = values.shape[2]
    half_side = grid_side // 2
    tile_grid = values.reshape(images, half_side, 2, half_side, 2, channels).transpose(
        0, 1, 3, 2, 4, 5
    )
    return tile_grid.reshape(images, half_side * half_side, 4 * channels)


def pairs_back(gradient, grid_side):
    images = gradient.shape[0]
    channels = gradient.shape[2] // 4
    half_side = grid_side // 2
    tile_grid = gradient.reshape(images, half_side, half_side, 2, 2, channels).transpose(
        0, 1, 3, 2, 4, 5
    )
    return tile_grid.reshape(images, grid_side * grid_side, channels)


def patch_taps(values, grid_side):
    images = values.shape[0]
    channels = values.shape[2]
    half_side = grid_side // 2
    padded = jnp.pad(
        values.reshape(images, grid_side, grid_side, channels), ((0, 0), (1, 1), (1, 1), (0, 0))
    )
    tap_list = [
        padded[:, row_tap : row_tap + grid_side : 2, col_tap : col_tap + grid_side : 2, :]
        for row_tap in range(3)
        for col_tap in range(3)
    ]
    return jnp.concatenate(tap_list, axis=-1).reshape(images, half_side * half_side, 9 * channels)


def depthwise(hidden, kernel, bias_row, grid_side):
    images = hidden.shape[0]
    channels = hidden.shape[2]
    padded = jnp.pad(
        hidden.reshape(images, grid_side, grid_side, channels), ((0, 0), (1, 1), (1, 1), (0, 0))
    )
    result = jnp.zeros((images, grid_side, grid_side, channels), jnp.float32)
    for row_tap in range(3):
        for col_tap in range(3):
            result = (
                result
                + kernel[3 * row_tap + col_tap]
                * padded[:, row_tap : row_tap + grid_side, col_tap : col_tap + grid_side, :]
            )
    return (result + bias_row).reshape(images, grid_side * grid_side, channels)


def conv_gelu(hidden, kernel, bias_row, grid_side):
    return jax.nn.gelu(depthwise(hidden, kernel, bias_row, grid_side), approximate=False)


def split_heads(values, head_count):
    return values.reshape(values.shape[0], values.shape[1], head_count, HEAD)


def score_block(query_heads, key_heads, key_valid):
    scores = (
        jnp.einsum("bnhd,bmhd->bhnm", query_heads, key_heads, preferred_element_type=jnp.float32)
        * 0.125
    )
    return jnp.where(key_valid[:, None, None, :], scores, -1e30)


def attend_forward(query, keys, values, key_valid, head_count):
    scores = score_block(split_heads(query, head_count), split_heads(keys, head_count), key_valid)
    biggest = jnp.max(scores, axis=-1, keepdims=True)
    log_total = biggest + jnp.log(jnp.sum(jnp.exp(scores - biggest), axis=-1, keepdims=True))
    attention_probs = jnp.exp(scores - log_total).astype(jnp.bfloat16)
    mixed = jnp.einsum(
        "bhnm,bmhd->bnhd",
        attention_probs,
        split_heads(values, head_count),
        preferred_element_type=jnp.float32,
    )
    return (mixed.reshape(query.shape), log_total)


def attend_backward(query, keys, values, key_valid, log_total, grad_out, head_count):
    query_heads = split_heads(query, head_count)
    key_heads = split_heads(keys, head_count)
    grad_heads = split_heads(grad_out, head_count)
    attention_probs = jnp.exp(score_block(query_heads, key_heads, key_valid) - log_total)
    prob_grad = jnp.einsum(
        "bnhd,bmhd->bhnm",
        grad_heads,
        split_heads(values, head_count),
        preferred_element_type=jnp.float32,
    )
    value_grad = jnp.einsum(
        "bhnm,bnhd->bmhd",
        attention_probs.astype(jnp.bfloat16),
        grad_heads,
        preferred_element_type=jnp.float32,
    )
    score_grad = attention_probs * (
        prob_grad - jnp.sum(attention_probs * prob_grad, axis=-1, keepdims=True)
    )
    score_grad = score_grad.astype(jnp.bfloat16)
    query_grad = (
        jnp.einsum("bhnm,bmhd->bnhd", score_grad, key_heads, preferred_element_type=jnp.float32)
        * 0.125
    )
    key_grad = (
        jnp.einsum("bhnm,bnhd->bmhd", score_grad, query_heads, preferred_element_type=jnp.float32)
        * 0.125
    )
    return (
        query_grad.reshape(query.shape),
        key_grad.reshape(keys.shape),
        value_grad.reshape(values.shape),
    )


def block_forward(inputs, params, key_valid, channels, grid_side, has_reduction):
    head_count = channels // HEAD
    normed_in = layer_norm(
        inputs, as_row(params["norm_gain"]), as_row(params["norm_bias"])
    ).astype(jnp.bfloat16)
    query = (product(normed_in, params["query_w"]) + as_row(params["query_b"])).astype(
        jnp.bfloat16
    )
    if has_reduction:
        reduced = product(patch_pairs(normed_in, grid_side), params["reduce_w"]) + as_row(params["reduce_b"])
        source = layer_norm(
            reduced, as_row(params["reduce_gain"]), as_row(params["reduce_bias"])
        ).astype(jnp.bfloat16)
    else:
        reduced = None
        source = normed_in
    value_shift = jnp.concatenate(
        [jnp.zeros((channels,), jnp.float32), as_row(params["value_b"])]
    )
    pair = (product(source, params["pair_w"]) + value_shift).astype(jnp.bfloat16)
    attended, log_total = attend_forward(
        query, pair[..., :channels], pair[..., channels:], key_valid, head_count
    )
    attended = attended.astype(jnp.bfloat16)
    middle = inputs + (product(attended, params["output_w"]) + as_row(params["output_b"]))
    normed_mid = layer_norm(
        middle, as_row(params["second_gain"]), as_row(params["second_bias"])
    ).astype(jnp.bfloat16)
    hidden = product(normed_mid, params["expand_w"]) + as_row(params["expand_b"])
    mixed = conv_gelu(
        hidden, params["depth_w"], as_row(params["depth_b"]), grid_side
    ).astype(jnp.bfloat16)
    result = middle + (product(mixed, params["shrink_w"]) + as_row(params["shrink_b"]))
    saved_state = (
        inputs,
        normed_in,
        query,
        reduced,
        source,
        pair,
        log_total,
        attended,
        middle,
        normed_mid,
        hidden,
        mixed,
    )
    return (result, saved_state)


def block_backward(gradient, saved_state, params, key_valid, channels, grid_side, has_reduction):
    (
        inputs,
        normed_in,
        query,
        reduced,
        source,
        pair,
        log_total,
        attended,
        middle,
        normed_mid,
        hidden,
        mixed,
    ) = saved_state
    head_count = channels // HEAD
    collected = {}
    branch_grad = gradient.astype(jnp.bfloat16)
    collected["shrink_w"] = weight_grad(mixed, branch_grad)
    collected["shrink_b"] = column_sum(branch_grad)
    mixed_grad = product_back(branch_grad, params["shrink_w"])

    def conv_part(hidden_in, kernel, bias_row):
        return conv_gelu(hidden_in, kernel, bias_row, grid_side)

    conv_result, conv_pull = jax.vjp(
        conv_part, hidden, params["depth_w"], as_row(params["depth_b"])
    )
    hidden_grad, collected["depth_w"], collected["depth_b"] = conv_pull(mixed_grad)
    hidden_grad = hidden_grad.astype(jnp.bfloat16)
    collected["expand_w"] = weight_grad(normed_mid, hidden_grad)
    collected["expand_b"] = column_sum(hidden_grad)
    mid_norm_grad = product_back(hidden_grad, params["expand_w"])
    mid_grad, collected["second_gain"], collected["second_bias"] = norm_back(
        middle, as_row(params["second_gain"]), as_row(params["second_bias"]), mid_norm_grad
    )
    mid_grad = gradient + mid_grad
    output_grad = mid_grad.astype(jnp.bfloat16)
    collected["output_w"] = weight_grad(attended, output_grad)
    collected["output_b"] = column_sum(output_grad)
    attended_grad = product_back(output_grad, params["output_w"]).astype(jnp.bfloat16)
    query_grad, key_grad, value_grad = attend_backward(
        query,
        pair[..., :channels],
        pair[..., channels:],
        key_valid,
        log_total,
        attended_grad,
        head_count,
    )
    query_grad = query_grad.astype(jnp.bfloat16)
    collected["query_w"] = weight_grad(normed_in, query_grad)
    collected["query_b"] = column_sum(query_grad)
    normed_grad = product_back(query_grad, params["query_w"])
    pair_grad = jnp.concatenate([key_grad, value_grad], axis=-1).astype(jnp.bfloat16)
    collected["pair_w"] = weight_grad(source, pair_grad)
    collected["value_b"] = column_sum(pair_grad[..., channels:])
    source_grad = product_back(pair_grad, params["pair_w"])
    if has_reduction:
        reduced_grad, collected["reduce_gain"], collected["reduce_bias"] = norm_back(
            reduced, as_row(params["reduce_gain"]), as_row(params["reduce_bias"]), source_grad
        )
        reduced_grad = reduced_grad.astype(jnp.bfloat16)
        collected["reduce_w"] = weight_grad(patch_pairs(normed_in, grid_side), reduced_grad)
        collected["reduce_b"] = column_sum(reduced_grad)
        normed_grad = normed_grad + pairs_back(
            product_back(reduced_grad, params["reduce_w"]), grid_side
        )
    else:
        normed_grad = normed_grad + source_grad
    input_part, collected["norm_gain"], collected["norm_bias"] = norm_back(
        inputs, as_row(params["norm_gain"]), as_row(params["norm_bias"]), normed_grad
    )
    return (mid_grad + input_part, collected)


def embed_forward(section_three, params):
    normed_in = layer_norm(
        section_three, as_row(params["final_gain"]), as_row(params["final_bias"])
    ).astype(jnp.bfloat16)
    tap_rows = patch_taps(normed_in, GRID)
    embedded = product(tap_rows, params["patch_w"]) + as_row(params["patch_b"])
    result = layer_norm(embedded, as_row(params["patch_gain"]), as_row(params["patch_bias"]))
    return (result, (section_three, tap_rows, embedded))


def embed_backward(gradient, saved_state, params):
    section_three, tap_rows, embedded = saved_state
    collected = {}
    embed_grad, collected["patch_gain"], collected["patch_bias"] = norm_back(
        embedded, as_row(params["patch_gain"]), as_row(params["patch_bias"]), gradient
    )
    embed_grad = embed_grad.astype(jnp.bfloat16)
    collected["patch_w"] = weight_grad(tap_rows, embed_grad)
    collected["patch_b"] = column_sum(embed_grad)
    tap_grad = product_back(embed_grad, params["patch_w"])

    def taps_only(values):
        return patch_taps(values, GRID)

    tap_result, tap_pull = jax.vjp(taps_only, section_three)
    normed_grad = tap_pull(tap_grad)[0]
    three_grad, collected["final_gain"], collected["final_bias"] = norm_back(
        section_three, as_row(params["final_gain"]), as_row(params["final_bias"]), normed_grad
    )
    return (three_grad, collected)


def adamw_update(weights, mean_old, square_old, gradient, clip_factor, rate_value, fix_one):
    clipped = gradient * clip_factor
    mean_new = 0.5 * mean_old + 0.5 * clipped
    square_new = 0.5 * square_old + 0.5 * clipped * clipped
    updated = weights * (1.0 - rate_value * 0.05) - rate_value * (mean_new / fix_one) / (
        jnp.sqrt(square_new / fix_one) + 1e-08
    )
    return (updated, mean_new, square_new)


def shards(
    features,
    key_rows,
    key_cols,
    out_grad,
    lower_weights,
    lower_mean,
    lower_square,
    embed_weights,
    embed_mean,
    embed_square,
    upper_weights,
    upper_mean,
    upper_square,
    learn_rate,
):
    key_valid = key_mask(key_rows, key_cols)
    side_four = GRID // 2
    shard_count = lax.axis_size("dp") * lax.axis_size("fsdp")
    lower_params = unpack_weights(lower_weights, lower_layout(), shard_count, MATRIX_NAMES)
    embed_params = unpack_weights(embed_weights, embed_layout(), shard_count, MATRIX_NAMES)
    upper_params = unpack_weights(upper_weights, upper_layout(), shard_count, MATRIX_NAMES)
    section_three, lower_saved = block_forward(
        to_float(features), lower_params, key_valid, D3, GRID, True
    )
    section_four, embed_saved = embed_forward(section_three, embed_params)
    block_out, upper_saved = block_forward(
        section_four, upper_params, key_valid, D4, side_four, False
    )
    four_grad, upper_found = block_backward(
        to_float(out_grad), upper_saved, upper_params, key_valid, D4, side_four, False
    )
    upper_grad = reduce_grads(
        upper_found, upper_layout(), upper_weights.shape[0] // LANES, shard_count
    )
    three_grad, embed_found = embed_backward(four_grad, embed_saved, embed_params)
    embed_grad = reduce_grads(
        embed_found, embed_layout(), embed_weights.shape[0] // LANES, shard_count
    )
    input_grad, lower_found = block_backward(
        three_grad, lower_saved, lower_params, key_valid, D3, GRID, True
    )
    lower_grad = reduce_grads(
        lower_found, lower_layout(), lower_weights.shape[0] // LANES, shard_count
    )
    local_squares = (
        jnp.sum(lower_grad * lower_grad)
        + jnp.sum(embed_grad * embed_grad)
        + jnp.sum(upper_grad * upper_grad)
    )
    squares = lax.psum(local_squares, ("dp", "fsdp"))
    grad_norm = jnp.sqrt(squares)
    clip_factor = jnp.minimum(1.0, 5.0 / (grad_norm + 1e-06))
    rate_value = learn_rate[0]
    fix_one = 1.0 - 0.5**ADAM_STEP
    lower_new, lower_mean_new, lower_square_new = adamw_update(
        lower_weights, lower_mean, lower_square, lower_grad, clip_factor, rate_value, fix_one
    )
    embed_new, embed_mean_new, embed_square_new = adamw_update(
        embed_weights, embed_mean, embed_square, embed_grad, clip_factor, rate_value, fix_one
    )
    upper_new, upper_mean_new, upper_square_new = adamw_update(
        upper_weights, upper_mean, upper_square, upper_grad, clip_factor, rate_value, fix_one
    )
    return (
        block_out,
        input_grad,
        grad_norm.reshape(1),
        lower_grad,
        lower_new,
        lower_mean_new,
        lower_square_new,
        lower_new.astype(jnp.bfloat16),
        embed_grad,
        embed_new,
        embed_mean_new,
        embed_square_new,
        embed_new.astype(jnp.bfloat16),
        upper_grad,
        upper_new,
        upper_mean_new,
        upper_square_new,
        upper_new.astype(jnp.bfloat16),
    )


def solution(mesh):
    return jax.shard_map(
        shards,
        mesh=mesh,
        in_specs=(
            P(("dp", "fsdp"), None, None),
            P(("dp", "fsdp")),
            P(("dp", "fsdp")),
            P(("dp", "fsdp"), None, None),
            P(("dp", "fsdp")),
            P(("dp", "fsdp")),
            P(("dp", "fsdp")),
            P(("dp", "fsdp")),
            P(("dp", "fsdp")),
            P(("dp", "fsdp")),
            P(("dp", "fsdp")),
            P(("dp", "fsdp")),
            P(("dp", "fsdp")),
            P(),
        ),
        out_specs=(
            P(("dp", "fsdp"), None, None),
            P(("dp", "fsdp"), None, None),
            P(),
            P(("dp", "fsdp")),
            P(("dp", "fsdp")),
            P(("dp", "fsdp")),
            P(("dp", "fsdp")),
            P(("dp", "fsdp")),
            P(("dp", "fsdp")),
            P(("dp", "fsdp")),
            P(("dp", "fsdp")),
            P(("dp", "fsdp")),
            P(("dp", "fsdp")),
            P(("dp", "fsdp")),
            P(("dp", "fsdp")),
            P(("dp", "fsdp")),
            P(("dp", "fsdp")),
            P(("dp", "fsdp")),
        ),
        check_vma=False,
    )
```

```python
import math

import jax
import jax.numpy as jnp
from jax import lax
from jax.experimental import pallas as pl
from jax.experimental.pallas import tpu as pltpu
from jax.sharding import PartitionSpec as P

D3 = 320
D4 = 512
HID3 = 1280
HID4 = 2048
HEAD = 64
GRID = 28
ADAM_STEP = 2
WIRE_TYPE = jnp.bfloat16


def block_layout(channels, units, has_reduction):
    row = (channels,)
    reduction = [(4 * channels, channels), row, row, row] if has_reduction else []
    return (
        [row, row, (channels, channels), row]
        + reduction
        + [(channels, 2 * channels), row, (channels, channels), row, row, row]
        + [(channels, units), (units,), (9, units), (units,), (units, channels), row]
    )


LOWER_LAYOUT = block_layout(D3, HID3, True)
UPPER_LAYOUT = block_layout(D4, HID4, False)
EMBED_LAYOUT = [(D3,), (D3,), (9 * D3, D4), (D4,), (D4,), (D4,)]


LANES = 128
PAIR_CHUNK = 32


def layout_places(layout):
    places = []
    offset = 0
    for entry_shape in layout:
        places.append((entry_shape, offset))
        offset = offset + math.prod(entry_shape)
    return places


def is_narrow(entry_shape, offset):
    return entry_shape[-1] % LANES != 0 or offset % LANES != 0


def narrow_ranges(layout):
    ranges = []
    for entry_shape, offset in layout_places(layout):
        if not is_narrow(entry_shape, offset):
            continue
        first = offset // D3
        last = first + math.prod(entry_shape) // D3
        if ranges and ranges[-1][1] == first:
            ranges[-1] = (ranges[-1][0], last)
        else:
            ranges.append((first, last))
    return [(first // 2, (last + 1) // 2) for first, last in ranges]


def round_up(amount, unit):
    return (amount + unit - 1) // unit * unit


def for_chunks(first, last, chunk, step):
    full = (last - first) // chunk

    def body(index, carry):
        step(first + index * chunk, chunk)
        return carry

    if full > 0:
        lax.fori_loop(0, full, body, 0)
    rest = (last - first) - full * chunk
    if rest > 0:
        step(first + full * chunk, rest)


def unpack_kernel(layout, shard_rows, shard_count, *refs):
    gathered_ref = refs[0]
    out_refs = refs[1 : 1 + len(layout)]
    dense_ref, narrow_ref = refs[1 + len(layout) :]
    padded_rows = gathered_ref.shape[1]

    def spread(index, carry):
        dense_ref[pl.ds(index * shard_rows, padded_rows), :] = gathered_ref[index].astype(
            jnp.float32
        )
        return carry

    lax.fori_loop(0, shard_count, spread, 0)

    def narrow_step(start, amount):
        parts = [
            dense_ref[pl.ds(5 * start + part, amount, stride=5), :] for part in range(5)
        ]
        low_lanes = lax.broadcasted_iota(jnp.int32, (amount, LANES), 1) < LANES // 2
        turned = [pltpu.roll(part, LANES // 2, 1) for part in parts[2:]]
        even_rows = pl.ds(2 * start, amount, stride=2)
        odd_rows = pl.ds(2 * start + 1, amount, stride=2)
        for part in range(3):
            narrow_ref[part, even_rows, :] = parts[part]
        narrow_ref[0, odd_rows, :] = jnp.where(low_lanes, turned[0], turned[1])
        narrow_ref[1, odd_rows, :] = jnp.where(low_lanes, turned[1], turned[2])
        narrow_ref[2, odd_rows, :] = turned[2]

    for first, last in narrow_ranges(layout):
        for_chunks(first, last, PAIR_CHUNK, narrow_step)

    for out_ref, (entry_shape, offset) in zip(out_refs, layout_places(layout)):
        rows = math.prod(entry_shape[:-1])
        cols = entry_shape[-1]
        narrow = is_narrow(entry_shape, offset)

        def copy_rows(start, amount):
            for part in range(-(-cols // LANES)):
                lanes = min(LANES, cols - part * LANES)
                if narrow:
                    piece = narrow_ref[part, pl.ds(offset // D3 + start, amount), :]
                else:
                    stride = cols // LANES
                    base = offset // LANES + part + start * stride
                    piece = dense_ref[pl.ds(base, amount, stride=stride), :]
                out_ref[pl.ds(start, amount), part * LANES : part * LANES + lanes] = piece[
                    :, :lanes
                ].astype(out_ref.dtype)

        if rows < 32:
            copy_rows(0, rows)
        else:
            for_chunks(0, rows, 32, copy_rows)


def unpack_weights(flat_shard, layout, shard_count):
    shard_rows = flat_shard.shape[0] // LANES
    padded_rows = round_up(shard_rows, 16)
    local = jnp.pad(
        flat_shard.reshape(shard_rows, LANES).astype(jnp.bfloat16),
        ((0, padded_rows - shard_rows), (0, 0)),
    )
    gathered = lax.all_gather(local, AXES, axis=0, tiled=True)
    gathered = gathered.reshape(shard_count, padded_rows, LANES)
    dense_rows = round_up(shard_rows * shard_count + padded_rows, 16)
    narrow_rows = max([16] + [2 * last for first, last in narrow_ranges(layout)])
    out_shapes = []
    for entry_shape in layout:
        is_matrix = len(entry_shape) == 2 and entry_shape[0] > 9
        kind = jnp.bfloat16 if is_matrix else jnp.float32
        shape = entry_shape if len(entry_shape) == 2 else (1,) + entry_shape
        out_shapes.append(jax.ShapeDtypeStruct(shape, kind))
    return pl.pallas_call(
        lambda *refs: unpack_kernel(layout, shard_rows, shard_count, *refs),
        out_shape=out_shapes,
        scratch_shapes=[
            pltpu.VMEM((dense_rows, LANES), jnp.float32),
            pltpu.VMEM((3, round_up(narrow_rows, 16), LANES), jnp.float32),
        ],
        compiler_params=pltpu.CompilerParams(vmem_limit_bytes=60 * 1024 * 1024),
        name="unpack_weights",
    )(gathered)


def pack_kernel(layout, sources, shard_rows, shard_count, *refs):
    in_refs = refs[:-3]
    packed_ref, dense_ref, narrow_ref = refs[-3:]
    padded_rows = packed_ref.shape[1]

    places = layout_places(layout)
    used_rows = (places[-1][1] + math.prod(places[-1][0])) // LANES
    tail = dense_ref.shape[0] - used_rows
    dense_ref[pl.ds(used_rows, tail), :] = jnp.zeros((tail, LANES), jnp.float32)

    for (operand, first_row), (entry_shape, offset) in zip(sources, places):
        in_ref = in_refs[operand]
        rows = math.prod(entry_shape[:-1])
        cols = entry_shape[-1]
        narrow = is_narrow(entry_shape, offset)

        def copy_rows(start, amount):
            for part in range(-(-cols // LANES)):
                lanes = min(LANES, cols - part * LANES)
                piece = in_ref[pl.ds(first_row + start, amount), part * LANES : part * LANES + lanes]
                if narrow:
                    narrow_ref[part, pl.ds(offset // D3 + start, amount), 0:lanes] = piece
                else:
                    stride = cols // LANES
                    base = offset // LANES + part + start * stride
                    dense_ref[pl.ds(base, amount, stride=stride), :] = piece

        if rows < 32:
            copy_rows(0, rows)
        else:
            for_chunks(0, rows, 32, copy_rows)

    if narrow and (offset // D3 + rows) % 2 == 1:
        beyond = offset // D3 + rows
        narrow_ref[:, beyond : beyond + 1, :] = jnp.zeros((3, 1, LANES), jnp.float32)

    def narrow_step(start, amount):
        even_rows = pl.ds(2 * start, amount, stride=2)
        odd_rows = pl.ds(2 * start + 1, amount, stride=2)
        low_lanes = lax.broadcasted_iota(jnp.int32, (amount, LANES), 1) < LANES // 2
        even = [narrow_ref[part, even_rows, :] for part in range(3)]
        odd = [pltpu.roll(narrow_ref[part, odd_rows, :], LANES // 2, 1) for part in range(3)]
        joined = [
            even[0],
            even[1],
            jnp.where(low_lanes, even[2], odd[0]),
            jnp.where(low_lanes, odd[0], odd[1]),
            jnp.where(low_lanes, odd[1], odd[2]),
        ]
        for part in range(5):
            dense_ref[pl.ds(5 * start + part, amount, stride=5), :] = joined[part]

    for first, last in narrow_ranges(layout):
        for_chunks(first, last, PAIR_CHUNK, narrow_step)

    def cut(index, carry):
        packed_ref[index] = dense_ref[pl.ds(index * shard_rows, padded_rows), :].astype(
            packed_ref.dtype
        )
        return carry

    lax.fori_loop(0, shard_count, cut, 0)


def reduce_grads(operands, sources, layout, shard_rows, shard_count):
    padded_rows = round_up(shard_rows, 16)
    dense_rows = round_up(shard_rows * shard_count + padded_rows, 16)
    narrow_rows = max([16] + [2 * last for first, last in narrow_ranges(layout)])
    packed = pl.pallas_call(
        lambda *refs: pack_kernel(layout, sources, shard_rows, shard_count, *refs),
        out_shape=jax.ShapeDtypeStruct((shard_count, padded_rows, LANES), WIRE_TYPE),
        scratch_shapes=[
            pltpu.VMEM((dense_rows, LANES), jnp.float32),
            pltpu.VMEM((3, round_up(narrow_rows, 16), LANES), jnp.float32),
        ],
        compiler_params=pltpu.CompilerParams(vmem_limit_bytes=60 * 1024 * 1024),
        name="pack_grads",
    )(*operands)
    summed = packed.reshape(shard_count * padded_rows, LANES)
    for axis in AXES:
        summed = lax.psum_scatter(summed, axis, scatter_dimension=0, tiled=True)
    return summed[:shard_rows].astype(jnp.float32).reshape(-1)


def dot(left, right):
    return lax.dot_general(
        left, right, (((1,), (0,)), ((), ())), preferred_element_type=jnp.float32
    )


def dot_nt(left, right):
    return lax.dot_general(
        left, right, (((1,), (1,)), ((), ())), preferred_element_type=jnp.float32
    )


def dot_tn(left, right):
    return lax.dot_general(
        left, right, (((0,), (0,)), ((), ())), preferred_element_type=jnp.float32
    )


def rows_sum(values):
    return jnp.sum(values, axis=0, keepdims=True)


def norm_parts(values):
    centred = values - jnp.mean(values, axis=-1, keepdims=True)
    spread = jnp.mean(centred * centred, axis=-1, keepdims=True)
    scale = lax.rsqrt(spread + 1e-06)
    return centred * scale, scale


def norm_grad(unit, scale, gain_row, gradient):
    inner = gradient * gain_row
    first = jnp.mean(inner, axis=-1, keepdims=True)
    second = jnp.mean(inner * unit, axis=-1, keepdims=True)
    return scale * (inner - first - unit * second)


def column_mask(rows, lanes, side, width):
    places = lax.broadcasted_iota(jnp.int32, (rows, lanes), 0)
    return (places & (width - 1)) < side


def softmax_rows(query, key, valid):
    scores = jnp.where(valid, dot_nt(query, key) * 0.125, -1e30)
    powers = jnp.exp(scores - jnp.max(scores, axis=-1, keepdims=True))
    return powers * (1.0 / jnp.sum(powers, axis=-1, keepdims=True))


def split_lanes(values):
    rows, channels = values.shape
    pieces = []
    for first in range(0, channels, LANES):
        piece = values[:, first : min(first + LANES, channels)]
        if piece.shape[1] < LANES:
            rest = jnp.zeros((rows, LANES - piece.shape[1]), values.dtype)
            piece = jnp.concatenate([piece, rest], axis=1)
        pieces.append(piece)
    return pieces


def join_lanes(pieces, channels):
    return jnp.concatenate(pieces, axis=1)[:, :channels]


def pair_place(width, part):
    return pl.ds((part // 2) * width + part % 2, width // 2, stride=2)


def pair_part(grid_ref, width, part, channels):
    pieces = []
    for index in range(grid_ref.shape[0]):
        piece = grid_ref[index, :, pair_place(width, part), :]
        pieces.append(piece.reshape(piece.shape[0] * piece.shape[1], LANES))
    return join_lanes(pieces, channels).astype(jnp.bfloat16)


def attend_kernel(channels, width, has_reduction, *refs):
    if has_reduction:
        (
            x_ref, valid_ref, gain_ref, bias_ref, wq_ref, bq_ref, wr_ref, br_ref, rgain_ref,
            rbias_ref, wp_ref, bv_ref, wo_ref, bo_ref, gain2_ref, bias2_ref,
            query_ref, pair_ref, mixed_ref, middle_ref, normed_ref, reduced_ref, grid_ref,
        ) = refs
    else:
        (
            x_ref, valid_ref, gain_ref, bias_ref, wq_ref, bq_ref,
            wp_ref, bv_ref, wo_ref, bo_ref, gain2_ref, bias2_ref,
            query_ref, pair_ref, mixed_ref, middle_ref, normed_ref,
        ) = refs
    inputs = x_ref[0].astype(jnp.float32)
    unit, _ = norm_parts(inputs)
    normed = (unit * gain_ref[...] + bias_ref[...]).astype(jnp.bfloat16)
    query_ref[0] = (dot(normed, wq_ref[...]) + bq_ref[...]).astype(jnp.bfloat16)
    if has_reduction:
        for index, piece in enumerate(split_lanes(normed.astype(jnp.float32))):
            grid_ref[index] = piece.reshape(grid_ref.shape[1:])
        reduced = br_ref[...]
        for part in range(4):
            reduced = reduced + dot(
                pair_part(grid_ref, width, part, channels),
                wr_ref[part * channels : (part + 1) * channels, :],
            )
        reduced_ref[0] = reduced
        unit, _ = norm_parts(reduced)
        source = (unit * rgain_ref[...] + rbias_ref[...]).astype(jnp.bfloat16)
    else:
        source = normed
    pair_ref[0, :, :channels] = dot(source, wp_ref[:, :channels]).astype(jnp.bfloat16)
    pair_ref[0, :, channels:] = (dot(source, wp_ref[:, channels:]) + bv_ref[...]).astype(
        jnp.bfloat16
    )
    valid = valid_ref[0] > 0.5
    for head in range(channels // HEAD):
        lanes = slice(head * HEAD, (head + 1) * HEAD)
        value_lanes = slice(channels + head * HEAD, channels + (head + 1) * HEAD)
        chances = softmax_rows(query_ref[0, :, lanes], pair_ref[0, :, lanes], valid)
        mixed_ref[0, :, lanes] = dot(
            chances.astype(jnp.bfloat16), pair_ref[0, :, value_lanes]
        ).astype(jnp.bfloat16)
    middle = inputs + (dot(mixed_ref[0], wo_ref[...]) + bo_ref[...])
    middle_ref[0] = middle
    unit, _ = norm_parts(middle)
    normed_ref[0] = (unit * gain2_ref[...] + bias2_ref[...]).astype(jnp.bfloat16)


def whole(shape):
    return pl.BlockSpec(shape, lambda *place: (0,) * len(shape))


def image_block(array):
    return pl.BlockSpec((1,) + array.shape[1:], lambda image: (image,) + (0,) * (len(array.shape) - 1))


def shaped(shape, kind):
    return jax.ShapeDtypeStruct(shape, kind)


PARAMS = pltpu.CompilerParams(vmem_limit_bytes=61000 * 1024)


def attend_block(inputs, valid, weights, width):
    images, tokens, channels = inputs.shape
    has_reduction = len(weights) == 14
    keys = valid.shape[2]
    outs = [
        shaped((images, tokens, channels), jnp.bfloat16),
        shaped((images, keys, 2 * channels), jnp.bfloat16),
        shaped((images, tokens, channels), jnp.bfloat16),
        shaped((images, tokens, channels), jnp.float32),
        shaped((images, tokens, channels), jnp.bfloat16),
    ]
    scratch = []
    if has_reduction:
        outs.append(shaped((images, keys, channels), jnp.float32))
        grid_shape = (-(-channels // LANES), tokens // (2 * width), 2 * width, LANES)
        scratch.append(pltpu.VMEM(grid_shape, jnp.float32))
    return pl.pallas_call(
        lambda *refs: attend_kernel(channels, width, has_reduction, *refs),
        grid=(images,),
        in_specs=[image_block(inputs), image_block(valid)] + [whole(w.shape) for w in weights],
        out_specs=[image_block(out) for out in outs],
        out_shape=outs,
        scratch_shapes=scratch,
        compiler_params=PARAMS,
        name="attend",
    )(inputs, valid, *weights)


def mix_kernel(side, width, *refs):
    (
        normed_ref, middle_ref, we_ref, be_ref, kd_ref, bd_ref, wc_ref, bc_ref,
        out_ref, mixed_ref, slope_ref, pad_ref,
    ) = refs
    tokens = side * width
    lanes = we_ref.shape[1]
    block = pl.program_id(1)
    hidden = dot(normed_ref[0], we_ref[...]) + be_ref[...]
    pad_ref[0:width, :] = jnp.zeros((width, lanes), jnp.float32)
    pad_ref[width + tokens : 2 * width + tokens, :] = jnp.zeros((width, lanes), jnp.float32)
    pad_ref[width : width + tokens, :] = jnp.where(
        column_mask(tokens, lanes, side, width), hidden, 0.0
    )

    def step(row, carry):
        start = pl.multiple_of(row * width, width)
        rows = [pad_ref[pl.ds(start + up * width, width), :] for up in range(3)]
        sums = [
            kd_ref[col : col + 1, :] * rows[0]
            + kd_ref[3 + col : 4 + col, :] * rows[1]
            + kd_ref[6 + col : 7 + col, :] * rows[2]
            for col in range(3)
        ]
        value = (
            sums[1]
            + pltpu.roll(sums[0], 1, 0)
            + pltpu.roll(sums[2], width - 1, 0)
            + bd_ref[...]
        )
        share = 0.5 + 0.5 * lax.erf(value * math.sqrt(0.5))
        bell = jnp.exp(-0.5 * value * value) * (1.0 / math.sqrt(2.0 * math.pi))
        mixed_ref[0, pl.ds(start, width), :] = (value * share).astype(jnp.bfloat16)
        slope_ref[0, pl.ds(start, width), :] = (share + value * bell).astype(jnp.bfloat16)
        return carry

    lax.fori_loop(0, side, step, 0)
    result = dot(mixed_ref[0], wc_ref[...])

    @pl.when(block == 0)
    def _():
        out_ref[0] = middle_ref[0] + bc_ref[...] + result

    @pl.when(block > 0)
    def _():
        out_ref[0] += result


def mix_block(normed, middle, weights, side, width, lanes):
    we, be, kd, bd, wc, bc = weights
    images, tokens, channels = middle.shape
    units = we.shape[1]
    outs = [
        shaped(middle.shape, jnp.float32),
        shaped((images, tokens, units), jnp.bfloat16),
        shaped((images, tokens, units), jnp.bfloat16),
    ]
    token_spec = pl.BlockSpec((1, tokens, channels), lambda i, c: (i, 0, 0))
    unit_spec = pl.BlockSpec((1, tokens, lanes), lambda i, c: (i, 0, c))

    def row_spec(rows):
        return pl.BlockSpec((rows, lanes), lambda i, c: (0, c))

    return pl.pallas_call(
        lambda *refs: mix_kernel(side, width, *refs),
        grid=(images, units // lanes),
        in_specs=[
            token_spec,
            token_spec,
            row_spec(channels),
            row_spec(1),
            row_spec(9),
            row_spec(1),
            pl.BlockSpec((lanes, channels), lambda i, c: (c, 0)),
            pl.BlockSpec((1, channels), lambda i, c: (0, 0)),
        ],
        out_specs=[token_spec, unit_spec, unit_spec],
        out_shape=outs,
        scratch_shapes=[pltpu.VMEM((tokens + 2 * width, lanes), jnp.float32)],
        compiler_params=PARAMS,
        name="mix",
    )(normed, middle, we, be, kd, bd, wc, bc)


def mix_back_kernel(side, width, *refs):
    (
        normed_ref, grad_ref, mixed_ref, slope_ref, we_ref, be_ref, kd_ref, wc_ref,
        dnormed_ref, dwe_ref, dwc_ref, drows_ref, pad_ref, dpad_ref, dhid_ref,
    ) = refs
    tokens = side * width
    lanes = we_ref.shape[1]
    block = pl.program_id(0)
    image = pl.program_id(1)
    gradient = grad_ref[0].astype(jnp.bfloat16)
    inside = column_mask(tokens, lanes, side, width)
    hidden = dot(normed_ref[0], we_ref[...]) + be_ref[...]
    for ref in (pad_ref, dpad_ref):
        ref[0:width, :] = jnp.zeros((width, lanes), jnp.float32)
        ref[width + tokens : 2 * width + tokens, :] = jnp.zeros((width, lanes), jnp.float32)
    pad_ref[width : width + tokens, :] = jnp.where(inside, hidden, 0.0)
    dpad_ref[width : width + tokens, :] = dot_nt(gradient, wc_ref[...]) * slope_ref[0].astype(
        jnp.float32
    )

    @pl.when(image == 0)
    def _():
        drows_ref[...] = jnp.zeros(drows_ref.shape, jnp.float32)
        dwe_ref[...] = jnp.zeros(dwe_ref.shape, jnp.float32)
        dwc_ref[...] = jnp.zeros(dwc_ref.shape, jnp.float32)

    row_inside = column_mask(width, lanes, side, width)

    def fold(values):
        total = values[0:8]
        for start in range(8, width, 8):
            total = total + values[start : start + 8]
        return total

    def step(row, sums):
        start = pl.multiple_of(row * width, width)
        rows = [pad_ref[pl.ds(start + up * width, width), :] for up in range(3)]
        drows = [dpad_ref[pl.ds(start + up * width, width), :] for up in range(3)]
        turned = [
            pltpu.roll(drows[1], width - 1, 0),
            drows[1],
            pltpu.roll(drows[1], 1, 0),
        ]
        found = []
        for up in range(3):
            for col in range(3):
                found.append(sums[3 * up + col] + fold(turned[col] * rows[up]))
        found.append(sums[9] + fold(drows[1]))
        parts = [
            kd_ref[col : col + 1, :] * drows[2]
            + kd_ref[3 + col : 4 + col, :] * drows[1]
            + kd_ref[6 + col : 7 + col, :] * drows[0]
            for col in range(3)
        ]
        value = parts[1] + pltpu.roll(parts[0], width - 1, 0) + pltpu.roll(parts[2], 1, 0)
        rounded = jnp.where(row_inside, value, 0.0).astype(jnp.bfloat16)
        dhid_ref[pl.ds(start, width), :] = rounded
        found.append(sums[10] + fold(rounded.astype(jnp.float32)))
        return tuple(found)

    zero = jnp.zeros((8, lanes), jnp.float32)
    totals = lax.fori_loop(0, side, step, (zero,) * 11)
    for index in range(11):
        drows_ref[index : index + 1, :] += rows_sum(totals[index])
    dhidden = dhid_ref[...]
    dwe_ref[...] += dot_tn(normed_ref[0], dhidden)
    dwc_ref[...] += dot_tn(mixed_ref[0], gradient)
    result = dot_nt(dhidden, we_ref[...])

    @pl.when(block == 0)
    def _():
        dnormed_ref[image] = result

    @pl.when(block > 0)
    def _():
        dnormed_ref[image] += result


def mix_back(normed, gradient, mixed, slope, weights, side, width, lanes):
    we, be, kd, bd, wc, bc = weights
    images, tokens, channels = normed.shape
    units = we.shape[1]
    token_spec = pl.BlockSpec((1, tokens, channels), lambda c, i: (i, 0, 0))
    unit_spec = pl.BlockSpec((1, tokens, lanes), lambda c, i: (i, 0, c))

    def row_spec(rows):
        return pl.BlockSpec((rows, lanes), lambda c, i: (0, c))

    col_spec = pl.BlockSpec((lanes, channels), lambda c, i: (c, 0))
    return pl.pallas_call(
        lambda *refs: mix_back_kernel(side, width, *refs),
        grid=(units // lanes, images),
        in_specs=[
            token_spec,
            token_spec,
            unit_spec,
            unit_spec,
            row_spec(channels),
            row_spec(1),
            row_spec(9),
            col_spec,
        ],
        out_specs=[whole((images, tokens, channels)), row_spec(channels), col_spec, row_spec(16)],
        out_shape=[
            shaped((images, tokens, channels), jnp.float32),
            shaped((channels, units), jnp.float32),
            shaped((units, channels), jnp.float32),
            shaped((16, units), jnp.float32),
        ],
        scratch_shapes=[
            pltpu.VMEM((tokens + 2 * width, lanes), jnp.float32),
            pltpu.VMEM((tokens + 2 * width, lanes), jnp.float32),
            pltpu.VMEM((tokens, lanes), jnp.bfloat16),
        ],
        compiler_params=PARAMS,
        name="mix_back",
    )(normed, gradient, mixed, slope, we, be, kd, wc)


def attend_back_kernel(channels, width, has_reduction, *refs):
    if has_reduction:
        (
            x_ref, valid_ref, grad_ref, dnormed_ref, middle_ref, query_ref, pair_ref, mixed_ref,
            reduced_ref, gain_ref, bias_ref, wq_ref, wr_ref, rgain_ref, rbias_ref, wp_ref, wo_ref,
            gain2_ref,
            dx_ref, dwq_ref, dwp_ref, dwo_ref, vec_ref, dwr_ref,
            dquery_ref, dpair_ref, grid_ref, dgrid_ref,
        ) = refs
    else:
        (
            x_ref, valid_ref, grad_ref, dnormed_ref, middle_ref, query_ref, pair_ref, mixed_ref,
            gain_ref, bias_ref, wq_ref, wp_ref, wo_ref, gain2_ref,
            dx_ref, dwq_ref, dwp_ref, dwo_ref, vec_ref,
            dquery_ref, dpair_ref,
        ) = refs

    @pl.when(pl.program_id(0) == 0)
    def _():
        sums = [dwq_ref, dwp_ref, dwo_ref, vec_ref] + ([dwr_ref] if has_reduction else [])
        for ref in sums:
            ref[...] = jnp.zeros(ref.shape, jnp.float32)

    def add_row(index, row):
        vec_ref[index : index + 1, :] += row

    gradient = grad_ref[0].astype(jnp.float32)
    add_row(0, rows_sum(gradient.astype(jnp.bfloat16).astype(jnp.float32)))
    dnormed = dnormed_ref[0]
    unit, scale = norm_parts(middle_ref[0])
    add_row(1, rows_sum(dnormed * unit))
    add_row(2, rows_sum(dnormed))
    dmiddle = gradient + norm_grad(unit, scale, gain2_ref[...], dnormed)
    dx_ref[0] = dmiddle
    doutput = dmiddle.astype(jnp.bfloat16)
    add_row(3, rows_sum(doutput.astype(jnp.float32)))
    dwo_ref[...] += dot_tn(mixed_ref[0], doutput)
    dmixed = dot_nt(doutput, wo_ref[...]).astype(jnp.bfloat16)
    valid = valid_ref[0] > 0.5
    for head in range(channels // HEAD):
        lanes = slice(head * HEAD, (head + 1) * HEAD)
        value_lanes = slice(channels + head * HEAD, channels + (head + 1) * HEAD)
        query = query_ref[0, :, lanes]
        key = pair_ref[0, :, lanes]
        chances = softmax_rows(query, key, valid)
        dhead = dmixed[:, lanes]
        dchances = dot_nt(dhead, pair_ref[0, :, value_lanes])
        dpair_ref[:, value_lanes] = dot_tn(chances.astype(jnp.bfloat16), dhead).astype(
            jnp.bfloat16
        )
        weighted = chances * dchances
        dscores = (
            weighted - chances * jnp.sum(weighted, axis=-1, keepdims=True)
        ).astype(jnp.bfloat16)
        dquery_ref[:, lanes] = (dot(dscores, key) * 0.125).astype(jnp.bfloat16)
        dpair_ref[:, lanes] = (dot_tn(dscores, query) * 0.125).astype(jnp.bfloat16)
    dquery = dquery_ref[...]
    dpair = dpair_ref[...]
    unit, scale = norm_parts(x_ref[0].astype(jnp.float32))
    normed = (unit * gain_ref[...] + bias_ref[...]).astype(jnp.bfloat16)
    add_row(4, rows_sum(dquery.astype(jnp.float32)))
    add_row(5, rows_sum(dpair[:, channels:].astype(jnp.float32)))
    dwq_ref[...] += dot_tn(normed, dquery)
    total = dot_nt(dquery, wq_ref[...])
    dsource = dot_nt(dpair, wp_ref[...])
    if has_reduction:
        runit, rscale = norm_parts(reduced_ref[0])
        source = (runit * rgain_ref[...] + rbias_ref[...]).astype(jnp.bfloat16)
        dwp_ref[...] += dot_tn(source, dpair)
        add_row(8, rows_sum(dsource * runit))
        add_row(9, rows_sum(dsource))
        dreduced = norm_grad(runit, rscale, rgain_ref[...], dsource).astype(jnp.bfloat16)
        add_row(10, rows_sum(dreduced.astype(jnp.float32)))
        for index, piece in enumerate(split_lanes(normed.astype(jnp.float32))):
            grid_ref[index] = piece.reshape(grid_ref.shape[1:])
        for index, piece in enumerate(split_lanes(total)):
            dgrid_ref[index] = piece.reshape(dgrid_ref.shape[1:])
        for part in range(4):
            rows = slice(part * channels, (part + 1) * channels)
            dwr_ref[rows, :] += dot_tn(pair_part(grid_ref, width, part, channels), dreduced)
            for index, piece in enumerate(split_lanes(dot_nt(dreduced, wr_ref[rows, :]))):
                dgrid_ref[index, :, pair_place(width, part), :] += piece.reshape(
                    dgrid_ref.shape[1], width // 2, LANES
                )
        total = join_lanes(
            [dgrid_ref[index].reshape(total.shape[0], LANES) for index in range(dgrid_ref.shape[0])],
            channels,
        )
    else:
        dwp_ref[...] += dot_tn(normed, dpair)
        total = total + dsource
    add_row(6, rows_sum(total * unit))
    add_row(7, rows_sum(total))
    dx_ref[0] += norm_grad(unit, scale, gain_ref[...], total)


def attend_back(inputs, valid, gradient, dnormed, saved, weights, width):
    query, pair, mixed, middle, normed = saved[:5]
    images, tokens, channels = middle.shape
    has_reduction = len(saved) == 6
    keys = valid.shape[2]
    operands = [inputs, valid, gradient, dnormed, middle, query, pair, mixed]
    outs = [
        shaped((images, tokens, channels), jnp.float32),
        shaped((channels, channels), jnp.float32),
        shaped((channels, 2 * channels), jnp.float32),
        shaped((channels, channels), jnp.float32),
        shaped((16, channels), jnp.float32),
    ]
    scratch = [
        pltpu.VMEM((tokens, channels), jnp.bfloat16),
        pltpu.VMEM((keys, 2 * channels), jnp.bfloat16),
    ]
    if has_reduction:
        gain, bias, wq, bq, wr, br, rgain, rbias, wp, bv, wo, bo, gain2, bias2 = weights
        used = [gain, bias, wq, wr, rgain, rbias, wp, wo, gain2]
        operands.append(saved[5])
        outs.append(shaped((4 * channels, channels), jnp.float32))
        grid_shape = (-(-channels // LANES), tokens // (2 * width), 2 * width, LANES)
        scratch += [pltpu.VMEM(grid_shape, jnp.float32), pltpu.VMEM(grid_shape, jnp.float32)]
    else:
        gain, bias, wq, bq, wp, bv, wo, bo, gain2, bias2 = weights
        used = [gain, bias, wq, wp, wo, gain2]
    return pl.pallas_call(
        lambda *refs: attend_back_kernel(channels, width, has_reduction, *refs),
        grid=(images,),
        in_specs=[image_block(op) for op in operands] + [whole(w.shape) for w in used],
        out_specs=[image_block(outs[0])] + [whole(out.shape) for out in outs[1:]],
        out_shape=outs,
        scratch_shapes=scratch,
        compiler_params=PARAMS,
        name="attend_back",
    )(*operands, *used)


def tap_place(width, tap, row):
    first = LEAD + (tap // 3) * width + tap % 3 - 1
    return pl.ds(first + 2 * width * row, width // 2, stride=2)


def load_tap(grid_ref, side, width, tap, channels):
    pieces = []
    for index in range(grid_ref.shape[0]):
        rows = [grid_ref[index, tap_place(width, tap, row), :] for row in range(side // 2)]
        pieces.append(jnp.concatenate(rows, axis=0))
    return join_lanes(pieces, channels).astype(jnp.bfloat16)


def fill_grid(grid_ref, values, width):
    rows = grid_ref.shape[1]
    first = LEAD + width
    last = first + values.shape[0]
    for index, piece in enumerate(split_lanes(values)):
        grid_ref[index, 0:first, :] = jnp.zeros((first, LANES), jnp.float32)
        grid_ref[index, first:last, :] = piece
        grid_ref[index, last:rows, :] = jnp.zeros((rows - last, LANES), jnp.float32)


LEAD = 8


def embed_kernel(side, width, *refs):
    x_ref, gain_ref, bias_ref, w_ref, b_ref, pgain_ref, pbias_ref = refs[:7]
    out_ref, patch_ref, grid_ref = refs[7:]
    tokens, channels = x_ref.shape[1:]
    unit, _ = norm_parts(x_ref[0])
    normed = (unit * gain_ref[...] + bias_ref[...]).astype(jnp.bfloat16).astype(jnp.float32)
    inside = column_mask(tokens, channels, side, width)
    fill_grid(grid_ref, jnp.where(inside, normed, 0.0), width)
    patch = b_ref[...]
    for tap in range(9):
        patch = patch + dot(
            load_tap(grid_ref, side, width, tap, channels),
            w_ref[tap * channels : (tap + 1) * channels, :]
        )
    patch_ref[0] = patch
    unit, _ = norm_parts(patch)
    out_ref[0] = unit * pgain_ref[...] + pbias_ref[...]


def embed_block(inputs, weights, side, width):
    images, tokens, channels = inputs.shape
    units = weights[2].shape[1]
    outs = [shaped((images, tokens // 4, units), jnp.float32)] * 2
    return pl.pallas_call(
        lambda *refs: embed_kernel(side, width, *refs),
        grid=(images,),
        in_specs=[image_block(inputs)] + [whole(w.shape) for w in weights],
        out_specs=[image_block(out) for out in outs],
        out_shape=outs,
        scratch_shapes=[pltpu.VMEM((-(-channels // LANES), LEAD + (side + 3) * width, LANES), jnp.float32)],
        compiler_params=PARAMS,
        name="embed",
    )(inputs, *weights)


def embed_back_kernel(side, width, *refs):
    x_ref, grad_ref, patch_ref, gain_ref, bias_ref, w_ref, pgain_ref = refs[:7]
    dx_ref, dw_ref, vec_ref, pvec_ref, grid_ref, dgrid_ref = refs[7:]
    tokens, channels = x_ref.shape[1:]

    @pl.when(pl.program_id(0) == 0)
    def _():
        for ref in (dw_ref, vec_ref, pvec_ref):
            ref[...] = jnp.zeros(ref.shape, jnp.float32)

    gradient = grad_ref[0]
    punit, pscale = norm_parts(patch_ref[0])
    pvec_ref[0:1, :] += rows_sum(gradient * punit)
    pvec_ref[1:2, :] += rows_sum(gradient)
    dpatch = norm_grad(punit, pscale, pgain_ref[...], gradient).astype(jnp.bfloat16)
    pvec_ref[2:3, :] += rows_sum(dpatch.astype(jnp.float32))
    unit, scale = norm_parts(x_ref[0])
    normed = (unit * gain_ref[...] + bias_ref[...]).astype(jnp.bfloat16).astype(jnp.float32)
    inside = column_mask(tokens, channels, side, width)
    fill_grid(grid_ref, jnp.where(inside, normed, 0.0), width)
    dgrid_ref[...] = jnp.zeros(dgrid_ref.shape, jnp.float32)
    half = width // 2
    for tap in range(9):
        rows = slice(tap * channels, (tap + 1) * channels)
        dw_ref[rows, :] += dot_tn(load_tap(grid_ref, side, width, tap, channels), dpatch)
        for index, piece in enumerate(split_lanes(dot_nt(dpatch, w_ref[rows, :]))):
            for row in range(side // 2):
                dgrid_ref[index, tap_place(width, tap, row), :] += piece[
                    row * half : (row + 1) * half, :
                ]
    first = LEAD + width
    pieces = [dgrid_ref[index, first : first + tokens, :] for index in range(dgrid_ref.shape[0])]
    total = jnp.where(inside, join_lanes(pieces, channels), 0.0)
    vec_ref[0:1, :] += rows_sum(total * unit)
    vec_ref[1:2, :] += rows_sum(total)
    dx_ref[0] = norm_grad(unit, scale, gain_ref[...], total)


def embed_back(inputs, gradient, patch, weights, side, width):
    gain, bias, w, b, pgain, pbias = weights
    images, tokens, channels = inputs.shape
    units = w.shape[1]
    outs = [
        shaped(inputs.shape, jnp.float32),
        shaped(w.shape, jnp.float32),
        shaped((8, channels), jnp.float32),
        shaped((8, units), jnp.float32),
    ]
    operands = [inputs, gradient, patch]
    used = [gain, bias, w, pgain]
    grid_scratch = pltpu.VMEM((-(-channels // LANES), LEAD + (side + 3) * width, LANES), jnp.float32)
    return pl.pallas_call(
        lambda *refs: embed_back_kernel(side, width, *refs),
        grid=(images,),
        in_specs=[image_block(op) for op in operands] + [whole(u.shape) for u in used],
        out_specs=[image_block(outs[0])] + [whole(out.shape) for out in outs[1:]],
        out_shape=outs,
        scratch_shapes=[grid_scratch, grid_scratch],
        compiler_params=PARAMS,
        name="embed_back",
    )(*operands, *used)


def to_grid(values, side, width):
    images, tokens, channels = values.shape
    grid = values.reshape(images, side, side, channels)
    grid = jnp.pad(grid, ((0, 0), (0, 0), (0, width - side), (0, 0)))
    return grid.reshape(images, side * width, channels)


def from_grid(values, side, width):
    images, tokens, channels = values.shape
    grid = values.reshape(images, side, width, channels)[:, :, :side]
    return grid.reshape(images, side * side, channels)


def key_mask(row_counts, col_counts, side, width):
    places = jnp.arange(side * width, dtype=jnp.int32)
    valid = ((places // width)[None, :] < row_counts[:, None]) & (
        (places % width)[None, :] < col_counts[:, None]
    )
    return valid.astype(jnp.float32)[:, None, :]


def block_sources(has_reduction):
    reduction = [(7, 0), (3, 10), (3, 8), (3, 9)] if has_reduction else []
    return (
        [(3, 6), (3, 7), (0, 0), (3, 4)]
        + reduction
        + [(1, 0), (3, 5), (2, 0), (3, 3), (3, 1), (3, 2)]
        + [(4, 0), (6, 10), (6, 0), (6, 9), (5, 0), (3, 0)]
    )


EMBED_SOURCES = [(1, 0), (1, 1), (0, 0), (2, 2), (2, 0), (2, 1)]


def adamw_update(weights, mean_old, square_old, gradient, clip_factor, rate_value, fix_one):
    clipped = gradient * clip_factor
    mean_new = 0.5 * mean_old + 0.5 * clipped
    square_new = 0.5 * square_old + 0.5 * clipped * clipped
    updated = weights * (1.0 - rate_value * 0.05) - rate_value * (mean_new / fix_one) / (
        jnp.sqrt(square_new / fix_one) + 1e-08
    )
    return (updated, mean_new, square_new)


def shards(
    features,
    key_rows,
    key_cols,
    out_grad,
    lower_weights,
    lower_mean,
    lower_square,
    embed_weights,
    embed_mean,
    embed_square,
    upper_weights,
    upper_mean,
    upper_square,
    learn_rate,
):
    side, half = GRID, GRID // 2
    width = round_up(side, 32)
    half_width = width // 2
    shard_count = lax.axis_size("dp") * lax.axis_size("fsdp")
    key_valid = key_mask(key_rows, key_cols, half, half_width)
    lower = unpack_weights(lower_weights, LOWER_LAYOUT, shard_count)
    embed = unpack_weights(embed_weights, EMBED_LAYOUT, shard_count)
    upper = unpack_weights(upper_weights, UPPER_LAYOUT, shard_count)
    three_in = to_grid(features, side, width)
    grad_in = to_grid(out_grad, half, half_width)

    lower_saved = attend_block(three_in, key_valid, lower[:14], width)
    section_three, lower_mixed, lower_slope = mix_block(
        lower_saved[4], lower_saved[3], lower[14:], side, width, 256
    )
    section_four, patch = embed_block(section_three, embed, side, width)
    upper_saved = attend_block(section_four, key_valid, upper[:10], half_width)
    block_out, upper_mixed, upper_slope = mix_block(
        upper_saved[4], upper_saved[3], upper[10:], half, half_width, 512
    )

    def back(inputs, gradient, saved, mixed, slope, weights, first, side, width, lanes):
        dnormed, dwe, dwc, drows = mix_back(
            saved[4], gradient, mixed, slope, weights[first:], side, width, lanes
        )
        dx, dwq, dwp, dwo, vec, *rest = attend_back(
            inputs, key_valid, gradient, dnormed, saved, weights[:first], width
        )
        return dx, [dwq, dwp, dwo, vec, dwe, dwc, drows] + rest

    four_grad, upper_found = back(
        section_four, grad_in, upper_saved, upper_mixed, upper_slope, upper, 10, half, half_width, 512
    )
    upper_grad = reduce_grads(
        upper_found,
        block_sources(False),
        UPPER_LAYOUT,
        upper_weights.shape[0] // LANES,
        shard_count,
    )
    three_grad, *embed_found = embed_back(section_three, four_grad, patch, embed, side, width)
    embed_grad = reduce_grads(
        embed_found, EMBED_SOURCES, EMBED_LAYOUT, embed_weights.shape[0] // LANES, shard_count
    )
    input_grad, lower_found = back(
        three_in, three_grad, lower_saved, lower_mixed, lower_slope, lower, 14, side, width, 256
    )
    lower_grad = reduce_grads(
        lower_found, block_sources(True), LOWER_LAYOUT, lower_weights.shape[0] // LANES, shard_count
    )
    input_grad = from_grid(input_grad, side, width)
    block_out = from_grid(block_out, half, half_width)
    local_squares = (
        jnp.sum(lower_grad * lower_grad)
        + jnp.sum(embed_grad * embed_grad)
        + jnp.sum(upper_grad * upper_grad)
    )
    squares = lax.psum(local_squares, AXES)
    grad_norm = jnp.sqrt(squares)
    clip_factor = jnp.minimum(1.0, 5.0 / (grad_norm + 1e-06))
    rate_value = learn_rate[0]
    fix_one = 1.0 - 0.5**ADAM_STEP
    lower_new, lower_mean_new, lower_square_new = adamw_update(
        lower_weights, lower_mean, lower_square, lower_grad, clip_factor, rate_value, fix_one
    )
    embed_new, embed_mean_new, embed_square_new = adamw_update(
        embed_weights, embed_mean, embed_square, embed_grad, clip_factor, rate_value, fix_one
    )
    upper_new, upper_mean_new, upper_square_new = adamw_update(
        upper_weights, upper_mean, upper_square, upper_grad, clip_factor, rate_value, fix_one
    )
    return (
        block_out,
        input_grad,
        grad_norm.reshape(1),
        lower_grad,
        lower_new,
        lower_mean_new,
        lower_square_new,
        lower_new.astype(jnp.bfloat16),
        embed_grad,
        embed_new,
        embed_mean_new,
        embed_square_new,
        embed_new.astype(jnp.bfloat16),
        upper_grad,
        upper_new,
        upper_mean_new,
        upper_square_new,
        upper_new.astype(jnp.bfloat16),
    )


AXES = ("dp", "fsdp")
TOKENS = P(AXES, None, None)
FLAT = P(AXES)


def solution(mesh):
    return jax.shard_map(
        shards,
        mesh=mesh,
        in_specs=(
            TOKENS,
            FLAT,
            FLAT,
            TOKENS,
            FLAT,
            FLAT,
            FLAT,
            FLAT,
            FLAT,
            FLAT,
            FLAT,
            FLAT,
            FLAT,
            P(),
        ),
        out_specs=(
            TOKENS,
            TOKENS,
            P(),
            FLAT,
            FLAT,
            FLAT,
            FLAT,
            FLAT,
            FLAT,
            FLAT,
            FLAT,
            FLAT,
            FLAT,
            FLAT,
            FLAT,
            FLAT,
            FLAT,
            FLAT,
        ),
        check_vma=False,
    )
```

```python
import math

import jax
import jax.numpy as jnp
from jax import lax
from jax.experimental import pallas as pl
from jax.experimental.pallas import tpu as pltpu
from jax.sharding import PartitionSpec as P

D3 = 320
D4 = 512
HID3 = 1280
HID4 = 2048
HEAD = 64
GRID = 28
ADAM_STEP = 2
WIRE_TYPE = jnp.bfloat16


def block_layout(channels, units, has_reduction):
    row = (channels,)
    reduction = [(4 * channels, channels), row, row, row] if has_reduction else []
    return (
        [row, row, (channels, channels), row]
        + reduction
        + [(channels, 2 * channels), row, (channels, channels), row, row, row]
        + [(channels, units), (units,), (9, units), (units,), (units, channels), row]
    )


LOWER_LAYOUT = block_layout(D3, HID3, True)
UPPER_LAYOUT = block_layout(D4, HID4, False)
EMBED_LAYOUT = [(D3,), (D3,), (9 * D3, D4), (D4,), (D4,), (D4,)]


LANES = 128
PAIR_CHUNK = 32


def layout_places(layout):
    places = []
    offset = 0
    for entry_shape in layout:
        places.append((entry_shape, offset))
        offset = offset + math.prod(entry_shape)
    return places


def is_narrow(entry_shape, offset):
    return entry_shape[-1] % LANES != 0 or offset % LANES != 0


def narrow_ranges(layout):
    ranges = []
    for entry_shape, offset in layout_places(layout):
        if not is_narrow(entry_shape, offset):
            continue
        first = offset // D3
        last = first + math.prod(entry_shape) // D3
        if ranges and ranges[-1][1] == first:
            ranges[-1] = (ranges[-1][0], last)
        else:
            ranges.append((first, last))
    return [(first // 2, (last + 1) // 2) for first, last in ranges]


def round_up(amount, unit):
    return (amount + unit - 1) // unit * unit


def for_chunks(first, last, chunk, step):
    full = (last - first) // chunk

    def body(index, carry):
        step(first + index * chunk, chunk)
        return carry

    if full > 0:
        lax.fori_loop(0, full, body, 0)
    rest = (last - first) - full * chunk
    if rest > 0:
        step(first + full * chunk, rest)


def unpack_group(layout, shard_rows, shard_count, spread, out_refs, dense_ref, narrow_ref):
    lax.fori_loop(0, shard_count, spread, 0)

    def narrow_step(start, amount):
        parts = [
            dense_ref[pl.ds(5 * start + part, amount, stride=5), :] for part in range(5)
        ]
        low_lanes = lax.broadcasted_iota(jnp.int32, (amount, LANES), 1) < LANES // 2
        turned = [pltpu.roll(part, LANES // 2, 1) for part in parts[2:]]
        even_rows = pl.ds(2 * start, amount, stride=2)
        odd_rows = pl.ds(2 * start + 1, amount, stride=2)
        for part in range(3):
            narrow_ref[part, even_rows, :] = parts[part]
        narrow_ref[0, odd_rows, :] = jnp.where(low_lanes, turned[0], turned[1])
        narrow_ref[1, odd_rows, :] = jnp.where(low_lanes, turned[1], turned[2])
        narrow_ref[2, odd_rows, :] = turned[2]

    for first, last in narrow_ranges(layout):
        for_chunks(first, last, PAIR_CHUNK, narrow_step)

    for out_ref, (entry_shape, offset) in zip(out_refs, layout_places(layout)):
        rows = math.prod(entry_shape[:-1])
        cols = entry_shape[-1]
        narrow = is_narrow(entry_shape, offset)

        def copy_rows(start, amount):
            for part in range(-(-cols // LANES)):
                lanes = min(LANES, cols - part * LANES)
                if narrow:
                    piece = narrow_ref[part, pl.ds(offset // D3 + start, amount), :]
                else:
                    stride = cols // LANES
                    base = offset // LANES + part + start * stride
                    piece = dense_ref[pl.ds(base, amount, stride=stride), :]
                out_ref[pl.ds(start, amount), part * LANES : part * LANES + lanes] = piece[
                    :, :lanes
                ].astype(out_ref.dtype)

        if rows < 32:
            copy_rows(0, rows)
        else:
            for_chunks(0, rows, 32, copy_rows)


def dense_rows_of(layouts, row_counts, shard_count):
    return max(
        round_up(rows * shard_count + round_up(rows, 16), 16)
        for layout, rows in zip(layouts, row_counts)
    )


def narrow_rows_of(layouts):
    return max(
        [16] + [2 * last for layout in layouts for first, last in narrow_ranges(layout)]
    )


def work_scratch(layouts, row_counts, shard_count):
    return [
        pltpu.VMEM((dense_rows_of(layouts, row_counts, shard_count), LANES), jnp.float32),
        pltpu.VMEM((3, round_up(narrow_rows_of(layouts), 16), LANES), jnp.float32),
    ]


def local_rows(flat_shard):
    shard_rows = flat_shard.shape[0] // LANES
    return jnp.pad(
        flat_shard.reshape(shard_rows, LANES).astype(jnp.bfloat16),
        ((0, round_up(shard_rows, 16) - shard_rows), (0, 0)),
    )


def weight_shapes(layout):
    shapes = []
    for entry_shape in layout:
        is_matrix = len(entry_shape) == 2 and entry_shape[0] > 9
        kind = jnp.bfloat16 if is_matrix else jnp.float32
        shape = entry_shape if len(entry_shape) == 2 else (1,) + entry_shape
        shapes.append(shaped(shape, kind))
    return shapes


def unpack_joined(gathered, layouts, row_counts):
    shard_count = gathered.shape[0]

    def kernel(gathered_ref, *refs):
        dense_ref, narrow_ref = refs[-2:]
        first_row = 0
        first_out = 0
        for layout, shard_rows in zip(layouts, row_counts):
            padded_rows = round_up(shard_rows, 16)

            def spread(index, carry, shard_rows=shard_rows, first=first_row, rows=padded_rows):
                dense_ref[pl.ds(index * shard_rows, rows), :] = gathered_ref[
                    index, first : first + rows, :
                ].astype(jnp.float32)
                return carry

            out_refs = refs[first_out : first_out + len(layout)]
            unpack_group(
                layout, shard_rows, shard_count, spread, out_refs, dense_ref, narrow_ref
            )
            first_row += padded_rows
            first_out += len(layout)

    results = pl.pallas_call(
        kernel,
        out_shape=[shape for layout in layouts for shape in weight_shapes(layout)],
        scratch_shapes=work_scratch(layouts, row_counts, shard_count),
        compiler_params=PARAMS,
        name="unpack_joined",
    )(gathered)
    groups = []
    for layout in layouts:
        groups.append(results[: len(layout)])
        results = results[len(layout) :]
    return groups


def swap(values, axis, bit):
    return lax.ppermute(
        values, axis, [(place, place ^ bit) for place in range(lax.axis_size(axis))]
    )


def bit_orders(count):
    bits = [1 << place for place in range(count.bit_length() - 1)]
    return [bits, bits[1::-1] + bits[2:]]


def device_place():
    return jnp.stack([lax.axis_index("dp"), lax.axis_index("fsdp")]).astype(jnp.int32)


PLACE_SPEC = pl.BlockSpec(memory_space=pltpu.SMEM)


def gather_halves(rows, orders):
    half = rows.shape[0] // 32 * 16
    gathered = []
    for piece, order in zip((rows[:half], rows[half:]), orders):
        held = piece[None]
        for bit in order:
            held = jnp.concatenate([held, swap(held, "fsdp", bit)], axis=0)
        for bit in bit_orders(lax.axis_size("dp"))[0]:
            held = jnp.concatenate([held, swap(held, "dp", bit)], axis=0)
        gathered.append(held)
    return gathered


def unpack_halves(halves, place, layout, shard_rows, orders):
    shard_count = halves[0].shape[0]
    chips = lax.axis_size("fsdp")
    half = halves[0].shape[1]

    def kernel(place_ref, *refs):
        half_refs = refs[:2]
        out_refs = refs[2:-2]
        dense_ref, narrow_ref = refs[-2:]

        def spread(index, carry):
            apart = (index % chips) ^ place_ref[1]
            cores = (index // chips) ^ place_ref[0]
            for number in range(2):
                position = cores * chips
                for step, bit in enumerate(orders[number]):
                    position = position + ((apart // bit) % 2) * (1 << step)
                rows = half_refs[number].shape[1]
                dense_ref[pl.ds(index * shard_rows + number * half, rows), :] = half_refs[number][
                    position
                ].astype(jnp.float32)
            return carry

        unpack_group(layout, shard_rows, shard_count, spread, out_refs, dense_ref, narrow_ref)

    vmem_spec = pl.BlockSpec(memory_space=pltpu.VMEM)
    return pl.pallas_call(
        kernel,
        in_specs=[PLACE_SPEC, vmem_spec, vmem_spec],
        out_shape=weight_shapes(layout),
        scratch_shapes=work_scratch([layout], [shard_rows], shard_count),
        compiler_params=PARAMS,
        name="unpack_halves",
    )(place, *halves)


def pack_group(layout, sources, in_refs, dense_ref, narrow_ref):
    places = layout_places(layout)
    used_rows = (places[-1][1] + math.prod(places[-1][0])) // LANES
    tail = dense_ref.shape[0] - used_rows
    dense_ref[pl.ds(used_rows, tail), :] = jnp.zeros((tail, LANES), jnp.float32)

    for (operand, first_row), (entry_shape, offset) in zip(sources, places):
        in_ref = in_refs[operand]
        rows = math.prod(entry_shape[:-1])
        cols = entry_shape[-1]
        narrow = is_narrow(entry_shape, offset)

        def copy_rows(start, amount):
            for part in range(-(-cols // LANES)):
                lanes = min(LANES, cols - part * LANES)
                piece = in_ref[pl.ds(first_row + start, amount), part * LANES : part * LANES + lanes]
                if narrow:
                    narrow_ref[part, pl.ds(offset // D3 + start, amount), 0:lanes] = piece
                else:
                    stride = cols // LANES
                    base = offset // LANES + part + start * stride
                    dense_ref[pl.ds(base, amount, stride=stride), :] = piece

        if rows < 32:
            copy_rows(0, rows)
        else:
            for_chunks(0, rows, 32, copy_rows)

    if narrow and (offset // D3 + rows) % 2 == 1:
        beyond = offset // D3 + rows
        narrow_ref[:, beyond : beyond + 1, :] = jnp.zeros((3, 1, LANES), jnp.float32)

    def narrow_step(start, amount):
        even_rows = pl.ds(2 * start, amount, stride=2)
        odd_rows = pl.ds(2 * start + 1, amount, stride=2)
        low_lanes = lax.broadcasted_iota(jnp.int32, (amount, LANES), 1) < LANES // 2
        even = [narrow_ref[part, even_rows, :] for part in range(3)]
        odd = [pltpu.roll(narrow_ref[part, odd_rows, :], LANES // 2, 1) for part in range(3)]
        joined = [
            even[0],
            even[1],
            jnp.where(low_lanes, even[2], odd[0]),
            jnp.where(low_lanes, odd[0], odd[1]),
            jnp.where(low_lanes, odd[1], odd[2]),
        ]
        for part in range(5):
            dense_ref[pl.ds(5 * start + part, amount, stride=5), :] = joined[part]

    for first, last in narrow_ranges(layout):
        for_chunks(first, last, PAIR_CHUNK, narrow_step)


def pack_grads(place, groups, parts):
    chips = lax.axis_size("fsdp")
    shard_count = lax.axis_size("dp") * chips
    layouts = [group[2] for group in groups]
    row_counts = [group[3] for group in groups]
    counts = [len(group[0]) for group in groups]

    def kernel(place_ref, *refs):
        out_refs = refs[sum(counts) : sum(counts) + len(parts)]
        dense_ref, narrow_ref = refs[-2:]
        first = 0
        for number, (operands, sources, layout, shard_rows) in enumerate(groups):
            in_refs = refs[first : first + len(operands)]
            first += len(operands)
            pack_group(layout, sources, in_refs, dense_ref, narrow_ref)

            def cut(index, carry, number=number, shard_rows=shard_rows):
                for out_ref, (pieces, core, turned) in zip(out_refs, parts):
                    out_row = 0
                    for group, first_row, rows in pieces:
                        if group == number:
                            chip = index ^ place_ref[1] if turned else index
                            shard = (place_ref[0] ^ core) * chips + chip
                            out_ref[index, out_row : out_row + rows, :] = dense_ref[
                                pl.ds(shard * shard_rows + first_row, rows), :
                            ].astype(out_ref.dtype)
                        out_row += rows
                return carry

            lax.fori_loop(0, chips, cut, 0)

    vmem_spec = pl.BlockSpec(memory_space=pltpu.VMEM)
    return pl.pallas_call(
        kernel,
        in_specs=[PLACE_SPEC] + [vmem_spec] * sum(counts),
        out_shape=[
            shaped((chips, sum(piece[2] for piece in pieces), LANES), WIRE_TYPE)
            for pieces, core, turned in parts
        ],
        scratch_shapes=work_scratch(layouts, row_counts, shard_count),
        compiler_params=PARAMS,
        name="pack_grads",
    )(place, *[operand for group in groups for operand in group[0]])


def add_rounded(kept, received):
    return (kept.astype(jnp.float32) + received.astype(jnp.float32)).astype(WIRE_TYPE)


def flat_rows(rows, shard_rows):
    return rows[:shard_rows].astype(jnp.float32).reshape(-1)


def sum_cores(parts):
    parts = list(parts)
    while len(parts) > 1:
        half = len(parts) // 2
        parts = [
            add_rounded(kept, swap(sent, "dp", half))
            for kept, sent in zip(parts[:half], parts[half:])
        ]
    return parts[0]


def scatter_half(parts, order):
    held = sum_cores(parts)
    left = sorted(order, reverse=True)
    held = held.reshape([2] * len(left) + list(held.shape[1:]))
    for bit in order:
        axis = left.index(bit)
        left.remove(bit)
        kept = lax.index_in_dim(held, 0, axis, keepdims=False)
        sent = lax.index_in_dim(held, 1, axis, keepdims=False)
        held = add_rounded(kept, swap(sent, "fsdp", bit))
    return held


def sum_devices(value):
    for axis in AXES:
        for bit in bit_orders(lax.axis_size(axis))[0]:
            value = value + swap(value, axis, bit)
    return value


def dot(left, right):
    return lax.dot_general(
        left, right, (((1,), (0,)), ((), ())), preferred_element_type=jnp.float32
    )


def dot_nt(left, right):
    return lax.dot_general(
        left, right, (((1,), (1,)), ((), ())), preferred_element_type=jnp.float32
    )


def dot_tn(left, right):
    return lax.dot_general(
        left, right, (((0,), (0,)), ((), ())), preferred_element_type=jnp.float32
    )


def rows_sum(values):
    return jnp.sum(values, axis=0, keepdims=True)


def norm_parts(values):
    centred = values - jnp.mean(values, axis=-1, keepdims=True)
    spread = jnp.mean(centred * centred, axis=-1, keepdims=True)
    scale = lax.rsqrt(spread + 1e-06)
    return centred * scale, scale


def norm_grad(unit, scale, gain_row, gradient):
    inner = gradient * gain_row
    first = jnp.mean(inner, axis=-1, keepdims=True)
    second = jnp.mean(inner * unit, axis=-1, keepdims=True)
    return scale * (inner - first - unit * second)


def column_mask(rows, lanes, side, width):
    places = lax.broadcasted_iota(jnp.int32, (rows, lanes), 0)
    return (places & (width - 1)) < side


def softmax_rows(query, key, valid):
    scores = jnp.where(valid, dot_nt(query, key) * 0.125, -1e30)
    powers = jnp.exp(scores - jnp.max(scores, axis=-1, keepdims=True))
    return powers * (1.0 / jnp.sum(powers, axis=-1, keepdims=True))


def split_lanes(values):
    rows, channels = values.shape
    pieces = []
    for first in range(0, channels, LANES):
        piece = values[:, first : min(first + LANES, channels)]
        if piece.shape[1] < LANES:
            rest = jnp.zeros((rows, LANES - piece.shape[1]), values.dtype)
            piece = jnp.concatenate([piece, rest], axis=1)
        pieces.append(piece)
    return pieces


def join_lanes(pieces, channels):
    return jnp.concatenate(pieces, axis=1)[:, :channels]


def pair_place(width, part):
    return pl.ds((part // 2) * width + part % 2, width // 2, stride=2)


def pair_part(grid_ref, width, part, channels):
    pieces = []
    for index in range(grid_ref.shape[0]):
        piece = grid_ref[index, :, pair_place(width, part), :]
        pieces.append(piece.reshape(piece.shape[0] * piece.shape[1], LANES))
    return join_lanes(pieces, channels).astype(jnp.bfloat16)


def attend_kernel(channels, width, has_reduction, *refs):
    if has_reduction:
        (
            x_ref, valid_ref, gain_ref, bias_ref, wq_ref, bq_ref, wr_ref, br_ref, rgain_ref,
            rbias_ref, wp_ref, bv_ref, wo_ref, bo_ref, gain2_ref, bias2_ref,
            query_ref, pair_ref, mixed_ref, middle_ref, normed_ref, reduced_ref, grid_ref,
        ) = refs
    else:
        (
            x_ref, valid_ref, gain_ref, bias_ref, wq_ref, bq_ref,
            wp_ref, bv_ref, wo_ref, bo_ref, gain2_ref, bias2_ref,
            query_ref, pair_ref, mixed_ref, middle_ref, normed_ref,
        ) = refs
    inputs = x_ref[0].astype(jnp.float32)
    unit, _ = norm_parts(inputs)
    normed = (unit * gain_ref[...] + bias_ref[...]).astype(jnp.bfloat16)
    query_ref[0] = (dot(normed, wq_ref[...]) + bq_ref[...]).astype(jnp.bfloat16)
    if has_reduction:
        for index, piece in enumerate(split_lanes(normed.astype(jnp.float32))):
            grid_ref[index] = piece.reshape(grid_ref.shape[1:])
        reduced = br_ref[...]
        for part in range(4):
            reduced = reduced + dot(
                pair_part(grid_ref, width, part, channels),
                wr_ref[part * channels : (part + 1) * channels, :],
            )
        reduced_ref[0] = reduced
        unit, _ = norm_parts(reduced)
        source = (unit * rgain_ref[...] + rbias_ref[...]).astype(jnp.bfloat16)
    else:
        source = normed
    pair_ref[0, :, :channels] = dot(source, wp_ref[:, :channels]).astype(jnp.bfloat16)
    pair_ref[0, :, channels:] = (dot(source, wp_ref[:, channels:]) + bv_ref[...]).astype(
        jnp.bfloat16
    )
    valid = valid_ref[0] > 0.5
    for head in range(channels // HEAD):
        lanes = slice(head * HEAD, (head + 1) * HEAD)
        value_lanes = slice(channels + head * HEAD, channels + (head + 1) * HEAD)
        chances = softmax_rows(query_ref[0, :, lanes], pair_ref[0, :, lanes], valid)
        mixed_ref[0, :, lanes] = dot(
            chances.astype(jnp.bfloat16), pair_ref[0, :, value_lanes]
        ).astype(jnp.bfloat16)
    middle = inputs + (dot(mixed_ref[0], wo_ref[...]) + bo_ref[...])
    middle_ref[0] = middle
    unit, _ = norm_parts(middle)
    normed_ref[0] = (unit * gain2_ref[...] + bias2_ref[...]).astype(jnp.bfloat16)


def whole(shape):
    return pl.BlockSpec(shape, lambda *place: (0,) * len(shape))


def image_block(array):
    return pl.BlockSpec((1,) + array.shape[1:], lambda image: (image,) + (0,) * (len(array.shape) - 1))


def shaped(shape, kind):
    return jax.ShapeDtypeStruct(shape, kind)


PARAMS = pltpu.CompilerParams(vmem_limit_bytes=61000 * 1024)


def attend_block(inputs, valid, weights, width):
    images, tokens, channels = inputs.shape
    has_reduction = len(weights) == 14
    keys = valid.shape[2]
    outs = [
        shaped((images, tokens, channels), jnp.bfloat16),
        shaped((images, keys, 2 * channels), jnp.bfloat16),
        shaped((images, tokens, channels), jnp.bfloat16),
        shaped((images, tokens, channels), jnp.float32),
        shaped((images, tokens, channels), jnp.bfloat16),
    ]
    scratch = []
    if has_reduction:
        outs.append(shaped((images, keys, channels), jnp.float32))
        grid_shape = (-(-channels // LANES), tokens // (2 * width), 2 * width, LANES)
        scratch.append(pltpu.VMEM(grid_shape, jnp.float32))
    return pl.pallas_call(
        lambda *refs: attend_kernel(channels, width, has_reduction, *refs),
        grid=(images,),
        in_specs=[image_block(inputs), image_block(valid)] + [whole(w.shape) for w in weights],
        out_specs=[image_block(out) for out in outs],
        out_shape=outs,
        scratch_shapes=scratch,
        compiler_params=PARAMS,
        name="attend",
    )(inputs, valid, *weights)


def mix_kernel(side, width, *refs):
    (
        normed_ref, middle_ref, we_ref, be_ref, kd_ref, bd_ref, wc_ref, bc_ref,
        out_ref, mixed_ref, slope_ref, pad_ref,
    ) = refs
    tokens = side * width
    lanes = we_ref.shape[1]
    block = pl.program_id(1)
    hidden = dot(normed_ref[0], we_ref[...]) + be_ref[...]
    pad_ref[0:width, :] = jnp.zeros((width, lanes), jnp.float32)
    pad_ref[width + tokens : 2 * width + tokens, :] = jnp.zeros((width, lanes), jnp.float32)
    pad_ref[width : width + tokens, :] = jnp.where(
        column_mask(tokens, lanes, side, width), hidden, 0.0
    )

    def step(row, carry):
        start = pl.multiple_of(row * width, width)
        rows = [pad_ref[pl.ds(start + up * width, width), :] for up in range(3)]
        sums = [
            kd_ref[col : col + 1, :] * rows[0]
            + kd_ref[3 + col : 4 + col, :] * rows[1]
            + kd_ref[6 + col : 7 + col, :] * rows[2]
            for col in range(3)
        ]
        value = (
            sums[1]
            + pltpu.roll(sums[0], 1, 0)
            + pltpu.roll(sums[2], width - 1, 0)
            + bd_ref[...]
        )
        share = 0.5 + 0.5 * lax.erf(value * math.sqrt(0.5))
        bell = jnp.exp(-0.5 * value * value) * (1.0 / math.sqrt(2.0 * math.pi))
        mixed_ref[0, pl.ds(start, width), :] = (value * share).astype(jnp.bfloat16)
        slope_ref[0, pl.ds(start, width), :] = (share + value * bell).astype(jnp.bfloat16)
        return carry

    lax.fori_loop(0, side, step, 0)
    result = dot(mixed_ref[0], wc_ref[...])

    @pl.when(block == 0)
    def _():
        out_ref[0] = middle_ref[0] + bc_ref[...] + result

    @pl.when(block > 0)
    def _():
        out_ref[0] += result


def mix_block(normed, middle, weights, side, width, lanes):
    we, be, kd, bd, wc, bc = weights
    images, tokens, channels = middle.shape
    units = we.shape[1]
    outs = [
        shaped(middle.shape, jnp.float32),
        shaped((images, tokens, units), jnp.bfloat16),
        shaped((images, tokens, units), jnp.bfloat16),
    ]
    token_spec = pl.BlockSpec((1, tokens, channels), lambda i, c: (i, 0, 0))
    unit_spec = pl.BlockSpec((1, tokens, lanes), lambda i, c: (i, 0, c))

    def row_spec(rows):
        return pl.BlockSpec((rows, lanes), lambda i, c: (0, c))

    return pl.pallas_call(
        lambda *refs: mix_kernel(side, width, *refs),
        grid=(images, units // lanes),
        in_specs=[
            token_spec,
            token_spec,
            row_spec(channels),
            row_spec(1),
            row_spec(9),
            row_spec(1),
            pl.BlockSpec((lanes, channels), lambda i, c: (c, 0)),
            pl.BlockSpec((1, channels), lambda i, c: (0, 0)),
        ],
        out_specs=[token_spec, unit_spec, unit_spec],
        out_shape=outs,
        scratch_shapes=[pltpu.VMEM((tokens + 2 * width, lanes), jnp.float32)],
        compiler_params=PARAMS,
        name="mix",
    )(normed, middle, we, be, kd, bd, wc, bc)


def mix_back_kernel(side, width, *refs):
    (
        normed_ref, grad_ref, mixed_ref, slope_ref, we_ref, be_ref, kd_ref, wc_ref,
        dnormed_ref, dwe_ref, dwc_ref, drows_ref, pad_ref, dpad_ref, dhid_ref,
    ) = refs
    tokens = side * width
    lanes = we_ref.shape[1]
    block = pl.program_id(0)
    image = pl.program_id(1)
    gradient = grad_ref[0].astype(jnp.bfloat16)
    inside = column_mask(tokens, lanes, side, width)
    hidden = dot(normed_ref[0], we_ref[...]) + be_ref[...]
    for ref in (pad_ref, dpad_ref):
        ref[0:width, :] = jnp.zeros((width, lanes), jnp.float32)
        ref[width + tokens : 2 * width + tokens, :] = jnp.zeros((width, lanes), jnp.float32)
    pad_ref[width : width + tokens, :] = jnp.where(inside, hidden, 0.0)
    dpad_ref[width : width + tokens, :] = dot_nt(gradient, wc_ref[...]) * slope_ref[0].astype(
        jnp.float32
    )

    @pl.when(image == 0)
    def _():
        drows_ref[...] = jnp.zeros(drows_ref.shape, jnp.float32)
        dwe_ref[...] = jnp.zeros(dwe_ref.shape, jnp.float32)
        dwc_ref[...] = jnp.zeros(dwc_ref.shape, jnp.float32)

    row_inside = column_mask(width, lanes, side, width)

    def fold(values):
        total = values[0:8]
        for start in range(8, width, 8):
            total = total + values[start : start + 8]
        return total

    def step(row, sums):
        start = pl.multiple_of(row * width, width)
        rows = [pad_ref[pl.ds(start + up * width, width), :] for up in range(3)]
        drows = [dpad_ref[pl.ds(start + up * width, width), :] for up in range(3)]
        turned = [
            pltpu.roll(drows[1], width - 1, 0),
            drows[1],
            pltpu.roll(drows[1], 1, 0),
        ]
        found = []
        for up in range(3):
            for col in range(3):
                found.append(sums[3 * up + col] + fold(turned[col] * rows[up]))
        found.append(sums[9] + fold(drows[1]))
        parts = [
            kd_ref[col : col + 1, :] * drows[2]
            + kd_ref[3 + col : 4 + col, :] * drows[1]
            + kd_ref[6 + col : 7 + col, :] * drows[0]
            for col in range(3)
        ]
        value = parts[1] + pltpu.roll(parts[0], width - 1, 0) + pltpu.roll(parts[2], 1, 0)
        rounded = jnp.where(row_inside, value, 0.0).astype(jnp.bfloat16)
        dhid_ref[pl.ds(start, width), :] = rounded
        found.append(sums[10] + fold(rounded.astype(jnp.float32)))
        return tuple(found)

    zero = jnp.zeros((8, lanes), jnp.float32)
    totals = lax.fori_loop(0, side, step, (zero,) * 11)
    for index in range(11):
        drows_ref[index : index + 1, :] += rows_sum(totals[index])
    dhidden = dhid_ref[...]
    dwe_ref[...] += dot_tn(normed_ref[0], dhidden)
    dwc_ref[...] += dot_tn(mixed_ref[0], gradient)
    result = dot_nt(dhidden, we_ref[...])

    @pl.when(block == 0)
    def _():
        dnormed_ref[image] = result

    @pl.when(block > 0)
    def _():
        dnormed_ref[image] += result


def mix_back(normed, gradient, mixed, slope, weights, side, width, lanes):
    we, be, kd, bd, wc, bc = weights
    images, tokens, channels = normed.shape
    units = we.shape[1]
    token_spec = pl.BlockSpec((1, tokens, channels), lambda c, i: (i, 0, 0))
    unit_spec = pl.BlockSpec((1, tokens, lanes), lambda c, i: (i, 0, c))

    def row_spec(rows):
        return pl.BlockSpec((rows, lanes), lambda c, i: (0, c))

    col_spec = pl.BlockSpec((lanes, channels), lambda c, i: (c, 0))
    return pl.pallas_call(
        lambda *refs: mix_back_kernel(side, width, *refs),
        grid=(units // lanes, images),
        in_specs=[
            token_spec,
            token_spec,
            unit_spec,
            unit_spec,
            row_spec(channels),
            row_spec(1),
            row_spec(9),
            col_spec,
        ],
        out_specs=[whole((images, tokens, channels)), row_spec(channels), col_spec, row_spec(16)],
        out_shape=[
            shaped((images, tokens, channels), jnp.float32),
            shaped((channels, units), jnp.float32),
            shaped((units, channels), jnp.float32),
            shaped((16, units), jnp.float32),
        ],
        scratch_shapes=[
            pltpu.VMEM((tokens + 2 * width, lanes), jnp.float32),
            pltpu.VMEM((tokens + 2 * width, lanes), jnp.float32),
            pltpu.VMEM((tokens, lanes), jnp.bfloat16),
        ],
        compiler_params=PARAMS,
        name="mix_back",
    )(normed, gradient, mixed, slope, we, be, kd, wc)


def attend_back_kernel(channels, width, has_reduction, *refs):
    if has_reduction:
        (
            x_ref, valid_ref, grad_ref, dnormed_ref, middle_ref, query_ref, pair_ref, mixed_ref,
            reduced_ref, gain_ref, bias_ref, wq_ref, wr_ref, rgain_ref, rbias_ref, wp_ref, wo_ref,
            gain2_ref,
            dx_ref, dwq_ref, dwp_ref, dwo_ref, vec_ref, dwr_ref,
            dquery_ref, dpair_ref, grid_ref, dgrid_ref,
        ) = refs
    else:
        (
            x_ref, valid_ref, grad_ref, dnormed_ref, middle_ref, query_ref, pair_ref, mixed_ref,
            gain_ref, bias_ref, wq_ref, wp_ref, wo_ref, gain2_ref,
            dx_ref, dwq_ref, dwp_ref, dwo_ref, vec_ref,
            dquery_ref, dpair_ref,
        ) = refs

    @pl.when(pl.program_id(0) == 0)
    def _():
        sums = [dwq_ref, dwp_ref, dwo_ref, vec_ref] + ([dwr_ref] if has_reduction else [])
        for ref in sums:
            ref[...] = jnp.zeros(ref.shape, jnp.float32)

    def add_row(index, row):
        vec_ref[index : index + 1, :] += row

    gradient = grad_ref[0].astype(jnp.float32)
    add_row(0, rows_sum(gradient.astype(jnp.bfloat16).astype(jnp.float32)))
    dnormed = dnormed_ref[0]
    unit, scale = norm_parts(middle_ref[0])
    add_row(1, rows_sum(dnormed * unit))
    add_row(2, rows_sum(dnormed))
    dmiddle = gradient + norm_grad(unit, scale, gain2_ref[...], dnormed)
    dx_ref[0] = dmiddle
    doutput = dmiddle.astype(jnp.bfloat16)
    add_row(3, rows_sum(doutput.astype(jnp.float32)))
    dwo_ref[...] += dot_tn(mixed_ref[0], doutput)
    dmixed = dot_nt(doutput, wo_ref[...]).astype(jnp.bfloat16)
    valid = valid_ref[0] > 0.5
    for head in range(channels // HEAD):
        lanes = slice(head * HEAD, (head + 1) * HEAD)
        value_lanes = slice(channels + head * HEAD, channels + (head + 1) * HEAD)
        query = query_ref[0, :, lanes]
        key = pair_ref[0, :, lanes]
        chances = softmax_rows(query, key, valid)
        dhead = dmixed[:, lanes]
        dchances = dot_nt(dhead, pair_ref[0, :, value_lanes])
        dpair_ref[:, value_lanes] = dot_tn(chances.astype(jnp.bfloat16), dhead).astype(
            jnp.bfloat16
        )
        weighted = chances * dchances
        dscores = (
            weighted - chances * jnp.sum(weighted, axis=-1, keepdims=True)
        ).astype(jnp.bfloat16)
        dquery_ref[:, lanes] = (dot(dscores, key) * 0.125).astype(jnp.bfloat16)
        dpair_ref[:, lanes] = (dot_tn(dscores, query) * 0.125).astype(jnp.bfloat16)
    dquery = dquery_ref[...]
    dpair = dpair_ref[...]
    unit, scale = norm_parts(x_ref[0].astype(jnp.float32))
    normed = (unit * gain_ref[...] + bias_ref[...]).astype(jnp.bfloat16)
    add_row(4, rows_sum(dquery.astype(jnp.float32)))
    add_row(5, rows_sum(dpair[:, channels:].astype(jnp.float32)))
    dwq_ref[...] += dot_tn(normed, dquery)
    total = dot_nt(dquery, wq_ref[...])
    dsource = dot_nt(dpair, wp_ref[...])
    if has_reduction:
        runit, rscale = norm_parts(reduced_ref[0])
        source = (runit * rgain_ref[...] + rbias_ref[...]).astype(jnp.bfloat16)
        dwp_ref[...] += dot_tn(source, dpair)
        add_row(8, rows_sum(dsource * runit))
        add_row(9, rows_sum(dsource))
        dreduced = norm_grad(runit, rscale, rgain_ref[...], dsource).astype(jnp.bfloat16)
        add_row(10, rows_sum(dreduced.astype(jnp.float32)))
        for index, piece in enumerate(split_lanes(normed.astype(jnp.float32))):
            grid_ref[index] = piece.reshape(grid_ref.shape[1:])
        for index, piece in enumerate(split_lanes(total)):
            dgrid_ref[index] = piece.reshape(dgrid_ref.shape[1:])
        for part in range(4):
            rows = slice(part * channels, (part + 1) * channels)
            dwr_ref[rows, :] += dot_tn(pair_part(grid_ref, width, part, channels), dreduced)
            for index, piece in enumerate(split_lanes(dot_nt(dreduced, wr_ref[rows, :]))):
                dgrid_ref[index, :, pair_place(width, part), :] += piece.reshape(
                    dgrid_ref.shape[1], width // 2, LANES
                )
        total = join_lanes(
            [dgrid_ref[index].reshape(total.shape[0], LANES) for index in range(dgrid_ref.shape[0])],
            channels,
        )
    else:
        dwp_ref[...] += dot_tn(normed, dpair)
        total = total + dsource
    add_row(6, rows_sum(total * unit))
    add_row(7, rows_sum(total))
    dx_ref[0] += norm_grad(unit, scale, gain_ref[...], total)


def attend_back(inputs, valid, gradient, dnormed, saved, weights, width):
    query, pair, mixed, middle, normed = saved[:5]
    images, tokens, channels = middle.shape
    has_reduction = len(saved) == 6
    keys = valid.shape[2]
    operands = [inputs, valid, gradient, dnormed, middle, query, pair, mixed]
    outs = [
        shaped((images, tokens, channels), jnp.float32),
        shaped((channels, channels), jnp.float32),
        shaped((channels, 2 * channels), jnp.float32),
        shaped((channels, channels), jnp.float32),
        shaped((16, channels), jnp.float32),
    ]
    scratch = [
        pltpu.VMEM((tokens, channels), jnp.bfloat16),
        pltpu.VMEM((keys, 2 * channels), jnp.bfloat16),
    ]
    if has_reduction:
        gain, bias, wq, bq, wr, br, rgain, rbias, wp, bv, wo, bo, gain2, bias2 = weights
        used = [gain, bias, wq, wr, rgain, rbias, wp, wo, gain2]
        operands.append(saved[5])
        outs.append(shaped((4 * channels, channels), jnp.float32))
        grid_shape = (-(-channels // LANES), tokens // (2 * width), 2 * width, LANES)
        scratch += [pltpu.VMEM(grid_shape, jnp.float32), pltpu.VMEM(grid_shape, jnp.float32)]
    else:
        gain, bias, wq, bq, wp, bv, wo, bo, gain2, bias2 = weights
        used = [gain, bias, wq, wp, wo, gain2]
    return pl.pallas_call(
        lambda *refs: attend_back_kernel(channels, width, has_reduction, *refs),
        grid=(images,),
        in_specs=[image_block(op) for op in operands] + [whole(w.shape) for w in used],
        out_specs=[image_block(outs[0])] + [whole(out.shape) for out in outs[1:]],
        out_shape=outs,
        scratch_shapes=scratch,
        compiler_params=PARAMS,
        name="attend_back",
    )(*operands, *used)


def tap_place(width, tap, row):
    first = LEAD + (tap // 3) * width + tap % 3 - 1
    return pl.ds(first + 2 * width * row, width // 2, stride=2)


def load_tap(grid_ref, side, width, tap, channels):
    pieces = []
    for index in range(grid_ref.shape[0]):
        rows = [grid_ref[index, tap_place(width, tap, row), :] for row in range(side // 2)]
        pieces.append(jnp.concatenate(rows, axis=0))
    return join_lanes(pieces, channels).astype(jnp.bfloat16)


def fill_grid(grid_ref, values, width):
    rows = grid_ref.shape[1]
    first = LEAD + width
    last = first + values.shape[0]
    for index, piece in enumerate(split_lanes(values)):
        grid_ref[index, 0:first, :] = jnp.zeros((first, LANES), jnp.float32)
        grid_ref[index, first:last, :] = piece
        grid_ref[index, last:rows, :] = jnp.zeros((rows - last, LANES), jnp.float32)


LEAD = 8


def embed_kernel(side, width, *refs):
    x_ref, gain_ref, bias_ref, w_ref, b_ref, pgain_ref, pbias_ref = refs[:7]
    out_ref, patch_ref, grid_ref = refs[7:]
    tokens, channels = x_ref.shape[1:]
    unit, _ = norm_parts(x_ref[0])
    normed = (unit * gain_ref[...] + bias_ref[...]).astype(jnp.bfloat16).astype(jnp.float32)
    inside = column_mask(tokens, channels, side, width)
    fill_grid(grid_ref, jnp.where(inside, normed, 0.0), width)
    patch = b_ref[...]
    for tap in range(9):
        patch = patch + dot(
            load_tap(grid_ref, side, width, tap, channels),
            w_ref[tap * channels : (tap + 1) * channels, :]
        )
    patch_ref[0] = patch
    unit, _ = norm_parts(patch)
    out_ref[0] = unit * pgain_ref[...] + pbias_ref[...]


def embed_block(inputs, weights, side, width):
    images, tokens, channels = inputs.shape
    units = weights[2].shape[1]
    outs = [shaped((images, tokens // 4, units), jnp.float32)] * 2
    return pl.pallas_call(
        lambda *refs: embed_kernel(side, width, *refs),
        grid=(images,),
        in_specs=[image_block(inputs)] + [whole(w.shape) for w in weights],
        out_specs=[image_block(out) for out in outs],
        out_shape=outs,
        scratch_shapes=[pltpu.VMEM((-(-channels // LANES), LEAD + (side + 3) * width, LANES), jnp.float32)],
        compiler_params=PARAMS,
        name="embed",
    )(inputs, *weights)


def embed_back_kernel(side, width, *refs):
    x_ref, grad_ref, patch_ref, gain_ref, bias_ref, w_ref, pgain_ref = refs[:7]
    dx_ref, dw_ref, vec_ref, pvec_ref, grid_ref, dgrid_ref = refs[7:]
    tokens, channels = x_ref.shape[1:]

    @pl.when(pl.program_id(0) == 0)
    def _():
        for ref in (dw_ref, vec_ref, pvec_ref):
            ref[...] = jnp.zeros(ref.shape, jnp.float32)

    gradient = grad_ref[0]
    punit, pscale = norm_parts(patch_ref[0])
    pvec_ref[0:1, :] += rows_sum(gradient * punit)
    pvec_ref[1:2, :] += rows_sum(gradient)
    dpatch = norm_grad(punit, pscale, pgain_ref[...], gradient).astype(jnp.bfloat16)
    pvec_ref[2:3, :] += rows_sum(dpatch.astype(jnp.float32))
    unit, scale = norm_parts(x_ref[0])
    normed = (unit * gain_ref[...] + bias_ref[...]).astype(jnp.bfloat16).astype(jnp.float32)
    inside = column_mask(tokens, channels, side, width)
    fill_grid(grid_ref, jnp.where(inside, normed, 0.0), width)
    dgrid_ref[...] = jnp.zeros(dgrid_ref.shape, jnp.float32)
    half = width // 2
    for tap in range(9):
        rows = slice(tap * channels, (tap + 1) * channels)
        dw_ref[rows, :] += dot_tn(load_tap(grid_ref, side, width, tap, channels), dpatch)
        for index, piece in enumerate(split_lanes(dot_nt(dpatch, w_ref[rows, :]))):
            for row in range(side // 2):
                dgrid_ref[index, tap_place(width, tap, row), :] += piece[
                    row * half : (row + 1) * half, :
                ]
    first = LEAD + width
    pieces = [dgrid_ref[index, first : first + tokens, :] for index in range(dgrid_ref.shape[0])]
    total = jnp.where(inside, join_lanes(pieces, channels), 0.0)
    vec_ref[0:1, :] += rows_sum(total * unit)
    vec_ref[1:2, :] += rows_sum(total)
    dx_ref[0] = norm_grad(unit, scale, gain_ref[...], total)


def embed_back(inputs, gradient, patch, weights, side, width):
    gain, bias, w, b, pgain, pbias = weights
    images, tokens, channels = inputs.shape
    units = w.shape[1]
    outs = [
        shaped(inputs.shape, jnp.float32),
        shaped(w.shape, jnp.float32),
        shaped((8, channels), jnp.float32),
        shaped((8, units), jnp.float32),
    ]
    operands = [inputs, gradient, patch]
    used = [gain, bias, w, pgain]
    grid_scratch = pltpu.VMEM((-(-channels // LANES), LEAD + (side + 3) * width, LANES), jnp.float32)
    return pl.pallas_call(
        lambda *refs: embed_back_kernel(side, width, *refs),
        grid=(images,),
        in_specs=[image_block(op) for op in operands] + [whole(u.shape) for u in used],
        out_specs=[image_block(outs[0])] + [whole(out.shape) for out in outs[1:]],
        out_shape=outs,
        scratch_shapes=[grid_scratch, grid_scratch],
        compiler_params=PARAMS,
        name="embed_back",
    )(*operands, *used)


def to_grid(values, side, width):
    images, tokens, channels = values.shape
    grid = values.reshape(images, side, side, channels)
    grid = jnp.pad(grid, ((0, 0), (0, 0), (0, width - side), (0, 0)))
    return grid.reshape(images, side * width, channels)


def from_grid(values, side, width):
    images, tokens, channels = values.shape
    grid = values.reshape(images, side, width, channels)[:, :, :side]
    return grid.reshape(images, side * side, channels)


def key_mask(row_counts, col_counts, side, width):
    places = jnp.arange(side * width, dtype=jnp.int32)
    valid = ((places // width)[None, :] < row_counts[:, None]) & (
        (places % width)[None, :] < col_counts[:, None]
    )
    return valid.astype(jnp.float32)[:, None, :]


def block_sources(has_reduction):
    reduction = [(7, 0), (3, 10), (3, 8), (3, 9)] if has_reduction else []
    return (
        [(3, 6), (3, 7), (0, 0), (3, 4)]
        + reduction
        + [(1, 0), (3, 5), (2, 0), (3, 3), (3, 1), (3, 2)]
        + [(4, 0), (6, 10), (6, 0), (6, 9), (5, 0), (3, 0)]
    )


EMBED_SOURCES = [(1, 0), (1, 1), (0, 0), (2, 2), (2, 0), (2, 1)]


def adamw_update(weights, mean_old, square_old, gradient, clip_factor, rate_value, fix_one):
    clipped = gradient * clip_factor
    mean_new = 0.5 * mean_old + 0.5 * clipped
    square_new = 0.5 * square_old + 0.5 * clipped * clipped
    updated = weights * (1.0 - rate_value * 0.05) - rate_value * (mean_new / fix_one) / (
        jnp.sqrt(square_new / fix_one) + 1e-08
    )
    return (updated, mean_new, square_new)


def shards(
    features,
    key_rows,
    key_cols,
    out_grad,
    lower_weights,
    lower_mean,
    lower_square,
    embed_weights,
    embed_mean,
    embed_square,
    upper_weights,
    upper_mean,
    upper_square,
    learn_rate,
):
    side, half = GRID, GRID // 2
    width = round_up(side, 32)
    half_width = width // 2
    key_valid = key_mask(key_rows, key_cols, half, half_width)
    cores = lax.axis_size("dp")
    orders = bit_orders(lax.axis_size("fsdp"))
    place = device_place()
    lower_rows, embed_rows, upper_rows = (
        flat.shape[0] // LANES for flat in (lower_weights, embed_weights, upper_weights)
    )
    lower_halves = gather_halves(
        local_rows(lower_weights), [order[2:] + order[:2] for order in orders]
    )
    rest_local = jnp.concatenate([local_rows(embed_weights), local_rows(upper_weights)], axis=0)
    *lower_halves, rest_local = lax.optimization_barrier((*lower_halves, rest_local))
    rest = lax.all_gather(rest_local, AXES, axis=0, tiled=False)
    lower = unpack_halves(
        lower_halves, place, LOWER_LAYOUT, lower_rows, [order[2:] + order[:2] for order in orders]
    )
    embed, upper = unpack_joined(rest, [EMBED_LAYOUT, UPPER_LAYOUT], [embed_rows, upper_rows])
    three_in = to_grid(features, side, width)
    grad_in = to_grid(out_grad, half, half_width)

    lower_saved = attend_block(three_in, key_valid, lower[:14], width)
    section_three, lower_mixed, lower_slope = mix_block(
        lower_saved[4], lower_saved[3], lower[14:], side, width, 256
    )
    section_four, patch = embed_block(section_three, embed, side, width)
    upper_saved = attend_block(section_four, key_valid, upper[:10], half_width)
    block_out, upper_mixed, upper_slope = mix_block(
        upper_saved[4], upper_saved[3], upper[10:], half, half_width, 512
    )

    def back(inputs, gradient, saved, mixed, slope, weights, first, side, width, lanes):
        dnormed, dwe, dwc, drows = mix_back(
            saved[4], gradient, mixed, slope, weights[first:], side, width, lanes
        )
        dx, dwq, dwp, dwo, vec, *rest = attend_back(
            inputs, key_valid, gradient, dnormed, saved, weights[:first], width
        )
        return dx, [dwq, dwp, dwo, vec, dwe, dwc, drows] + rest

    four_grad, upper_found = back(
        section_four, grad_in, upper_saved, upper_mixed, upper_slope, upper, 10, half, half_width, 512
    )
    three_grad, *embed_found = embed_back(section_three, four_grad, patch, embed, side, width)
    pieces = [(0, 0, round_up(embed_rows, 16)), (1, 0, round_up(upper_rows, 16))]
    wire = pack_grads(
        place,
        [
            (embed_found, EMBED_SOURCES, EMBED_LAYOUT, embed_rows),
            (upper_found, block_sources(False), UPPER_LAYOUT, upper_rows),
        ],
        [(pieces, core, False) for core in range(cores)],
    )
    rest_sum = sum_cores(wire)
    rest_sum, three_grad = lax.optimization_barrier((rest_sum, three_grad))
    rest_grad = lax.psum_scatter(rest_sum, "fsdp", scatter_dimension=0, tiled=False)
    input_grad, lower_found = back(
        three_in, three_grad, lower_saved, lower_mixed, lower_slope, lower, 14, side, width, 256
    )
    padded_rows = round_up(lower_rows, 16)
    half_rows = padded_rows // 32 * 16
    parts = []
    for first, rows in ((0, half_rows), (half_rows, padded_rows - half_rows)):
        parts += [([(0, first, rows)], core, True) for core in range(cores)]
    wire = pack_grads(
        place, [(lower_found, block_sources(True), LOWER_LAYOUT, lower_rows)], parts
    )
    lower_sum = jnp.concatenate(
        [scatter_half(wire[:cores], orders[0]), scatter_half(wire[cores:], orders[1])], axis=0
    )
    lower_grad = flat_rows(lower_sum, lower_rows)
    embed_grad = flat_rows(rest_grad, embed_rows)
    upper_grad = flat_rows(rest_grad[round_up(embed_rows, 16) :], upper_rows)
    input_grad = from_grid(input_grad, side, width)
    block_out = from_grid(block_out, half, half_width)
    local_squares = (
        jnp.sum(lower_grad * lower_grad)
        + jnp.sum(embed_grad * embed_grad)
        + jnp.sum(upper_grad * upper_grad)
    )
    squares = sum_devices(local_squares.reshape(1, 1))[0, 0]
    grad_norm = jnp.sqrt(squares)
    clip_factor = jnp.minimum(1.0, 5.0 / (grad_norm + 1e-06))
    rate_value = learn_rate[0]
    fix_one = 1.0 - 0.5**ADAM_STEP
    lower_new, lower_mean_new, lower_square_new = adamw_update(
        lower_weights, lower_mean, lower_square, lower_grad, clip_factor, rate_value, fix_one
    )
    embed_new, embed_mean_new, embed_square_new = adamw_update(
        embed_weights, embed_mean, embed_square, embed_grad, clip_factor, rate_value, fix_one
    )
    upper_new, upper_mean_new, upper_square_new = adamw_update(
        upper_weights, upper_mean, upper_square, upper_grad, clip_factor, rate_value, fix_one
    )
    return (
        block_out,
        input_grad,
        grad_norm.reshape(1),
        lower_grad,
        lower_new,
        lower_mean_new,
        lower_square_new,
        lower_new.astype(jnp.bfloat16),
        embed_grad,
        embed_new,
        embed_mean_new,
        embed_square_new,
        embed_new.astype(jnp.bfloat16),
        upper_grad,
        upper_new,
        upper_mean_new,
        upper_square_new,
        upper_new.astype(jnp.bfloat16),
    )


AXES = ("dp", "fsdp")
TOKENS = P(AXES, None, None)
FLAT = P(AXES)


def solution(mesh):
    return jax.shard_map(
        shards,
        mesh=mesh,
        in_specs=(
            TOKENS,
            FLAT,
            FLAT,
            TOKENS,
            FLAT,
            FLAT,
            FLAT,
            FLAT,
            FLAT,
            FLAT,
            FLAT,
            FLAT,
            FLAT,
            P(),
        ),
        out_specs=(
            TOKENS,
            TOKENS,
            P(),
            FLAT,
            FLAT,
            FLAT,
            FLAT,
            FLAT,
            FLAT,
            FLAT,
            FLAT,
            FLAT,
            FLAT,
            FLAT,
            FLAT,
            FLAT,
            FLAT,
            FLAT,
        ),
        check_vma=False,
    )
```

```python
import math

import jax
import jax.numpy as jnp
from jax import lax
from jax.experimental import pallas as pl
from jax.experimental.pallas import tpu as pltpu
from jax.sharding import PartitionSpec as P

D3 = 320
D4 = 512
HID3 = 1280
HID4 = 2048
HEAD = 64
GRID = 28
ADAM_STEP = 2
WIRE_TYPE = jnp.bfloat16


def block_layout(channels, units, has_reduction):
    row = (channels,)
    reduction = [(4 * channels, channels), row, row, row] if has_reduction else []
    return (
        [row, row, (channels, channels), row]
        + reduction
        + [(channels, 2 * channels), row, (channels, channels), row, row, row]
        + [(channels, units), (units,), (9, units), (units,), (units, channels), row]
    )


LOWER_LAYOUT = block_layout(D3, HID3, True)
UPPER_LAYOUT = block_layout(D4, HID4, False)
EMBED_LAYOUT = [(D3,), (D3,), (9 * D3, D4), (D4,), (D4,), (D4,)]


LANES = 128
PAIR_CHUNK = 32


def layout_places(layout):
    places = []
    offset = 0
    for entry_shape in layout:
        places.append((entry_shape, offset))
        offset = offset + math.prod(entry_shape)
    return places


def is_narrow(entry_shape, offset):
    return entry_shape[-1] % LANES != 0 or offset % LANES != 0


def narrow_ranges(layout):
    ranges = []
    for entry_shape, offset in layout_places(layout):
        if not is_narrow(entry_shape, offset):
            continue
        first = offset // D3
        last = first + math.prod(entry_shape) // D3
        if ranges and ranges[-1][1] == first:
            ranges[-1] = (ranges[-1][0], last)
        else:
            ranges.append((first, last))
    return [(first // 2, (last + 1) // 2) for first, last in ranges]


def round_up(amount, unit):
    return (amount + unit - 1) // unit * unit


def for_chunks(first, last, chunk, step):
    full = (last - first) // chunk

    def body(index, carry):
        step(first + index * chunk, chunk)
        return carry

    if full > 0:
        lax.fori_loop(0, full, body, 0)
    rest = (last - first) - full * chunk
    if rest > 0:
        step(first + full * chunk, rest)


def unpack_group(layout, shard_rows, shard_count, spread, out_refs, dense_ref, narrow_ref):
    lax.fori_loop(0, shard_count, spread, 0)

    def narrow_step(start, amount):
        parts = [
            dense_ref[pl.ds(5 * start + part, amount, stride=5), :] for part in range(5)
        ]
        low_lanes = lax.broadcasted_iota(jnp.int32, (amount, LANES), 1) < LANES // 2
        turned = [pltpu.roll(part, LANES // 2, 1) for part in parts[2:]]
        even_rows = pl.ds(2 * start, amount, stride=2)
        odd_rows = pl.ds(2 * start + 1, amount, stride=2)
        for part in range(3):
            narrow_ref[part, even_rows, :] = parts[part]
        narrow_ref[0, odd_rows, :] = jnp.where(low_lanes, turned[0], turned[1])
        narrow_ref[1, odd_rows, :] = jnp.where(low_lanes, turned[1], turned[2])
        narrow_ref[2, odd_rows, :] = turned[2]

    for first, last in narrow_ranges(layout):
        for_chunks(first, last, PAIR_CHUNK, narrow_step)

    for out_ref, (entry_shape, offset) in zip(out_refs, layout_places(layout)):
        rows = math.prod(entry_shape[:-1])
        cols = entry_shape[-1]
        narrow = is_narrow(entry_shape, offset)

        def copy_rows(start, amount):
            for part in range(-(-cols // LANES)):
                lanes = min(LANES, cols - part * LANES)
                if narrow:
                    piece = narrow_ref[part, pl.ds(offset // D3 + start, amount), :]
                else:
                    stride = cols // LANES
                    base = offset // LANES + part + start * stride
                    piece = dense_ref[pl.ds(base, amount, stride=stride), :]
                out_ref[pl.ds(start, amount), part * LANES : part * LANES + lanes] = piece[
                    :, :lanes
                ].astype(out_ref.dtype)

        if rows < 32:
            copy_rows(0, rows)
        else:
            for_chunks(0, rows, 32, copy_rows)


def dense_rows_of(layouts, row_counts, shard_count):
    return max(
        round_up(rows * shard_count + round_up(rows, 16), 16)
        for layout, rows in zip(layouts, row_counts)
    )


def narrow_rows_of(layouts):
    return max(
        [16] + [2 * last for layout in layouts for first, last in narrow_ranges(layout)]
    )


def work_scratch(layouts, row_counts, shard_count):
    return [
        pltpu.VMEM((dense_rows_of(layouts, row_counts, shard_count), LANES), jnp.float32),
        pltpu.VMEM((3, round_up(narrow_rows_of(layouts), 16), LANES), jnp.float32),
    ]


def local_rows(flat_shard):
    shard_rows = flat_shard.shape[0] // LANES
    return jnp.pad(
        flat_shard.reshape(shard_rows, LANES).astype(jnp.bfloat16),
        ((0, round_up(shard_rows, 16) - shard_rows), (0, 0)),
    )


def weight_shapes(layout):
    shapes = []
    for entry_shape in layout:
        is_matrix = len(entry_shape) == 2 and entry_shape[0] > 9
        kind = jnp.bfloat16 if is_matrix else jnp.float32
        shape = entry_shape if len(entry_shape) == 2 else (1,) + entry_shape
        shapes.append(shaped(shape, kind))
    return shapes


def unpack_joined(gathered, layouts, row_counts):
    shard_count = gathered.shape[0]

    def kernel(gathered_ref, *refs):
        dense_ref, narrow_ref = refs[-2:]
        first_row = 0
        first_out = 0
        for layout, shard_rows in zip(layouts, row_counts):
            padded_rows = round_up(shard_rows, 16)

            def spread(index, carry, shard_rows=shard_rows, first=first_row, rows=padded_rows):
                dense_ref[pl.ds(index * shard_rows, rows), :] = gathered_ref[
                    index, first : first + rows, :
                ].astype(jnp.float32)
                return carry

            out_refs = refs[first_out : first_out + len(layout)]
            unpack_group(
                layout, shard_rows, shard_count, spread, out_refs, dense_ref, narrow_ref
            )
            first_row += padded_rows
            first_out += len(layout)

    results = pl.pallas_call(
        kernel,
        out_shape=[shape for layout in layouts for shape in weight_shapes(layout)],
        scratch_shapes=work_scratch(layouts, row_counts, shard_count),
        compiler_params=PARAMS,
        name="unpack_joined",
    )(gathered)
    groups = []
    for layout in layouts:
        groups.append(results[: len(layout)])
        results = results[len(layout) :]
    return groups


def swap(values, axis, bit):
    return lax.ppermute(
        values, axis, [(place, place ^ bit) for place in range(lax.axis_size(axis))]
    )


def bit_orders(count):
    bits = [1 << place for place in range(count.bit_length() - 1)]
    return [bits, bits[1::-1] + bits[2:]]


def device_place():
    return jnp.stack([lax.axis_index("dp"), lax.axis_index("fsdp")]).astype(jnp.int32)


PLACE_SPEC = pl.BlockSpec(memory_space=pltpu.SMEM)


def gather_halves(rows, orders, beside):
    half = rows.shape[0] // 32 * 16
    gathered = []
    for number, (piece, order) in enumerate(zip((rows[:half], rows[half:]), orders)):
        held = piece[None]
        for bit in order:
            held = jnp.concatenate([held, swap(held, "fsdp", bit)], axis=0)
        if number == 0:
            held, beside = lax.optimization_barrier((held, beside))
        for bit in bit_orders(lax.axis_size("dp"))[0]:
            held = jnp.concatenate([held, swap(held, "dp", bit)], axis=0)
        gathered.append(held)
    return gathered, beside


def unpack_halves(halves, place, layout, shard_rows, orders):
    shard_count = halves[0].shape[0]
    chips = lax.axis_size("fsdp")
    half = halves[0].shape[1]

    def kernel(place_ref, *refs):
        half_refs = refs[:2]
        out_refs = refs[2:-2]
        dense_ref, narrow_ref = refs[-2:]

        def spread(index, carry):
            apart = (index % chips) ^ place_ref[1]
            cores = (index // chips) ^ place_ref[0]
            for number in range(2):
                position = cores * chips
                for step, bit in enumerate(orders[number]):
                    position = position + ((apart // bit) % 2) * (1 << step)
                rows = half_refs[number].shape[1]
                dense_ref[pl.ds(index * shard_rows + number * half, rows), :] = half_refs[number][
                    position
                ].astype(jnp.float32)
            return carry

        unpack_group(layout, shard_rows, shard_count, spread, out_refs, dense_ref, narrow_ref)

    vmem_spec = pl.BlockSpec(memory_space=pltpu.VMEM)
    return pl.pallas_call(
        kernel,
        in_specs=[PLACE_SPEC, vmem_spec, vmem_spec],
        out_shape=weight_shapes(layout),
        scratch_shapes=work_scratch([layout], [shard_rows], shard_count),
        compiler_params=PARAMS,
        name="unpack_halves",
    )(place, *halves)


def pack_group(layout, sources, in_refs, dense_ref, narrow_ref):
    places = layout_places(layout)
    used_rows = (places[-1][1] + math.prod(places[-1][0])) // LANES
    tail = dense_ref.shape[0] - used_rows
    dense_ref[pl.ds(used_rows, tail), :] = jnp.zeros((tail, LANES), jnp.float32)

    for (operand, first_row), (entry_shape, offset) in zip(sources, places):
        in_ref = in_refs[operand]
        rows = math.prod(entry_shape[:-1])
        cols = entry_shape[-1]
        narrow = is_narrow(entry_shape, offset)

        def copy_rows(start, amount):
            for part in range(-(-cols // LANES)):
                lanes = min(LANES, cols - part * LANES)
                piece = in_ref[pl.ds(first_row + start, amount), part * LANES : part * LANES + lanes]
                if narrow:
                    narrow_ref[part, pl.ds(offset // D3 + start, amount), 0:lanes] = piece
                else:
                    stride = cols // LANES
                    base = offset // LANES + part + start * stride
                    dense_ref[pl.ds(base, amount, stride=stride), :] = piece

        if rows < 32:
            copy_rows(0, rows)
        else:
            for_chunks(0, rows, 32, copy_rows)

    if narrow and (offset // D3 + rows) % 2 == 1:
        beyond = offset // D3 + rows
        narrow_ref[:, beyond : beyond + 1, :] = jnp.zeros((3, 1, LANES), jnp.float32)

    def narrow_step(start, amount):
        even_rows = pl.ds(2 * start, amount, stride=2)
        odd_rows = pl.ds(2 * start + 1, amount, stride=2)
        low_lanes = lax.broadcasted_iota(jnp.int32, (amount, LANES), 1) < LANES // 2
        even = [narrow_ref[part, even_rows, :] for part in range(3)]
        odd = [pltpu.roll(narrow_ref[part, odd_rows, :], LANES // 2, 1) for part in range(3)]
        joined = [
            even[0],
            even[1],
            jnp.where(low_lanes, even[2], odd[0]),
            jnp.where(low_lanes, odd[0], odd[1]),
            jnp.where(low_lanes, odd[1], odd[2]),
        ]
        for part in range(5):
            dense_ref[pl.ds(5 * start + part, amount, stride=5), :] = joined[part]

    for first, last in narrow_ranges(layout):
        for_chunks(first, last, PAIR_CHUNK, narrow_step)


def pack_grads(place, groups, parts):
    chips = lax.axis_size("fsdp")
    shard_count = lax.axis_size("dp") * chips
    layouts = [group[2] for group in groups]
    row_counts = [group[3] for group in groups]
    counts = [len(group[0]) for group in groups]

    def kernel(place_ref, *refs):
        out_refs = refs[sum(counts) : sum(counts) + len(parts)]
        dense_ref, narrow_ref = refs[-2:]
        first = 0
        for number, (operands, sources, layout, shard_rows) in enumerate(groups):
            in_refs = refs[first : first + len(operands)]
            first += len(operands)
            pack_group(layout, sources, in_refs, dense_ref, narrow_ref)

            def cut(index, carry, number=number, shard_rows=shard_rows):
                for out_ref, (pieces, core, turned) in zip(out_refs, parts):
                    out_row = 0
                    for group, first_row, rows in pieces:
                        if group == number:
                            chip = index ^ place_ref[1] if turned else index
                            shard = (place_ref[0] ^ core) * chips + chip
                            out_ref[index, out_row : out_row + rows, :] = dense_ref[
                                pl.ds(shard * shard_rows + first_row, rows), :
                            ].astype(out_ref.dtype)
                        out_row += rows
                return carry

            lax.fori_loop(0, chips, cut, 0)

    vmem_spec = pl.BlockSpec(memory_space=pltpu.VMEM)
    return pl.pallas_call(
        kernel,
        in_specs=[PLACE_SPEC] + [vmem_spec] * sum(counts),
        out_shape=[
            shaped((chips, sum(piece[2] for piece in pieces), LANES), WIRE_TYPE)
            for pieces, core, turned in parts
        ],
        scratch_shapes=work_scratch(layouts, row_counts, shard_count),
        compiler_params=PARAMS,
        name="pack_grads",
    )(place, *[operand for group in groups for operand in group[0]])


def add_rounded(kept, received):
    return (kept.astype(jnp.float32) + received.astype(jnp.float32)).astype(WIRE_TYPE)


def flat_rows(rows, shard_rows):
    return rows[:shard_rows].astype(jnp.float32).reshape(-1)


def sum_cores(parts):
    parts = list(parts)
    while len(parts) > 1:
        half = len(parts) // 2
        parts = [
            add_rounded(kept, swap(sent, "dp", half))
            for kept, sent in zip(parts[:half], parts[half:])
        ]
    return parts[0]


def scatter_half(parts, order):
    held = sum_cores(parts)
    left = sorted(order, reverse=True)
    held = held.reshape([2] * len(left) + list(held.shape[1:]))
    for bit in order:
        axis = left.index(bit)
        left.remove(bit)
        kept = lax.index_in_dim(held, 0, axis, keepdims=False)
        sent = lax.index_in_dim(held, 1, axis, keepdims=False)
        held = add_rounded(kept, swap(sent, "fsdp", bit))
    return held


def sum_devices(value):
    bits = [(axis, bit) for axis in AXES for bit in bit_orders(lax.axis_size(axis))[0]]
    while bits:
        first, *bits = bits
        near = swap(value, *first)
        if bits and bits[0][0] == first[0]:
            second, *bits = bits
            far = swap(value, *second)
            both = swap(value, first[0], first[1] | second[1])
            value = (value + near) + (far + both)
        else:
            value = value + near
    return value


def dot(left, right):
    return lax.dot_general(
        left, right, (((1,), (0,)), ((), ())), preferred_element_type=jnp.float32
    )


def dot_nt(left, right):
    return lax.dot_general(
        left, right, (((1,), (1,)), ((), ())), preferred_element_type=jnp.float32
    )


def dot_tn(left, right):
    return lax.dot_general(
        left, right, (((0,), (0,)), ((), ())), preferred_element_type=jnp.float32
    )


def rows_sum(values):
    return jnp.sum(values, axis=0, keepdims=True)


def norm_parts(values):
    centred = values - jnp.mean(values, axis=-1, keepdims=True)
    spread = jnp.mean(centred * centred, axis=-1, keepdims=True)
    scale = lax.rsqrt(spread + 1e-06)
    return centred * scale, scale


def norm_grad(unit, scale, gain_row, gradient):
    inner = gradient * gain_row
    first = jnp.mean(inner, axis=-1, keepdims=True)
    second = jnp.mean(inner * unit, axis=-1, keepdims=True)
    return scale * (inner - first - unit * second)


def column_mask(rows, lanes, side, width):
    places = lax.broadcasted_iota(jnp.int32, (rows, lanes), 0)
    return (places & (width - 1)) < side


def softmax_rows(query, key, valid):
    scores = jnp.where(valid, dot_nt(query, key) * 0.125, -1e30)
    powers = jnp.exp(scores - jnp.max(scores, axis=-1, keepdims=True))
    return powers * (1.0 / jnp.sum(powers, axis=-1, keepdims=True))


def split_lanes(values):
    rows, channels = values.shape
    pieces = []
    for first in range(0, channels, LANES):
        piece = values[:, first : min(first + LANES, channels)]
        if piece.shape[1] < LANES:
            rest = jnp.zeros((rows, LANES - piece.shape[1]), values.dtype)
            piece = jnp.concatenate([piece, rest], axis=1)
        pieces.append(piece)
    return pieces


def join_lanes(pieces, channels):
    return jnp.concatenate(pieces, axis=1)[:, :channels]


def pair_place(width, part):
    return pl.ds((part // 2) * width + part % 2, width // 2, stride=2)


def pair_part(grid_ref, width, part, channels):
    pieces = []
    for index in range(grid_ref.shape[0]):
        piece = grid_ref[index, :, pair_place(width, part), :]
        pieces.append(piece.reshape(piece.shape[0] * piece.shape[1], LANES))
    return join_lanes(pieces, channels).astype(jnp.bfloat16)


def attend_kernel(channels, side, width, has_reduction, *refs):
    if has_reduction:
        (
            x_ref, valid_ref, gain_ref, bias_ref, wq_ref, bq_ref, wr_ref, br_ref, rgain_ref,
            rbias_ref, wp_ref, bv_ref, wo_ref, bo_ref, gain2_ref, bias2_ref,
            query_ref, pair_ref, mixed_ref, middle_ref, normed_ref, reduced_ref, padded_ref,
            grid_ref, inputs_ref,
        ) = refs
    else:
        (
            x_ref, valid_ref, gain_ref, bias_ref, wq_ref, bq_ref,
            wp_ref, bv_ref, wo_ref, bo_ref, gain2_ref, bias2_ref,
            query_ref, pair_ref, mixed_ref, middle_ref, normed_ref,
        ) = refs
    inputs = x_ref[0].astype(jnp.float32)
    if has_reduction:
        for row in range(side):
            first = row * width
            inputs_ref[first : first + side, :] = inputs[row * side : (row + 1) * side]
            inputs_ref[first + side : first + width, :] = jnp.zeros(
                (width - side, channels), jnp.float32
            )
        inputs = inputs_ref[...]
        padded_ref[0] = inputs.astype(jnp.bfloat16)
    unit, _ = norm_parts(inputs)
    normed = (unit * gain_ref[...] + bias_ref[...]).astype(jnp.bfloat16)
    query_ref[0] = (dot(normed, wq_ref[...]) + bq_ref[...]).astype(jnp.bfloat16)
    if has_reduction:
        for index, piece in enumerate(split_lanes(normed.astype(jnp.float32))):
            grid_ref[index] = piece.reshape(grid_ref.shape[1:])
        reduced = br_ref[...]
        for part in range(4):
            reduced = reduced + dot(
                pair_part(grid_ref, width, part, channels),
                wr_ref[part * channels : (part + 1) * channels, :],
            )
        reduced_ref[0] = reduced
        unit, _ = norm_parts(reduced)
        source = (unit * rgain_ref[...] + rbias_ref[...]).astype(jnp.bfloat16)
    else:
        source = normed
    pair_ref[0, :, :channels] = dot(source, wp_ref[:, :channels]).astype(jnp.bfloat16)
    pair_ref[0, :, channels:] = (dot(source, wp_ref[:, channels:]) + bv_ref[...]).astype(
        jnp.bfloat16
    )
    valid = valid_ref[0] > 0.5
    for head in range(channels // HEAD):
        lanes = slice(head * HEAD, (head + 1) * HEAD)
        value_lanes = slice(channels + head * HEAD, channels + (head + 1) * HEAD)
        chances = softmax_rows(query_ref[0, :, lanes], pair_ref[0, :, lanes], valid)
        mixed_ref[0, :, lanes] = dot(
            chances.astype(jnp.bfloat16), pair_ref[0, :, value_lanes]
        ).astype(jnp.bfloat16)
    middle = inputs + (dot(mixed_ref[0], wo_ref[...]) + bo_ref[...])
    middle_ref[0] = middle
    unit, _ = norm_parts(middle)
    normed_ref[0] = (unit * gain2_ref[...] + bias2_ref[...]).astype(jnp.bfloat16)


def whole(shape):
    return pl.BlockSpec(shape, lambda *place: (0,) * len(shape))


def image_block(array):
    return pl.BlockSpec((1,) + array.shape[1:], lambda image: (image,) + (0,) * (len(array.shape) - 1))


def shaped(shape, kind):
    return jax.ShapeDtypeStruct(shape, kind)


PARAMS = pltpu.CompilerParams(vmem_limit_bytes=61000 * 1024)


def attend_block(inputs, valid, weights, side, width):
    images, _, channels = inputs.shape
    tokens = side * width
    has_reduction = len(weights) == 14
    keys = valid.shape[2]
    outs = [
        shaped((images, tokens, channels), jnp.bfloat16),
        shaped((images, keys, 2 * channels), jnp.bfloat16),
        shaped((images, tokens, channels), jnp.bfloat16),
        shaped((images, tokens, channels), jnp.float32),
        shaped((images, tokens, channels), jnp.bfloat16),
    ]
    scratch = []
    if has_reduction:
        outs.append(shaped((images, keys, channels), jnp.float32))
        outs.append(shaped((images, tokens, channels), jnp.bfloat16))
        grid_shape = (-(-channels // LANES), tokens // (2 * width), 2 * width, LANES)
        scratch.append(pltpu.VMEM(grid_shape, jnp.float32))
        scratch.append(pltpu.VMEM((tokens, channels), jnp.float32))
    return pl.pallas_call(
        lambda *refs: attend_kernel(channels, side, width, has_reduction, *refs),
        grid=(images,),
        in_specs=[image_block(inputs), image_block(valid)] + [whole(w.shape) for w in weights],
        out_specs=[image_block(out) for out in outs],
        out_shape=outs,
        scratch_shapes=scratch,
        compiler_params=PARAMS,
        name="attend",
    )(inputs, valid, *weights)


def zero_edges(ref, side, width, columns):
    tokens = side * width
    lanes = ref.shape[1]
    ref[0:width, :] = jnp.zeros((width, lanes), jnp.float32)
    ref[width + tokens : 2 * width + tokens, :] = jnp.zeros((width, lanes), jnp.float32)
    if columns:
        for row in range(1, side + 1):
            ref[row * width + side : (row + 1) * width, :] = jnp.zeros(
                (width - side, lanes), jnp.float32
            )


def store_cells(ref, values, side, width):
    for row in range(side):
        ref[0, row * side : (row + 1) * side, :] = values[row * width : row * width + side]


def mix_kernel(side, width, lanes, dense, *refs):
    (
        normed_ref, middle_ref, we_ref, be_ref, kd_ref, bd_ref, wc_ref, bc_ref,
        out_ref, mixed_ref, slope_ref, pad_ref,
    ) = refs
    tokens = side * width
    units = we_ref.shape[1]
    pad_ref[width : width + tokens, :] = dot(normed_ref[0], we_ref[...]) + be_ref[...]
    zero_edges(pad_ref, side, width, True)

    def step(row, carry):
        start = pl.multiple_of(row * width, width)
        for first in range(0, units, lanes):
            block = slice(first, first + lanes)
            rows = [pad_ref[pl.ds(start + up * width, width), block] for up in range(3)]
            sums = [
                kd_ref[col : col + 1, block] * rows[0]
                + kd_ref[3 + col : 4 + col, block] * rows[1]
                + kd_ref[6 + col : 7 + col, block] * rows[2]
                for col in range(3)
            ]
            value = (
                sums[1]
                + pltpu.roll(sums[0], 1, 0)
                + pltpu.roll(sums[2], width - 1, 0)
                + bd_ref[:, block]
            )
            share = 0.5 + 0.5 * lax.erf(value * math.sqrt(0.5))
            bell = jnp.exp(value * value * -0.5) * (1.0 / math.sqrt(2.0 * math.pi))
            mixed_ref[0, pl.ds(start, width), block] = (value * share).astype(jnp.bfloat16)
            slope_ref[0, pl.ds(start, width), block] = (share + value * bell).astype(jnp.bfloat16)
        return carry

    lax.fori_loop(0, side, step, 0)
    result = middle_ref[0] + bc_ref[...] + dot(mixed_ref[0], wc_ref[...])
    if dense:
        store_cells(out_ref, result, side, width)
    else:
        out_ref[0] = result


def mix_block(normed, middle, weights, side, width, lanes, dense):
    images, tokens, channels = middle.shape
    units = weights[0].shape[1]
    outs = [
        shaped((images, side * side if dense else tokens, channels), jnp.float32),
        shaped((images, tokens, units), jnp.bfloat16),
        shaped((images, tokens, units), jnp.bfloat16),
    ]
    return pl.pallas_call(
        lambda *refs: mix_kernel(side, width, lanes, dense, *refs),
        grid=(images,),
        in_specs=[image_block(normed), image_block(middle)] + [whole(w.shape) for w in weights],
        out_specs=[image_block(out) for out in outs],
        out_shape=outs,
        scratch_shapes=[pltpu.VMEM((tokens + 2 * width, units), jnp.float32)],
        compiler_params=PARAMS,
        name="mix",
    )(normed, middle, *weights)


def mix_back_kernel(side, width, lanes, *refs):
    (
        normed_ref, grad_ref, mixed_ref, slope_ref, we_ref, be_ref, kd_ref, wc_ref,
        dnormed_ref, dwe_ref, dwc_ref, drows_ref, pad_ref, dpad_ref, dhid_ref,
    ) = refs
    tokens = side * width
    units = we_ref.shape[1]
    gradient = grad_ref[0].astype(jnp.bfloat16)
    pad_ref[width : width + tokens, :] = dot(normed_ref[0], we_ref[...]) + be_ref[...]
    dpad_ref[width : width + tokens, :] = dot_nt(gradient, wc_ref[...]) * slope_ref[0].astype(
        jnp.float32
    )
    zero_edges(pad_ref, side, width, True)
    zero_edges(dpad_ref, side, width, False)

    @pl.when(pl.program_id(0) == 0)
    def _():
        for ref in (drows_ref, dwe_ref, dwc_ref):
            ref[...] = jnp.zeros(ref.shape, jnp.float32)

    inside = column_mask(width, lanes, side, width)

    def fold(values):
        total = values[0:8]
        for start in range(8, width, 8):
            total = total + values[start : start + 8]
        return total

    for first in range(0, units, lanes):
        block = slice(first, first + lanes)

        def step(row, sums, block=block):
            start = pl.multiple_of(row * width, width)
            rows = [pad_ref[pl.ds(start + up * width, width), block] for up in range(3)]
            drows = [dpad_ref[pl.ds(start + up * width, width), block] for up in range(3)]
            turned = [
                pltpu.roll(drows[1], width - 1, 0),
                drows[1],
                pltpu.roll(drows[1], 1, 0),
            ]
            found = []
            for up in range(3):
                for col in range(3):
                    found.append(sums[3 * up + col] + fold(turned[col] * rows[up]))
            found.append(sums[9] + fold(drows[1]))
            parts = [
                kd_ref[col : col + 1, block] * drows[2]
                + kd_ref[3 + col : 4 + col, block] * drows[1]
                + kd_ref[6 + col : 7 + col, block] * drows[0]
                for col in range(3)
            ]
            value = parts[1] + pltpu.roll(parts[0], width - 1, 0) + pltpu.roll(parts[2], 1, 0)
            value = jnp.where(inside, value, 0.0)
            dhid_ref[pl.ds(start, width), block] = value.astype(jnp.bfloat16)
            found.append(sums[10] + fold(value))
            return tuple(found)

        zero = jnp.zeros((8, lanes), jnp.float32)
        totals = lax.fori_loop(0, side, step, (zero,) * 11, unroll=2)
        for index in range(11):
            drows_ref[index : index + 1, block] += rows_sum(totals[index])
    dhidden = dhid_ref[...]
    dwe_ref[...] += dot_tn(normed_ref[0], dhidden)
    dwc_ref[...] += dot_tn(mixed_ref[0], gradient)
    dnormed_ref[0] = dot_nt(dhidden, we_ref[...])


def mix_back(normed, gradient, mixed, slope, weights, side, width, lanes):
    we, be, kd, bd, wc, bc = weights
    images, tokens, channels = normed.shape
    units = we.shape[1]
    operands = [normed, gradient, mixed, slope]
    used = [we, be, kd, wc]
    outs = [
        shaped((images, tokens, channels), jnp.float32),
        shaped((channels, units), jnp.float32),
        shaped((units, channels), jnp.float32),
        shaped((16, units), jnp.float32),
    ]
    return pl.pallas_call(
        lambda *refs: mix_back_kernel(side, width, lanes, *refs),
        grid=(images,),
        in_specs=[image_block(op) for op in operands] + [whole(u.shape) for u in used],
        out_specs=[image_block(outs[0])] + [whole(out.shape) for out in outs[1:]],
        out_shape=outs,
        scratch_shapes=[
            pltpu.VMEM((tokens + 2 * width, units), jnp.float32),
            pltpu.VMEM((tokens + 2 * width, units), jnp.float32),
            pltpu.VMEM((tokens, units), jnp.bfloat16),
        ],
        compiler_params=PARAMS,
        name="mix_back",
    )(*operands, *used)


def attend_back_kernel(channels, side, width, has_reduction, *refs):
    if has_reduction:
        (
            x_ref, valid_ref, grad_ref, dnormed_ref, middle_ref, query_ref, pair_ref, mixed_ref,
            reduced_ref, gain_ref, bias_ref, wq_ref, wr_ref, rgain_ref, rbias_ref, wp_ref, wo_ref,
            gain2_ref,
            dx_ref, dwq_ref, dwp_ref, dwo_ref, vec_ref, dwr_ref,
            dquery_ref, dpair_ref, dmiddle_ref, grid_ref, dgrid_ref,
        ) = refs
    else:
        (
            x_ref, valid_ref, grad_ref, dnormed_ref, middle_ref, query_ref, pair_ref, mixed_ref,
            gain_ref, bias_ref, wq_ref, wp_ref, wo_ref, gain2_ref,
            dx_ref, dwq_ref, dwp_ref, dwo_ref, vec_ref,
            dquery_ref, dpair_ref, dmiddle_ref,
        ) = refs

    @pl.when(pl.program_id(0) == 0)
    def _():
        sums = [dwq_ref, dwp_ref, dwo_ref, vec_ref] + ([dwr_ref] if has_reduction else [])
        for ref in sums:
            ref[...] = jnp.zeros(ref.shape, jnp.float32)

    def add_row(index, row):
        vec_ref[index : index + 1, :] += row

    gradient = grad_ref[0].astype(jnp.float32)
    add_row(0, rows_sum(gradient.astype(jnp.bfloat16).astype(jnp.float32)))
    dnormed = dnormed_ref[0]
    unit, scale = norm_parts(middle_ref[0])
    add_row(1, rows_sum(dnormed * unit))
    add_row(2, rows_sum(dnormed))
    dmiddle = gradient + norm_grad(unit, scale, gain2_ref[...], dnormed)
    dmiddle_ref[...] = dmiddle
    doutput = dmiddle.astype(jnp.bfloat16)
    add_row(3, rows_sum(doutput.astype(jnp.float32)))
    dwo_ref[...] += dot_tn(mixed_ref[0], doutput)
    dmixed = dot_nt(doutput, wo_ref[...]).astype(jnp.bfloat16)
    valid = valid_ref[0] > 0.5
    for head in range(channels // HEAD):
        lanes = slice(head * HEAD, (head + 1) * HEAD)
        value_lanes = slice(channels + head * HEAD, channels + (head + 1) * HEAD)
        query = query_ref[0, :, lanes]
        key = pair_ref[0, :, lanes]
        chances = softmax_rows(query, key, valid)
        dhead = dmixed[:, lanes]
        dchances = dot_nt(dhead, pair_ref[0, :, value_lanes])
        dpair_ref[:, value_lanes] = dot_tn(chances.astype(jnp.bfloat16), dhead).astype(
            jnp.bfloat16
        )
        weighted = chances * dchances
        dscores = (
            weighted - chances * jnp.sum(weighted, axis=-1, keepdims=True)
        ).astype(jnp.bfloat16)
        dquery_ref[:, lanes] = (dot(dscores, key) * 0.125).astype(jnp.bfloat16)
        dpair_ref[:, lanes] = (dot_tn(dscores, query) * 0.125).astype(jnp.bfloat16)
    dquery = dquery_ref[...]
    dpair = dpair_ref[...]
    unit, scale = norm_parts(x_ref[0].astype(jnp.float32))
    normed = (unit * gain_ref[...] + bias_ref[...]).astype(jnp.bfloat16)
    add_row(4, rows_sum(dquery.astype(jnp.float32)))
    add_row(5, rows_sum(dpair[:, channels:].astype(jnp.float32)))
    dwq_ref[...] += dot_tn(normed, dquery)
    total = dot_nt(dquery, wq_ref[...])
    dsource = dot_nt(dpair, wp_ref[...])
    if has_reduction:
        runit, rscale = norm_parts(reduced_ref[0])
        source = (runit * rgain_ref[...] + rbias_ref[...]).astype(jnp.bfloat16)
        dwp_ref[...] += dot_tn(source, dpair)
        add_row(8, rows_sum(dsource * runit))
        add_row(9, rows_sum(dsource))
        dreduced = norm_grad(runit, rscale, rgain_ref[...], dsource).astype(jnp.bfloat16)
        add_row(10, rows_sum(dreduced.astype(jnp.float32)))
        for index, piece in enumerate(split_lanes(normed.astype(jnp.float32))):
            grid_ref[index] = piece.reshape(grid_ref.shape[1:])
        for index, piece in enumerate(split_lanes(total)):
            dgrid_ref[index] = piece.reshape(dgrid_ref.shape[1:])
        for part in range(4):
            rows = slice(part * channels, (part + 1) * channels)
            dwr_ref[rows, :] += dot_tn(pair_part(grid_ref, width, part, channels), dreduced)
            for index, piece in enumerate(split_lanes(dot_nt(dreduced, wr_ref[rows, :]))):
                dgrid_ref[index, :, pair_place(width, part), :] += piece.reshape(
                    dgrid_ref.shape[1], width // 2, LANES
                )
        total = join_lanes(
            [dgrid_ref[index].reshape(total.shape[0], LANES) for index in range(dgrid_ref.shape[0])],
            channels,
        )
    else:
        dwp_ref[...] += dot_tn(normed, dpair)
        total = total + dsource
    add_row(6, rows_sum(total * unit))
    add_row(7, rows_sum(total))
    result = dmiddle_ref[...] + norm_grad(unit, scale, gain_ref[...], total)
    if has_reduction:
        store_cells(dx_ref, result, side, width)
    else:
        dx_ref[0] = result


def attend_back(inputs, valid, gradient, dnormed, saved, weights, side, width):
    query, pair, mixed, middle, normed = saved[:5]
    images, tokens, channels = middle.shape
    has_reduction = len(saved) > 5
    keys = valid.shape[2]
    operands = [inputs, valid, gradient, dnormed, middle, query, pair, mixed]
    outs = [
        shaped((images, side * side if has_reduction else tokens, channels), jnp.float32),
        shaped((channels, channels), jnp.float32),
        shaped((channels, 2 * channels), jnp.float32),
        shaped((channels, channels), jnp.float32),
        shaped((16, channels), jnp.float32),
    ]
    scratch = [
        pltpu.VMEM((tokens, channels), jnp.bfloat16),
        pltpu.VMEM((keys, 2 * channels), jnp.bfloat16),
        pltpu.VMEM((tokens, channels), jnp.float32),
    ]
    if has_reduction:
        gain, bias, wq, bq, wr, br, rgain, rbias, wp, bv, wo, bo, gain2, bias2 = weights
        used = [gain, bias, wq, wr, rgain, rbias, wp, wo, gain2]
        operands.append(saved[5])
        outs.append(shaped((4 * channels, channels), jnp.float32))
        grid_shape = (-(-channels // LANES), tokens // (2 * width), 2 * width, LANES)
        scratch += [pltpu.VMEM(grid_shape, jnp.float32), pltpu.VMEM(grid_shape, jnp.float32)]
    else:
        gain, bias, wq, bq, wp, bv, wo, bo, gain2, bias2 = weights
        used = [gain, bias, wq, wp, wo, gain2]
    return pl.pallas_call(
        lambda *refs: attend_back_kernel(channels, side, width, has_reduction, *refs),
        grid=(images,),
        in_specs=[image_block(op) for op in operands] + [whole(w.shape) for w in used],
        out_specs=[image_block(outs[0])] + [whole(out.shape) for out in outs[1:]],
        out_shape=outs,
        scratch_shapes=scratch,
        compiler_params=PARAMS,
        name="attend_back",
    )(*operands, *used)


def tap_place(width, tap, row):
    first = LEAD + (tap // 3) * width + tap % 3 - 1
    return pl.ds(first + 2 * width * row, width // 2, stride=2)


def load_tap(grid_ref, side, width, tap, channels):
    pieces = []
    for index in range(grid_ref.shape[0]):
        rows = [grid_ref[index, tap_place(width, tap, row), :] for row in range(side // 2)]
        pieces.append(jnp.concatenate(rows, axis=0))
    return join_lanes(pieces, channels).astype(jnp.bfloat16)


def fill_grid(grid_ref, values, width):
    rows = grid_ref.shape[1]
    first = LEAD + width
    last = first + values.shape[0]
    for index, piece in enumerate(split_lanes(values)):
        grid_ref[index, 0:first, :] = jnp.zeros((first, LANES), jnp.float32)
        grid_ref[index, first:last, :] = piece
        grid_ref[index, last:rows, :] = jnp.zeros((rows - last, LANES), jnp.float32)


LEAD = 8


def embed_kernel(side, width, *refs):
    x_ref, gain_ref, bias_ref, w_ref, b_ref, pgain_ref, pbias_ref = refs[:7]
    out_ref, patch_ref, grid_ref = refs[7:]
    tokens, channels = x_ref.shape[1:]
    unit, _ = norm_parts(x_ref[0])
    normed = (unit * gain_ref[...] + bias_ref[...]).astype(jnp.bfloat16).astype(jnp.float32)
    inside = column_mask(tokens, channels, side, width)
    fill_grid(grid_ref, jnp.where(inside, normed, 0.0), width)
    patch = b_ref[...]
    for tap in range(9):
        patch = patch + dot(
            load_tap(grid_ref, side, width, tap, channels),
            w_ref[tap * channels : (tap + 1) * channels, :]
        )
    patch_ref[0] = patch
    unit, _ = norm_parts(patch)
    out_ref[0] = unit * pgain_ref[...] + pbias_ref[...]


def embed_block(inputs, weights, side, width):
    images, tokens, channels = inputs.shape
    units = weights[2].shape[1]
    outs = [shaped((images, tokens // 4, units), jnp.float32)] * 2
    return pl.pallas_call(
        lambda *refs: embed_kernel(side, width, *refs),
        grid=(images,),
        in_specs=[image_block(inputs)] + [whole(w.shape) for w in weights],
        out_specs=[image_block(out) for out in outs],
        out_shape=outs,
        scratch_shapes=[pltpu.VMEM((-(-channels // LANES), LEAD + (side + 3) * width, LANES), jnp.float32)],
        compiler_params=PARAMS,
        name="embed",
    )(inputs, *weights)


def embed_back_kernel(side, width, *refs):
    x_ref, grad_ref, patch_ref, gain_ref, bias_ref, w_ref, pgain_ref = refs[:7]
    dx_ref, dw_ref, vec_ref, pvec_ref, grid_ref, dgrid_ref = refs[7:]
    tokens, channels = x_ref.shape[1:]

    @pl.when(pl.program_id(0) == 0)
    def _():
        for ref in (dw_ref, vec_ref, pvec_ref):
            ref[...] = jnp.zeros(ref.shape, jnp.float32)

    gradient = grad_ref[0]
    punit, pscale = norm_parts(patch_ref[0])
    pvec_ref[0:1, :] += rows_sum(gradient * punit)
    pvec_ref[1:2, :] += rows_sum(gradient)
    dpatch = norm_grad(punit, pscale, pgain_ref[...], gradient).astype(jnp.bfloat16)
    pvec_ref[2:3, :] += rows_sum(dpatch.astype(jnp.float32))
    unit, scale = norm_parts(x_ref[0])
    normed = (unit * gain_ref[...] + bias_ref[...]).astype(jnp.bfloat16).astype(jnp.float32)
    inside = column_mask(tokens, channels, side, width)
    fill_grid(grid_ref, jnp.where(inside, normed, 0.0), width)
    dgrid_ref[...] = jnp.zeros(dgrid_ref.shape, jnp.float32)
    half = width // 2
    for tap in range(9):
        rows = slice(tap * channels, (tap + 1) * channels)
        dw_ref[rows, :] += dot_tn(load_tap(grid_ref, side, width, tap, channels), dpatch)
        for index, piece in enumerate(split_lanes(dot_nt(dpatch, w_ref[rows, :]))):
            for row in range(side // 2):
                dgrid_ref[index, tap_place(width, tap, row), :] += piece[
                    row * half : (row + 1) * half, :
                ]
    first = LEAD + width
    pieces = [dgrid_ref[index, first : first + tokens, :] for index in range(dgrid_ref.shape[0])]
    total = jnp.where(inside, join_lanes(pieces, channels), 0.0)
    vec_ref[0:1, :] += rows_sum(total * unit)
    vec_ref[1:2, :] += rows_sum(total)
    dx_ref[0] = norm_grad(unit, scale, gain_ref[...], total)


def embed_back(inputs, gradient, patch, weights, side, width):
    gain, bias, w, b, pgain, pbias = weights
    images, tokens, channels = inputs.shape
    units = w.shape[1]
    outs = [
        shaped(inputs.shape, jnp.float32),
        shaped(w.shape, jnp.float32),
        shaped((8, channels), jnp.float32),
        shaped((8, units), jnp.float32),
    ]
    operands = [inputs, gradient, patch]
    used = [gain, bias, w, pgain]
    grid_scratch = pltpu.VMEM((-(-channels // LANES), LEAD + (side + 3) * width, LANES), jnp.float32)
    return pl.pallas_call(
        lambda *refs: embed_back_kernel(side, width, *refs),
        grid=(images,),
        in_specs=[image_block(op) for op in operands] + [whole(u.shape) for u in used],
        out_specs=[image_block(outs[0])] + [whole(out.shape) for out in outs[1:]],
        out_shape=outs,
        scratch_shapes=[grid_scratch, grid_scratch],
        compiler_params=PARAMS,
        name="embed_back",
    )(*operands, *used)


def to_grid(values, side, width):
    images, tokens, channels = values.shape
    grid = values.reshape(images, side, side, channels)
    grid = jnp.pad(grid, ((0, 0), (0, 0), (0, width - side), (0, 0)))
    return grid.reshape(images, side * width, channels)


def key_mask(row_counts, col_counts, side, width):
    places = jnp.arange(side * width, dtype=jnp.int32)
    valid = ((places // width)[None, :] < row_counts[:, None]) & (
        (places % width)[None, :] < col_counts[:, None]
    )
    return valid.astype(jnp.float32)[:, None, :]


def block_sources(has_reduction):
    reduction = [(7, 0), (3, 10), (3, 8), (3, 9)] if has_reduction else []
    return (
        [(3, 6), (3, 7), (0, 0), (3, 4)]
        + reduction
        + [(1, 0), (3, 5), (2, 0), (3, 3), (3, 1), (3, 2)]
        + [(4, 0), (6, 10), (6, 0), (6, 9), (5, 0), (3, 0)]
    )


EMBED_SOURCES = [(1, 0), (1, 1), (0, 0), (2, 2), (2, 0), (2, 1)]


def adamw_update(weights, mean_old, square_old, gradient, clip_factor, rate_value, fix_one):
    clipped = gradient * clip_factor
    mean_new = 0.5 * mean_old + 0.5 * clipped
    square_new = 0.5 * square_old + 0.5 * clipped * clipped
    updated = weights * (1.0 - rate_value * 0.05) - rate_value * (mean_new / fix_one) / (
        jnp.sqrt(square_new / fix_one) + 1e-08
    )
    return (updated, mean_new, square_new)


def shards(
    features,
    key_rows,
    key_cols,
    out_grad,
    lower_weights,
    lower_mean,
    lower_square,
    embed_weights,
    embed_mean,
    embed_square,
    upper_weights,
    upper_mean,
    upper_square,
    learn_rate,
):
    side, half = GRID, GRID // 2
    width = round_up(side, 32)
    half_width = width // 2
    key_valid = key_mask(key_rows, key_cols, half, half_width)
    cores = lax.axis_size("dp")
    orders = bit_orders(lax.axis_size("fsdp"))
    place = device_place()
    lower_rows, embed_rows, upper_rows = (
        flat.shape[0] // LANES for flat in (lower_weights, embed_weights, upper_weights)
    )
    lower_halves, grad_in = gather_halves(
        local_rows(lower_weights), [order[2:] + order[:2] for order in orders], to_grid(out_grad, half, half_width)
    )
    rest_local = jnp.concatenate([local_rows(embed_weights), local_rows(upper_weights)], axis=0)
    *lower_halves, rest_local = lax.optimization_barrier((*lower_halves, rest_local))
    rest = lax.all_gather(rest_local, AXES, axis=0, tiled=False)
    lower = unpack_halves(
        lower_halves, place, LOWER_LAYOUT, lower_rows, [order[2:] + order[:2] for order in orders]
    )
    embed, upper = unpack_joined(rest, [EMBED_LAYOUT, UPPER_LAYOUT], [embed_rows, upper_rows])

    lower_saved = attend_block(features, key_valid, lower[:14], side, width)
    three_in = lower_saved[6]
    section_three, lower_mixed, lower_slope = mix_block(
        lower_saved[4], lower_saved[3], lower[14:], side, width, 256, False
    )
    section_four, patch = embed_block(section_three, embed, side, width)
    upper_saved = attend_block(section_four, key_valid, upper[:10], half, half_width)
    block_out, upper_mixed, upper_slope = mix_block(
        upper_saved[4], upper_saved[3], upper[10:], half, half_width, 256, True
    )

    def back(inputs, gradient, saved, mixed, slope, weights, first, side, width, lanes):
        dnormed, dwe, dwc, drows = mix_back(
            saved[4], gradient, mixed, slope, weights[first:], side, width, lanes
        )
        dx, dwq, dwp, dwo, vec, *rest = attend_back(
            inputs, key_valid, gradient, dnormed, saved, weights[:first], side, width
        )
        return dx, [dwq, dwp, dwo, vec, dwe, dwc, drows] + rest

    four_grad, upper_found = back(
        section_four, grad_in, upper_saved, upper_mixed, upper_slope, upper, 10, half, half_width, 256
    )
    upper_wire = pack_grads(
        place,
        [(upper_found, block_sources(False), UPPER_LAYOUT, upper_rows)],
        [([(0, 0, round_up(upper_rows, 16))], core, False) for core in range(cores)],
    )
    *upper_wire, four_grad = lax.optimization_barrier((*upper_wire, four_grad))
    three_grad, *embed_found = embed_back(section_three, four_grad, patch, embed, side, width)
    embed_wire = pack_grads(
        place,
        [(embed_found, EMBED_SOURCES, EMBED_LAYOUT, embed_rows)],
        [([(0, 0, round_up(embed_rows, 16))], core, False) for core in range(cores)],
    )
    rest_sum = jnp.concatenate([sum_cores(embed_wire), sum_cores(upper_wire)], axis=1)
    rest_sum, three_grad = lax.optimization_barrier((rest_sum, three_grad))
    rest_grad = lax.psum_scatter(rest_sum, "fsdp", scatter_dimension=0, tiled=False)
    input_grad, lower_found = back(
        three_in, three_grad, lower_saved, lower_mixed, lower_slope, lower, 14, side, width, 256
    )
    padded_rows = round_up(lower_rows, 16)
    half_rows = padded_rows // 32 * 16
    parts = []
    for first, rows in ((0, half_rows), (half_rows, padded_rows - half_rows)):
        parts += [([(0, first, rows)], core, True) for core in range(cores)]
    wire = pack_grads(
        place, [(lower_found, block_sources(True), LOWER_LAYOUT, lower_rows)], parts
    )
    lower_sum = jnp.concatenate(
        [scatter_half(wire[:cores], orders[0]), scatter_half(wire[cores:], orders[1])], axis=0
    )
    lower_grad = flat_rows(lower_sum, lower_rows)
    embed_grad = flat_rows(rest_grad, embed_rows)
    upper_grad = flat_rows(rest_grad[round_up(embed_rows, 16) :], upper_rows)
    local_squares = (
        jnp.sum(lower_grad * lower_grad)
        + jnp.sum(embed_grad * embed_grad)
        + jnp.sum(upper_grad * upper_grad)
    )
    squares = sum_devices(local_squares.reshape(1, 1))[0, 0]
    grad_norm = jnp.sqrt(squares)
    clip_factor = jnp.minimum(1.0, 5.0 / (grad_norm + 1e-06))
    rate_value = learn_rate[0]
    fix_one = 1.0 - 0.5**ADAM_STEP
    lower_new, lower_mean_new, lower_square_new = adamw_update(
        lower_weights, lower_mean, lower_square, lower_grad, clip_factor, rate_value, fix_one
    )
    embed_new, embed_mean_new, embed_square_new = adamw_update(
        embed_weights, embed_mean, embed_square, embed_grad, clip_factor, rate_value, fix_one
    )
    upper_new, upper_mean_new, upper_square_new = adamw_update(
        upper_weights, upper_mean, upper_square, upper_grad, clip_factor, rate_value, fix_one
    )
    return (
        block_out,
        input_grad,
        grad_norm.reshape(1),
        lower_grad,
        lower_new,
        lower_mean_new,
        lower_square_new,
        lower_new.astype(jnp.bfloat16),
        embed_grad,
        embed_new,
        embed_mean_new,
        embed_square_new,
        embed_new.astype(jnp.bfloat16),
        upper_grad,
        upper_new,
        upper_mean_new,
        upper_square_new,
        upper_new.astype(jnp.bfloat16),
    )


AXES = ("dp", "fsdp")
TOKENS = P(AXES, None, None)
FLAT = P(AXES)


def solution(mesh):
    return jax.shard_map(
        shards,
        mesh=mesh,
        in_specs=(
            TOKENS,
            FLAT,
            FLAT,
            TOKENS,
            FLAT,
            FLAT,
            FLAT,
            FLAT,
            FLAT,
            FLAT,
            FLAT,
            FLAT,
            FLAT,
            P(),
        ),
        out_specs=(
            TOKENS,
            TOKENS,
            P(),
            FLAT,
            FLAT,
            FLAT,
            FLAT,
            FLAT,
            FLAT,
            FLAT,
            FLAT,
            FLAT,
            FLAT,
            FLAT,
            FLAT,
            FLAT,
            FLAT,
            FLAT,
        ),
        check_vma=False,
    )
```

```python
import math

import jax
import jax.numpy as jnp
from jax import lax
from jax.experimental import pallas as pl
from jax.experimental.pallas import tpu as pltpu
from jax.sharding import PartitionSpec as P

D3 = 320
D4 = 512
HID3 = 1280
HID4 = 2048
HEAD = 64
GRID = 28
ADAM_STEP = 2
WIRE_TYPE = jnp.bfloat16


def block_layout(channels, units, has_reduction):
    row = (channels,)
    reduction = [(4 * channels, channels), row, row, row] if has_reduction else []
    return (
        [row, row, (channels, channels), row]
        + reduction
        + [(channels, 2 * channels), row, (channels, channels), row, row, row]
        + [(channels, units), (units,), (9, units), (units,), (units, channels), row]
    )


LOWER_LAYOUT = block_layout(D3, HID3, True)
UPPER_LAYOUT = block_layout(D4, HID4, False)
EMBED_LAYOUT = [(D3,), (D3,), (9 * D3, D4), (D4,), (D4,), (D4,)]


LANES = 128
PAIR_CHUNK = 64
ROW_CHUNK = 160


def layout_places(layout):
    places = []
    offset = 0
    for entry_shape in layout:
        places.append((entry_shape, offset))
        offset = offset + math.prod(entry_shape)
    return places


def is_narrow(entry_shape, offset):
    return entry_shape[-1] % LANES != 0 or offset % LANES != 0


def narrow_ranges(layout):
    ranges = []
    for entry_shape, offset in layout_places(layout):
        if not is_narrow(entry_shape, offset):
            continue
        first = offset // D3
        last = first + math.prod(entry_shape) // D3
        if ranges and ranges[-1][1] == first:
            ranges[-1] = (ranges[-1][0], last)
        else:
            ranges.append((first, last))
    return [(first // 2, (last + 1) // 2) for first, last in ranges]


def round_up(amount, unit):
    return (amount + unit - 1) // unit * unit


def for_chunks(first, last, chunk, step):
    full = (last - first) // chunk

    def body(index, carry):
        step(first + index * chunk, chunk)
        return carry

    if full > 0:
        lax.fori_loop(0, full, body, 0)
    rest = (last - first) - full * chunk
    if rest > 0:
        step(first + full * chunk, rest)


def unpack_group(layout, shard_rows, shard_count, spread, out_refs, dense_ref, narrow_ref):
    lax.fori_loop(0, shard_count, spread, 0)

    def narrow_step(start, amount):
        parts = [
            dense_ref[pl.ds(5 * start + part, amount, stride=5), :] for part in range(5)
        ]
        low_lanes = lax.broadcasted_iota(jnp.int32, (amount, LANES), 1) < LANES // 2
        turned = [pltpu.roll(part, LANES // 2, 1) for part in parts[2:]]
        even_rows = pl.ds(2 * start, amount, stride=2)
        odd_rows = pl.ds(2 * start + 1, amount, stride=2)
        for part in range(3):
            narrow_ref[part, even_rows, :] = parts[part]
        narrow_ref[0, odd_rows, :] = jnp.where(low_lanes, turned[0], turned[1])
        narrow_ref[1, odd_rows, :] = jnp.where(low_lanes, turned[1], turned[2])
        narrow_ref[2, odd_rows, :] = turned[2]

    for first, last in narrow_ranges(layout):
        for_chunks(first, last, PAIR_CHUNK, narrow_step)

    for out_ref, (entry_shape, offset) in zip(out_refs, layout_places(layout)):
        rows = math.prod(entry_shape[:-1])
        cols = entry_shape[-1]
        narrow = is_narrow(entry_shape, offset)

        def copy_rows(start, amount):
            for part in range(-(-cols // LANES)):
                lanes = min(LANES, cols - part * LANES)
                if narrow:
                    piece = narrow_ref[part, pl.ds(offset // D3 + start, amount), :]
                else:
                    stride = cols // LANES
                    base = offset // LANES + part + start * stride
                    piece = dense_ref[pl.ds(base, amount, stride=stride), :]
                out_ref[pl.ds(start, amount), part * LANES : part * LANES + lanes] = piece[
                    :, :lanes
                ].astype(out_ref.dtype)

        if rows < 32:
            copy_rows(0, rows)
        else:
            for_chunks(0, rows, ROW_CHUNK, copy_rows)


def dense_rows_of(layouts, row_counts, shard_count):
    return max(
        round_up(rows * shard_count + round_up(rows, 16), 16)
        for layout, rows in zip(layouts, row_counts)
    )


def narrow_rows_of(layouts):
    return max(
        [16] + [2 * last for layout in layouts for first, last in narrow_ranges(layout)]
    )


def work_scratch(layouts, row_counts, shard_count):
    return [
        pltpu.VMEM((dense_rows_of(layouts, row_counts, shard_count), LANES), jnp.float32),
        pltpu.VMEM((3, round_up(narrow_rows_of(layouts), 16), LANES), jnp.float32),
    ]


def local_rows(flat_shard):
    shard_rows = flat_shard.shape[0] // LANES
    return jnp.pad(
        flat_shard.reshape(shard_rows, LANES).astype(jnp.bfloat16),
        ((0, round_up(shard_rows, 16) - shard_rows), (0, 0)),
    )


def weight_shapes(layout):
    shapes = []
    for entry_shape in layout:
        is_matrix = len(entry_shape) == 2 and entry_shape[0] > 9
        kind = jnp.bfloat16 if is_matrix else jnp.float32
        shape = entry_shape if len(entry_shape) == 2 else (1,) + entry_shape
        shapes.append(shaped(shape, kind))
    return shapes


def unpack_joined(gathered, layouts, row_counts):
    shard_count = gathered.shape[0]

    def kernel(gathered_ref, *refs):
        dense_ref, narrow_ref = refs[-2:]
        first_row = 0
        first_out = 0
        for layout, shard_rows in zip(layouts, row_counts):
            padded_rows = round_up(shard_rows, 16)

            def spread(index, carry, shard_rows=shard_rows, first=first_row, rows=padded_rows):
                dense_ref[pl.ds(index * shard_rows, rows), :] = gathered_ref[
                    index, first : first + rows, :
                ].astype(jnp.float32)
                return carry

            out_refs = refs[first_out : first_out + len(layout)]
            unpack_group(
                layout, shard_rows, shard_count, spread, out_refs, dense_ref, narrow_ref
            )
            first_row += padded_rows
            first_out += len(layout)

    results = pl.pallas_call(
        kernel,
        out_shape=[shape for layout in layouts for shape in weight_shapes(layout)],
        scratch_shapes=work_scratch(layouts, row_counts, shard_count),
        compiler_params=PARAMS,
        name="unpack_joined",
    )(gathered)
    groups = []
    for layout in layouts:
        groups.append(results[: len(layout)])
        results = results[len(layout) :]
    return groups


def swap(values, axis, bit):
    return lax.ppermute(
        values, axis, [(place, place ^ bit) for place in range(lax.axis_size(axis))]
    )


def bit_orders(count):
    bits = [1 << place for place in range(count.bit_length() - 1)]
    return [bits, bits[1::-1] + bits[2:]]


def device_place():
    return jnp.stack([lax.axis_index("dp"), lax.axis_index("fsdp")]).astype(jnp.int32)


PLACE_SPEC = pl.BlockSpec(memory_space=pltpu.SMEM)


def gather_halves(rows, orders, beside):
    half = rows.shape[0] // 32 * 16
    gathered = []
    for number, (piece, order) in enumerate(zip((rows[:half], rows[half:]), orders)):
        held = piece[None]
        for bit in order:
            held = jnp.concatenate([held, swap(held, "fsdp", bit)], axis=0)
        if number == 0:
            held, beside = lax.optimization_barrier((held, beside))
        for bit in bit_orders(lax.axis_size("dp"))[0]:
            held = jnp.concatenate([held, swap(held, "dp", bit)], axis=0)
        gathered.append(held)
    return gathered, beside


def unpack_halves(halves, place, layout, shard_rows, orders):
    shard_count = halves[0].shape[0]
    chips = lax.axis_size("fsdp")
    half = halves[0].shape[1]

    def kernel(place_ref, *refs):
        half_refs = refs[:2]
        out_refs = refs[2:-2]
        dense_ref, narrow_ref = refs[-2:]

        def spread(index, carry):
            apart = (index % chips) ^ place_ref[1]
            cores = (index // chips) ^ place_ref[0]
            for number in range(2):
                position = cores * chips
                for step, bit in enumerate(orders[number]):
                    position = position + ((apart // bit) % 2) * (1 << step)
                rows = half_refs[number].shape[1]
                dense_ref[pl.ds(index * shard_rows + number * half, rows), :] = half_refs[number][
                    position
                ].astype(jnp.float32)
            return carry

        unpack_group(layout, shard_rows, shard_count, spread, out_refs, dense_ref, narrow_ref)

    vmem_spec = pl.BlockSpec(memory_space=pltpu.VMEM)
    return pl.pallas_call(
        kernel,
        in_specs=[PLACE_SPEC, vmem_spec, vmem_spec],
        out_shape=weight_shapes(layout),
        scratch_shapes=work_scratch([layout], [shard_rows], shard_count),
        compiler_params=PARAMS,
        name="unpack_halves",
    )(place, *halves)


def pack_group(layout, sources, in_refs, dense_ref, narrow_ref):
    places = layout_places(layout)
    used_rows = (places[-1][1] + math.prod(places[-1][0])) // LANES
    tail = dense_ref.shape[0] - used_rows
    dense_ref[pl.ds(used_rows, tail), :] = jnp.zeros((tail, LANES), jnp.float32)

    for (operand, first_row), (entry_shape, offset) in zip(sources, places):
        in_ref = in_refs[operand]
        rows = math.prod(entry_shape[:-1])
        cols = entry_shape[-1]
        narrow = is_narrow(entry_shape, offset)

        def copy_rows(start, amount):
            for part in range(-(-cols // LANES)):
                lanes = min(LANES, cols - part * LANES)
                piece = in_ref[pl.ds(first_row + start, amount), part * LANES : part * LANES + lanes]
                if narrow:
                    narrow_ref[part, pl.ds(offset // D3 + start, amount), 0:lanes] = piece
                else:
                    stride = cols // LANES
                    base = offset // LANES + part + start * stride
                    dense_ref[pl.ds(base, amount, stride=stride), :] = piece

        if rows < 32:
            copy_rows(0, rows)
        else:
            for_chunks(0, rows, ROW_CHUNK, copy_rows)

    if narrow and (offset // D3 + rows) % 2 == 1:
        beyond = offset // D3 + rows
        narrow_ref[:, beyond : beyond + 1, :] = jnp.zeros((3, 1, LANES), jnp.float32)

    def narrow_step(start, amount):
        even_rows = pl.ds(2 * start, amount, stride=2)
        odd_rows = pl.ds(2 * start + 1, amount, stride=2)
        low_lanes = lax.broadcasted_iota(jnp.int32, (amount, LANES), 1) < LANES // 2
        even = [narrow_ref[part, even_rows, :] for part in range(3)]
        odd = [pltpu.roll(narrow_ref[part, odd_rows, :], LANES // 2, 1) for part in range(3)]
        joined = [
            even[0],
            even[1],
            jnp.where(low_lanes, even[2], odd[0]),
            jnp.where(low_lanes, odd[0], odd[1]),
            jnp.where(low_lanes, odd[1], odd[2]),
        ]
        for part in range(5):
            dense_ref[pl.ds(5 * start + part, amount, stride=5), :] = joined[part]

    for first, last in narrow_ranges(layout):
        for_chunks(first, last, PAIR_CHUNK, narrow_step)


def pack_grads(place, groups, parts):
    chips = lax.axis_size("fsdp")
    shard_count = lax.axis_size("dp") * chips
    layouts = [group[2] for group in groups]
    row_counts = [group[3] for group in groups]
    counts = [len(group[0]) for group in groups]

    def kernel(place_ref, *refs):
        out_refs = refs[sum(counts) : sum(counts) + len(parts)]
        dense_ref, narrow_ref = refs[-2:]
        first = 0
        for number, (operands, sources, layout, shard_rows) in enumerate(groups):
            in_refs = refs[first : first + len(operands)]
            first += len(operands)
            pack_group(layout, sources, in_refs, dense_ref, narrow_ref)

            def cut(index, carry, number=number, shard_rows=shard_rows):
                for out_ref, (pieces, core, turned) in zip(out_refs, parts):
                    out_row = 0
                    for group, first_row, rows in pieces:
                        if group == number:
                            chip = index ^ place_ref[1] if turned else index
                            shard = (place_ref[0] ^ core) * chips + chip
                            out_ref[index, out_row : out_row + rows, :] = dense_ref[
                                pl.ds(shard * shard_rows + first_row, rows), :
                            ].astype(out_ref.dtype)
                        out_row += rows
                return carry

            lax.fori_loop(0, chips, cut, 0)

    vmem_spec = pl.BlockSpec(memory_space=pltpu.VMEM)
    return pl.pallas_call(
        kernel,
        in_specs=[PLACE_SPEC] + [vmem_spec] * sum(counts),
        out_shape=[
            shaped((chips, sum(piece[2] for piece in pieces), LANES), WIRE_TYPE)
            for pieces, core, turned in parts
        ],
        scratch_shapes=work_scratch(layouts, row_counts, shard_count),
        compiler_params=PARAMS,
        name="pack_grads",
    )(place, *[operand for group in groups for operand in group[0]])


def add_rounded(kept, received):
    return (kept.astype(jnp.float32) + received.astype(jnp.float32)).astype(WIRE_TYPE)


def flat_rows(rows, shard_rows):
    return rows[:shard_rows].astype(jnp.float32).reshape(-1)


def sum_cores(parts):
    parts = list(parts)
    while len(parts) > 1:
        half = len(parts) // 2
        parts = [
            add_rounded(kept, swap(sent, "dp", half))
            for kept, sent in zip(parts[:half], parts[half:])
        ]
    return parts[0]


def scatter_half(parts, order):
    held = sum_cores(parts)
    left = sorted(order, reverse=True)
    held = held.reshape([2] * len(left) + list(held.shape[1:]))
    for bit in order:
        axis = left.index(bit)
        left.remove(bit)
        kept = lax.index_in_dim(held, 0, axis, keepdims=False)
        sent = lax.index_in_dim(held, 1, axis, keepdims=False)
        held = add_rounded(kept, swap(sent, "fsdp", bit))
    return held


def sum_devices(value):
    for axis in AXES:
        for bit in bit_orders(lax.axis_size(axis))[0]:
            value = value + swap(value, axis, bit)
    return value


def dot(left, right):
    return lax.dot_general(
        left, right, (((1,), (0,)), ((), ())), preferred_element_type=jnp.float32
    )


def dot_nt(left, right):
    return lax.dot_general(
        left, right, (((1,), (1,)), ((), ())), preferred_element_type=jnp.float32
    )


def dot_tn(left, right):
    return lax.dot_general(
        left, right, (((0,), (0,)), ((), ())), preferred_element_type=jnp.float32
    )


def rows_sum(values):
    return jnp.sum(values, axis=0, keepdims=True)


def norm_parts(values):
    centred = values - jnp.mean(values, axis=-1, keepdims=True)
    spread = jnp.mean(centred * centred, axis=-1, keepdims=True)
    scale = lax.rsqrt(spread + 1e-06)
    return centred * scale, scale


def norm_grad(unit, scale, gain_row, gradient):
    inner = gradient * gain_row
    first = jnp.mean(inner, axis=-1, keepdims=True)
    second = jnp.mean(inner * unit, axis=-1, keepdims=True)
    return scale * (inner - first - unit * second)


def column_mask(rows, lanes, side, width):
    places = lax.broadcasted_iota(jnp.int32, (rows, lanes), 0)
    return (places & (width - 1)) < side


def softmax_rows(query, key, valid):
    scores = jnp.where(valid, dot_nt(query, key) * 0.125, -1e30)
    powers = jnp.exp(scores - jnp.max(scores, axis=-1, keepdims=True))
    return powers * (1.0 / jnp.sum(powers, axis=-1, keepdims=True))


def split_lanes(values):
    rows, channels = values.shape
    pieces = []
    for first in range(0, channels, LANES):
        piece = values[:, first : min(first + LANES, channels)]
        if piece.shape[1] < LANES:
            rest = jnp.zeros((rows, LANES - piece.shape[1]), values.dtype)
            piece = jnp.concatenate([piece, rest], axis=1)
        pieces.append(piece)
    return pieces


def join_lanes(pieces, channels):
    return jnp.concatenate(pieces, axis=1)[:, :channels]


def softmax_columns(query, key, valid):
    scores = jnp.where(valid, dot_nt(key, query) * 0.125, -1e30)
    powers = jnp.exp(scores - jnp.max(scores, axis=0, keepdims=True))
    return powers * (1.0 / rows_sum(powers))


def pair_place(width, part):
    return pl.ds((part // 2) * width + part % 2, width // 2, stride=2)


def pair_part(grid_ref, width, part, channels):
    pieces = []
    for index in range(grid_ref.shape[0]):
        piece = grid_ref[index, :, pair_place(width, part), :]
        pieces.append(piece.reshape(piece.shape[0] * piece.shape[1], LANES))
    return join_lanes(pieces, channels).astype(jnp.bfloat16)


def attend_kernel(channels, side, width, has_reduction, *refs):
    if has_reduction:
        (
            x_ref, valid_ref, gain_ref, bias_ref, wq_ref, bq_ref, wr_ref, br_ref, rgain_ref,
            rbias_ref, wp_ref, bv_ref, wo_ref, bo_ref, gain2_ref, bias2_ref,
            query_ref, pair_ref, mixed_ref, middle_ref, normed_ref, reduced_ref, padded_ref,
            grid_ref, inputs_ref,
        ) = refs
    else:
        (
            x_ref, valid_ref, gain_ref, bias_ref, wq_ref, bq_ref,
            wp_ref, bv_ref, wo_ref, bo_ref, gain2_ref, bias2_ref,
            query_ref, pair_ref, mixed_ref, middle_ref, normed_ref,
        ) = refs
    inputs = x_ref[0].astype(jnp.float32)
    if has_reduction:
        for row in range(side):
            first = row * width
            inputs_ref[first : first + side, :] = inputs[row * side : (row + 1) * side]
            inputs_ref[first + side : first + width, :] = jnp.zeros(
                (width - side, channels), jnp.float32
            )
        inputs = inputs_ref[...]
        padded_ref[0] = inputs.astype(jnp.bfloat16)
    unit, _ = norm_parts(inputs)
    normed = (unit * gain_ref[...] + bias_ref[...]).astype(jnp.bfloat16)
    query_ref[0] = (dot(normed, wq_ref[...]) + bq_ref[...]).astype(jnp.bfloat16)
    if has_reduction:
        for index, piece in enumerate(split_lanes(normed.astype(jnp.float32))):
            grid_ref[index] = piece.reshape(grid_ref.shape[1:])
        reduced = br_ref[...]
        for part in range(4):
            reduced = reduced + dot(
                pair_part(grid_ref, width, part, channels),
                wr_ref[part * channels : (part + 1) * channels, :],
            )
        reduced_ref[0] = reduced
        unit, _ = norm_parts(reduced)
        source = (unit * rgain_ref[...] + rbias_ref[...]).astype(jnp.bfloat16)
    else:
        source = normed
    pair_ref[0, :, :channels] = dot(source, wp_ref[:, :channels]).astype(jnp.bfloat16)
    pair_ref[0, :, channels:] = (dot(source, wp_ref[:, channels:]) + bv_ref[...]).astype(
        jnp.bfloat16
    )
    valid = valid_ref[0] > 0.5
    for head in range(channels // HEAD):
        lanes = slice(head * HEAD, (head + 1) * HEAD)
        value_lanes = slice(channels + head * HEAD, channels + (head + 1) * HEAD)
        query = query_ref[0, :, lanes]
        key = pair_ref[0, :, lanes]
        value = pair_ref[0, :, value_lanes]
        if has_reduction:
            chances = softmax_columns(query, key, valid).astype(jnp.bfloat16)
            mixed = dot_tn(chances, value)
        else:
            chances = softmax_rows(query, key, valid).astype(jnp.bfloat16)
            mixed = dot(chances, value)
        mixed_ref[0, :, lanes] = mixed.astype(jnp.bfloat16)
    middle = inputs + (dot(mixed_ref[0], wo_ref[...]) + bo_ref[...])
    middle_ref[0] = middle
    unit, _ = norm_parts(middle)
    normed_ref[0] = (unit * gain2_ref[...] + bias2_ref[...]).astype(jnp.bfloat16)


def whole(shape):
    return pl.BlockSpec(shape, lambda *place: (0,) * len(shape))


def image_block(array):
    return pl.BlockSpec((1,) + array.shape[1:], lambda image: (image,) + (0,) * (len(array.shape) - 1))


def shaped(shape, kind):
    return jax.ShapeDtypeStruct(shape, kind)


PARAMS = pltpu.CompilerParams(vmem_limit_bytes=61000 * 1024)


def attend_block(inputs, valid, weights, side, width):
    images, _, channels = inputs.shape
    tokens = side * width
    has_reduction = len(weights) == 14
    keys = valid.shape[2]
    if has_reduction:
        valid = valid.swapaxes(1, 2)
    outs = [
        shaped((images, tokens, channels), jnp.bfloat16),
        shaped((images, keys, 2 * channels), jnp.bfloat16),
        shaped((images, tokens, channels), jnp.bfloat16),
        shaped((images, tokens, channels), jnp.float32),
        shaped((images, tokens, channels), jnp.bfloat16),
    ]
    scratch = []
    if has_reduction:
        outs.append(shaped((images, keys, channels), jnp.float32))
        outs.append(shaped((images, tokens, channels), jnp.bfloat16))
        grid_shape = (-(-channels // LANES), tokens // (2 * width), 2 * width, LANES)
        scratch.append(pltpu.VMEM(grid_shape, jnp.float32))
        scratch.append(pltpu.VMEM((tokens, channels), jnp.float32))
    return pl.pallas_call(
        lambda *refs: attend_kernel(channels, side, width, has_reduction, *refs),
        grid=(images,),
        in_specs=[image_block(inputs), image_block(valid)] + [whole(w.shape) for w in weights],
        out_specs=[image_block(out) for out in outs],
        out_shape=outs,
        scratch_shapes=scratch,
        compiler_params=PARAMS,
        name="attend",
    )(inputs, valid, *weights)


def zero_edges(ref, side, width, columns):
    tokens = side * width
    lanes = ref.shape[1]
    ref[0:width, :] = jnp.zeros((width, lanes), jnp.float32)
    ref[width + tokens : 2 * width + tokens, :] = jnp.zeros((width, lanes), jnp.float32)
    if columns:
        for row in range(1, side + 1):
            ref[row * width + side : (row + 1) * width, :] = jnp.zeros(
                (width - side, lanes), jnp.float32
            )


def store_cells(ref, values, side, width):
    for row in range(side):
        ref[0, row * side : (row + 1) * side, :] = values[row * width : row * width + side]


def mix_kernel(side, width, lanes, dense, *refs):
    (
        normed_ref, middle_ref, we_ref, be_ref, kd_ref, bd_ref, wc_ref, bc_ref,
        out_ref, mixed_ref, slope_ref, pad_ref,
    ) = refs
    tokens = side * width
    units = we_ref.shape[1]
    pad_ref[width : width + tokens, :] = dot(normed_ref[0], we_ref[...]) + be_ref[...]
    zero_edges(pad_ref, side, width, True)

    def step(row, carry):
        start = pl.multiple_of(row * width, width)
        for first in range(0, units, lanes):
            block = slice(first, first + lanes)
            rows = [pad_ref[pl.ds(start + up * width, width), block] for up in range(3)]
            sums = [
                kd_ref[col : col + 1, block] * rows[0]
                + kd_ref[3 + col : 4 + col, block] * rows[1]
                + kd_ref[6 + col : 7 + col, block] * rows[2]
                for col in range(3)
            ]
            value = (
                sums[1]
                + pltpu.roll(sums[0], 1, 0)
                + pltpu.roll(sums[2], width - 1, 0)
                + bd_ref[:, block]
            )
            share = 0.5 + 0.5 * lax.erf(value * math.sqrt(0.5))
            bell = jnp.exp(value * value * -0.5) * (1.0 / math.sqrt(2.0 * math.pi))
            mixed_ref[0, pl.ds(start, width), block] = (value * share).astype(jnp.bfloat16)
            slope_ref[0, pl.ds(start, width), block] = (share + value * bell).astype(jnp.bfloat16)
        return carry

    lax.fori_loop(0, side, step, 0)
    result = middle_ref[0] + bc_ref[...] + dot(mixed_ref[0], wc_ref[...])
    if dense:
        store_cells(out_ref, result, side, width)
    else:
        out_ref[0] = result


def mix_block(normed, middle, weights, side, width, lanes, dense):
    images, tokens, channels = middle.shape
    units = weights[0].shape[1]
    outs = [
        shaped((images, side * side if dense else tokens, channels), jnp.float32),
        shaped((images, tokens, units), jnp.bfloat16),
        shaped((images, tokens, units), jnp.bfloat16),
    ]
    return pl.pallas_call(
        lambda *refs: mix_kernel(side, width, lanes, dense, *refs),
        grid=(images,),
        in_specs=[image_block(normed), image_block(middle)] + [whole(w.shape) for w in weights],
        out_specs=[image_block(out) for out in outs],
        out_shape=outs,
        scratch_shapes=[pltpu.VMEM((tokens + 2 * width, units), jnp.float32)],
        compiler_params=PARAMS,
        name="mix",
    )(normed, middle, *weights)


def mix_back_kernel(side, width, lanes, *refs):
    (
        normed_ref, grad_ref, mixed_ref, slope_ref, we_ref, be_ref, kd_ref, wc_ref,
        dnormed_ref, dwe_ref, dwc_ref, drows_ref, pad_ref, dpad_ref, dhid_ref,
    ) = refs
    tokens = side * width
    units = we_ref.shape[1]
    gradient = grad_ref[0].astype(jnp.bfloat16)
    pad_ref[width : width + tokens, :] = dot(normed_ref[0], we_ref[...]) + be_ref[...]
    dpad_ref[width : width + tokens, :] = dot_nt(gradient, wc_ref[...]) * slope_ref[0].astype(
        jnp.float32
    )
    zero_edges(pad_ref, side, width, True)
    zero_edges(dpad_ref, side, width, False)

    @pl.when(pl.program_id(0) == 0)
    def _():
        for ref in (drows_ref, dwe_ref, dwc_ref):
            ref[...] = jnp.zeros(ref.shape, jnp.float32)

    inside = column_mask(width, lanes, side, width)

    def fold(values):
        total = values[0:8]
        for start in range(8, width, 8):
            total = total + values[start : start + 8]
        return total

    for first in range(0, units, lanes):
        block = slice(first, first + lanes)

        def step(row, sums, block=block):
            start = pl.multiple_of(row * width, width)
            rows = [pad_ref[pl.ds(start + up * width, width), block] for up in range(3)]
            drows = [dpad_ref[pl.ds(start + up * width, width), block] for up in range(3)]
            turned = [
                pltpu.roll(drows[1], width - 1, 0),
                drows[1],
                pltpu.roll(drows[1], 1, 0),
            ]
            found = []
            for up in range(3):
                for col in range(3):
                    found.append(sums[3 * up + col] + fold(turned[col] * rows[up]))
            found.append(sums[9] + fold(drows[1]))
            parts = [
                kd_ref[col : col + 1, block] * drows[2]
                + kd_ref[3 + col : 4 + col, block] * drows[1]
                + kd_ref[6 + col : 7 + col, block] * drows[0]
                for col in range(3)
            ]
            value = parts[1] + pltpu.roll(parts[0], width - 1, 0) + pltpu.roll(parts[2], 1, 0)
            value = jnp.where(inside, value, 0.0)
            dhid_ref[pl.ds(start, width), block] = value.astype(jnp.bfloat16)
            found.append(sums[10] + fold(value))
            return tuple(found)

        zero = jnp.zeros((8, lanes), jnp.float32)
        totals = lax.fori_loop(0, side, step, (zero,) * 11, unroll=2)
        for index in range(11):
            drows_ref[index : index + 1, block] += rows_sum(totals[index])
    dhidden = dhid_ref[...]
    dwe_ref[...] += dot_tn(normed_ref[0], dhidden)
    dwc_ref[...] += dot_tn(mixed_ref[0], gradient)
    dnormed_ref[0] = dot_nt(dhidden, we_ref[...])


def mix_back(normed, gradient, mixed, slope, weights, side, width, lanes):
    we, be, kd, bd, wc, bc = weights
    images, tokens, channels = normed.shape
    units = we.shape[1]
    operands = [normed, gradient, mixed, slope]
    used = [we, be, kd, wc]
    outs = [
        shaped((images, tokens, channels), jnp.float32),
        shaped((channels, units), jnp.float32),
        shaped((units, channels), jnp.float32),
        shaped((16, units), jnp.float32),
    ]
    return pl.pallas_call(
        lambda *refs: mix_back_kernel(side, width, lanes, *refs),
        grid=(images,),
        in_specs=[image_block(op) for op in operands] + [whole(u.shape) for u in used],
        out_specs=[image_block(outs[0])] + [whole(out.shape) for out in outs[1:]],
        out_shape=outs,
        scratch_shapes=[
            pltpu.VMEM((tokens + 2 * width, units), jnp.float32),
            pltpu.VMEM((tokens + 2 * width, units), jnp.float32),
            pltpu.VMEM((tokens, units), jnp.bfloat16),
        ],
        compiler_params=PARAMS,
        name="mix_back",
    )(*operands, *used)


def attend_back_kernel(channels, side, width, has_reduction, *refs):
    if has_reduction:
        (
            x_ref, valid_ref, grad_ref, dnormed_ref, middle_ref, query_ref, pair_ref, mixed_ref,
            reduced_ref, gain_ref, bias_ref, wq_ref, wr_ref, rgain_ref, rbias_ref, wp_ref, wo_ref,
            gain2_ref,
            dx_ref, dwq_ref, dwp_ref, dwo_ref, vec_ref, dwr_ref,
            dquery_ref, dpair_ref, dmiddle_ref, grid_ref, dgrid_ref,
        ) = refs
    else:
        (
            x_ref, valid_ref, grad_ref, dnormed_ref, middle_ref, query_ref, pair_ref, mixed_ref,
            gain_ref, bias_ref, wq_ref, wp_ref, wo_ref, gain2_ref,
            dx_ref, dwq_ref, dwp_ref, dwo_ref, vec_ref,
            dquery_ref, dpair_ref, dmiddle_ref,
        ) = refs

    @pl.when(pl.program_id(0) == 0)
    def _():
        sums = [dwq_ref, dwp_ref, dwo_ref, vec_ref] + ([dwr_ref] if has_reduction else [])
        for ref in sums:
            ref[...] = jnp.zeros(ref.shape, jnp.float32)

    def add_row(index, row):
        vec_ref[index : index + 1, :] += row

    gradient = grad_ref[0].astype(jnp.float32)
    add_row(0, rows_sum(gradient.astype(jnp.bfloat16).astype(jnp.float32)))
    dnormed = dnormed_ref[0]
    unit, scale = norm_parts(middle_ref[0])
    add_row(1, rows_sum(dnormed * unit))
    add_row(2, rows_sum(dnormed))
    dmiddle = gradient + norm_grad(unit, scale, gain2_ref[...], dnormed)
    dmiddle_ref[...] = dmiddle
    doutput = dmiddle.astype(jnp.bfloat16)
    add_row(3, rows_sum(doutput.astype(jnp.float32)))
    dwo_ref[...] += dot_tn(mixed_ref[0], doutput)
    dmixed = dot_nt(doutput, wo_ref[...]).astype(jnp.bfloat16)
    valid = valid_ref[0] > 0.5
    for head in range(channels // HEAD):
        lanes = slice(head * HEAD, (head + 1) * HEAD)
        value_lanes = slice(channels + head * HEAD, channels + (head + 1) * HEAD)
        query = query_ref[0, :, lanes]
        key = pair_ref[0, :, lanes]
        chances = softmax_columns(query, key, valid)
        dhead = dmixed[:, lanes]
        dchances = dot_nt(pair_ref[0, :, value_lanes], dhead)
        dpair_ref[:, value_lanes] = dot(chances.astype(jnp.bfloat16), dhead).astype(jnp.bfloat16)
        weighted = chances * dchances
        dscores = (weighted - chances * rows_sum(weighted)).astype(jnp.bfloat16)
        dquery_ref[:, lanes] = (dot_tn(dscores, key) * 0.125).astype(jnp.bfloat16)
        dpair_ref[:, lanes] = (dot(dscores, query) * 0.125).astype(jnp.bfloat16)
    dquery = dquery_ref[...]
    dpair = dpair_ref[...]
    unit, scale = norm_parts(x_ref[0].astype(jnp.float32))
    normed = (unit * gain_ref[...] + bias_ref[...]).astype(jnp.bfloat16)
    add_row(4, rows_sum(dquery.astype(jnp.float32)))
    add_row(5, rows_sum(dpair[:, channels:].astype(jnp.float32)))
    dwq_ref[...] += dot_tn(normed, dquery)
    total = dot_nt(dquery, wq_ref[...])
    dsource = dot_nt(dpair, wp_ref[...])
    if has_reduction:
        runit, rscale = norm_parts(reduced_ref[0])
        source = (runit * rgain_ref[...] + rbias_ref[...]).astype(jnp.bfloat16)
        dwp_ref[...] += dot_tn(source, dpair)
        add_row(8, rows_sum(dsource * runit))
        add_row(9, rows_sum(dsource))
        dreduced = norm_grad(runit, rscale, rgain_ref[...], dsource).astype(jnp.bfloat16)
        add_row(10, rows_sum(dreduced.astype(jnp.float32)))
        for index, piece in enumerate(split_lanes(normed.astype(jnp.float32))):
            grid_ref[index] = piece.reshape(grid_ref.shape[1:])
        for index, piece in enumerate(split_lanes(total)):
            dgrid_ref[index] = piece.reshape(dgrid_ref.shape[1:])
        for part in range(4):
            rows = slice(part * channels, (part + 1) * channels)
            dwr_ref[rows, :] += dot_tn(pair_part(grid_ref, width, part, channels), dreduced)
            for index, piece in enumerate(split_lanes(dot_nt(dreduced, wr_ref[rows, :]))):
                dgrid_ref[index, :, pair_place(width, part), :] += piece.reshape(
                    dgrid_ref.shape[1], width // 2, LANES
                )
        total = join_lanes(
            [dgrid_ref[index].reshape(total.shape[0], LANES) for index in range(dgrid_ref.shape[0])],
            channels,
        )
    else:
        dwp_ref[...] += dot_tn(normed, dpair)
        total = total + dsource
    add_row(6, rows_sum(total * unit))
    add_row(7, rows_sum(total))
    result = dmiddle_ref[...] + norm_grad(unit, scale, gain_ref[...], total)
    if has_reduction:
        store_cells(dx_ref, result, side, width)
    else:
        dx_ref[0] = result


def attend_back(inputs, valid, gradient, dnormed, saved, weights, side, width):
    query, pair, mixed, middle, normed = saved[:5]
    images, tokens, channels = middle.shape
    has_reduction = len(saved) > 5
    keys = valid.shape[2]
    operands = [inputs, valid.swapaxes(1, 2), gradient, dnormed, middle, query, pair, mixed]
    outs = [
        shaped((images, side * side if has_reduction else tokens, channels), jnp.float32),
        shaped((channels, channels), jnp.float32),
        shaped((channels, 2 * channels), jnp.float32),
        shaped((channels, channels), jnp.float32),
        shaped((16, channels), jnp.float32),
    ]
    scratch = [
        pltpu.VMEM((tokens, channels), jnp.bfloat16),
        pltpu.VMEM((keys, 2 * channels), jnp.bfloat16),
        pltpu.VMEM((tokens, channels), jnp.float32),
    ]
    if has_reduction:
        gain, bias, wq, bq, wr, br, rgain, rbias, wp, bv, wo, bo, gain2, bias2 = weights
        used = [gain, bias, wq, wr, rgain, rbias, wp, wo, gain2]
        operands.append(saved[5])
        outs.append(shaped((4 * channels, channels), jnp.float32))
        grid_shape = (-(-channels // LANES), tokens // (2 * width), 2 * width, LANES)
        scratch += [pltpu.VMEM(grid_shape, jnp.float32), pltpu.VMEM(grid_shape, jnp.float32)]
    else:
        gain, bias, wq, bq, wp, bv, wo, bo, gain2, bias2 = weights
        used = [gain, bias, wq, wp, wo, gain2]
    return pl.pallas_call(
        lambda *refs: attend_back_kernel(channels, side, width, has_reduction, *refs),
        grid=(images,),
        in_specs=[image_block(op) for op in operands] + [whole(w.shape) for w in used],
        out_specs=[image_block(outs[0])] + [whole(out.shape) for out in outs[1:]],
        out_shape=outs,
        scratch_shapes=scratch,
        compiler_params=PARAMS,
        name="attend_back",
    )(*operands, *used)


def tap_place(width, tap, row):
    first = LEAD + (tap // 3) * width + tap % 3 - 1
    return pl.ds(first + 2 * width * row, width // 2, stride=2)


def load_tap(grid_ref, side, width, tap, channels):
    pieces = []
    for index in range(grid_ref.shape[0]):
        rows = [grid_ref[index, tap_place(width, tap, row), :] for row in range(side // 2)]
        pieces.append(jnp.concatenate(rows, axis=0))
    return join_lanes(pieces, channels).astype(jnp.bfloat16)


def fill_grid(grid_ref, values, width):
    rows = grid_ref.shape[1]
    first = LEAD + width
    last = first + values.shape[0]
    for index, piece in enumerate(split_lanes(values)):
        grid_ref[index, 0:first, :] = jnp.zeros((first, LANES), jnp.float32)
        grid_ref[index, first:last, :] = piece
        grid_ref[index, last:rows, :] = jnp.zeros((rows - last, LANES), jnp.float32)


LEAD = 8


def embed_kernel(side, width, *refs):
    x_ref, gain_ref, bias_ref, w_ref, b_ref, pgain_ref, pbias_ref = refs[:7]
    out_ref, patch_ref, grid_ref = refs[7:]
    tokens, channels = x_ref.shape[1:]
    unit, _ = norm_parts(x_ref[0])
    normed = (unit * gain_ref[...] + bias_ref[...]).astype(jnp.bfloat16).astype(jnp.float32)
    inside = column_mask(tokens, channels, side, width)
    fill_grid(grid_ref, jnp.where(inside, normed, 0.0), width)
    patch = b_ref[...]
    for tap in range(9):
        patch = patch + dot(
            load_tap(grid_ref, side, width, tap, channels),
            w_ref[tap * channels : (tap + 1) * channels, :]
        )
    patch_ref[0] = patch
    unit, _ = norm_parts(patch)
    out_ref[0] = unit * pgain_ref[...] + pbias_ref[...]


def embed_block(inputs, weights, side, width):
    images, tokens, channels = inputs.shape
    units = weights[2].shape[1]
    outs = [shaped((images, tokens // 4, units), jnp.float32)] * 2
    return pl.pallas_call(
        lambda *refs: embed_kernel(side, width, *refs),
        grid=(images,),
        in_specs=[image_block(inputs)] + [whole(w.shape) for w in weights],
        out_specs=[image_block(out) for out in outs],
        out_shape=outs,
        scratch_shapes=[pltpu.VMEM((-(-channels // LANES), LEAD + (side + 3) * width, LANES), jnp.float32)],
        compiler_params=PARAMS,
        name="embed",
    )(inputs, *weights)


def embed_back_kernel(side, width, *refs):
    x_ref, grad_ref, patch_ref, gain_ref, bias_ref, w_ref, pgain_ref = refs[:7]
    dx_ref, dw_ref, vec_ref, pvec_ref, grid_ref, dgrid_ref = refs[7:]
    tokens, channels = x_ref.shape[1:]

    @pl.when(pl.program_id(0) == 0)
    def _():
        for ref in (dw_ref, vec_ref, pvec_ref):
            ref[...] = jnp.zeros(ref.shape, jnp.float32)

    gradient = grad_ref[0]
    punit, pscale = norm_parts(patch_ref[0])
    pvec_ref[0:1, :] += rows_sum(gradient * punit)
    pvec_ref[1:2, :] += rows_sum(gradient)
    dpatch = norm_grad(punit, pscale, pgain_ref[...], gradient).astype(jnp.bfloat16)
    pvec_ref[2:3, :] += rows_sum(dpatch.astype(jnp.float32))
    unit, scale = norm_parts(x_ref[0])
    normed = (unit * gain_ref[...] + bias_ref[...]).astype(jnp.bfloat16).astype(jnp.float32)
    inside = column_mask(tokens, channels, side, width)
    fill_grid(grid_ref, jnp.where(inside, normed, 0.0), width)
    dgrid_ref[...] = jnp.zeros(dgrid_ref.shape, jnp.float32)
    half = width // 2
    for tap in range(9):
        rows = slice(tap * channels, (tap + 1) * channels)
        dw_ref[rows, :] += dot_tn(load_tap(grid_ref, side, width, tap, channels), dpatch)
        for index, piece in enumerate(split_lanes(dot_nt(dpatch, w_ref[rows, :]))):
            for row in range(side // 2):
                dgrid_ref[index, tap_place(width, tap, row), :] += piece[
                    row * half : (row + 1) * half, :
                ]
    first = LEAD + width
    pieces = [dgrid_ref[index, first : first + tokens, :] for index in range(dgrid_ref.shape[0])]
    total = jnp.where(inside, join_lanes(pieces, channels), 0.0)
    vec_ref[0:1, :] += rows_sum(total * unit)
    vec_ref[1:2, :] += rows_sum(total)
    dx_ref[0] = norm_grad(unit, scale, gain_ref[...], total)


def embed_back(inputs, gradient, patch, weights, side, width):
    gain, bias, w, b, pgain, pbias = weights
    images, tokens, channels = inputs.shape
    units = w.shape[1]
    outs = [
        shaped(inputs.shape, jnp.float32),
        shaped(w.shape, jnp.float32),
        shaped((8, channels), jnp.float32),
        shaped((8, units), jnp.float32),
    ]
    operands = [inputs, gradient, patch]
    used = [gain, bias, w, pgain]
    grid_scratch = pltpu.VMEM((-(-channels // LANES), LEAD + (side + 3) * width, LANES), jnp.float32)
    return pl.pallas_call(
        lambda *refs: embed_back_kernel(side, width, *refs),
        grid=(images,),
        in_specs=[image_block(op) for op in operands] + [whole(u.shape) for u in used],
        out_specs=[image_block(outs[0])] + [whole(out.shape) for out in outs[1:]],
        out_shape=outs,
        scratch_shapes=[grid_scratch, grid_scratch],
        compiler_params=PARAMS,
        name="embed_back",
    )(*operands, *used)


def to_grid(values, side, width):
    images, tokens, channels = values.shape
    grid = values.reshape(images, side, side, channels)
    grid = jnp.pad(grid, ((0, 0), (0, 0), (0, width - side), (0, 0)))
    return grid.reshape(images, side * width, channels)


def key_mask(row_counts, col_counts, side, width):
    places = jnp.arange(side * width, dtype=jnp.int32)
    valid = ((places // width)[None, :] < row_counts[:, None]) & (
        (places % width)[None, :] < col_counts[:, None]
    )
    return valid.astype(jnp.float32)[:, None, :]


def block_sources(has_reduction):
    reduction = [(7, 0), (3, 10), (3, 8), (3, 9)] if has_reduction else []
    return (
        [(3, 6), (3, 7), (0, 0), (3, 4)]
        + reduction
        + [(1, 0), (3, 5), (2, 0), (3, 3), (3, 1), (3, 2)]
        + [(4, 0), (6, 10), (6, 0), (6, 9), (5, 0), (3, 0)]
    )


EMBED_SOURCES = [(1, 0), (1, 1), (0, 0), (2, 2), (2, 0), (2, 1)]


def adamw_update(weights, mean_old, square_old, gradient, clip_factor, rate_value, fix_one):
    clipped = gradient * clip_factor
    mean_new = 0.5 * mean_old + 0.5 * clipped
    square_new = 0.5 * square_old + 0.5 * clipped * clipped
    updated = weights * (1.0 - rate_value * 0.05) - rate_value * (mean_new / fix_one) / (
        jnp.sqrt(square_new / fix_one) + 1e-08
    )
    return (updated, mean_new, square_new)


def shards(
    features,
    key_rows,
    key_cols,
    out_grad,
    lower_weights,
    lower_mean,
    lower_square,
    embed_weights,
    embed_mean,
    embed_square,
    upper_weights,
    upper_mean,
    upper_square,
    learn_rate,
):
    side, half = GRID, GRID // 2
    width = round_up(side, 32)
    half_width = width // 2
    key_valid = key_mask(key_rows, key_cols, half, half_width)
    cores = lax.axis_size("dp")
    orders = bit_orders(lax.axis_size("fsdp"))
    place = device_place()
    lower_rows, embed_rows, upper_rows = (
        flat.shape[0] // LANES for flat in (lower_weights, embed_weights, upper_weights)
    )
    lower_halves, grad_in = gather_halves(
        local_rows(lower_weights), [order[2:] + order[:2] for order in orders], to_grid(out_grad, half, half_width)
    )
    rest_local = jnp.concatenate([local_rows(embed_weights), local_rows(upper_weights)], axis=0)
    *lower_halves, rest_local = lax.optimization_barrier((*lower_halves, rest_local))
    rest = lax.all_gather(rest_local, AXES, axis=0, tiled=False)
    lower = unpack_halves(
        lower_halves, place, LOWER_LAYOUT, lower_rows, [order[2:] + order[:2] for order in orders]
    )
    embed, upper = unpack_joined(rest, [EMBED_LAYOUT, UPPER_LAYOUT], [embed_rows, upper_rows])

    lower_saved = attend_block(features, key_valid, lower[:14], side, width)
    three_in = lower_saved[6]
    section_three, lower_mixed, lower_slope = mix_block(
        lower_saved[4], lower_saved[3], lower[14:], side, width, 256, False
    )
    section_four, patch = embed_block(section_three, embed, side, width)
    upper_saved = attend_block(section_four, key_valid, upper[:10], half, half_width)
    block_out, upper_mixed, upper_slope = mix_block(
        upper_saved[4], upper_saved[3], upper[10:], half, half_width, 256, True
    )

    def back(inputs, gradient, saved, mixed, slope, weights, first, side, width, lanes):
        dnormed, dwe, dwc, drows = mix_back(
            saved[4], gradient, mixed, slope, weights[first:], side, width, lanes
        )
        dx, dwq, dwp, dwo, vec, *rest = attend_back(
            inputs, key_valid, gradient, dnormed, saved, weights[:first], side, width
        )
        return dx, [dwq, dwp, dwo, vec, dwe, dwc, drows] + rest

    four_grad, upper_found = back(
        section_four, grad_in, upper_saved, upper_mixed, upper_slope, upper, 10, half, half_width, 256
    )
    upper_wire = pack_grads(
        place,
        [(upper_found, block_sources(False), UPPER_LAYOUT, upper_rows)],
        [([(0, 0, round_up(upper_rows, 16))], core, False) for core in range(cores)],
    )
    *upper_wire, four_grad = lax.optimization_barrier((*upper_wire, four_grad))
    three_grad, *embed_found = embed_back(section_three, four_grad, patch, embed, side, width)
    embed_wire = pack_grads(
        place,
        [(embed_found, EMBED_SOURCES, EMBED_LAYOUT, embed_rows)],
        [([(0, 0, round_up(embed_rows, 16))], core, False) for core in range(cores)],
    )
    rest_sum = jnp.concatenate([sum_cores(embed_wire), sum_cores(upper_wire)], axis=1)
    rest_sum, three_grad = lax.optimization_barrier((rest_sum, three_grad))
    rest_grad = lax.psum_scatter(rest_sum, "fsdp", scatter_dimension=0, tiled=False)
    input_grad, lower_found = back(
        three_in, three_grad, lower_saved, lower_mixed, lower_slope, lower, 14, side, width, 256
    )
    padded_rows = round_up(lower_rows, 16)
    half_rows = padded_rows // 32 * 16
    parts = []
    for first, rows in ((0, half_rows), (half_rows, padded_rows - half_rows)):
        parts += [([(0, first, rows)], core, True) for core in range(cores)]
    wire = pack_grads(
        place, [(lower_found, block_sources(True), LOWER_LAYOUT, lower_rows)], parts
    )
    lower_sum = jnp.concatenate(
        [scatter_half(wire[:cores], orders[0]), scatter_half(wire[cores:], orders[1])], axis=0
    )
    lower_grad = flat_rows(lower_sum, lower_rows)
    embed_grad = flat_rows(rest_grad, embed_rows)
    upper_grad = flat_rows(rest_grad[round_up(embed_rows, 16) :], upper_rows)
    local_squares = (
        jnp.sum(lower_grad * lower_grad)
        + jnp.sum(embed_grad * embed_grad)
        + jnp.sum(upper_grad * upper_grad)
    )
    squares = sum_devices(local_squares.reshape(1, 1))[0, 0]
    grad_norm = jnp.sqrt(squares)
    clip_factor = jnp.minimum(1.0, 5.0 / (grad_norm + 1e-06))
    rate_value = learn_rate[0]
    fix_one = 1.0 - 0.5**ADAM_STEP
    lower_new, lower_mean_new, lower_square_new = adamw_update(
        lower_weights, lower_mean, lower_square, lower_grad, clip_factor, rate_value, fix_one
    )
    embed_new, embed_mean_new, embed_square_new = adamw_update(
        embed_weights, embed_mean, embed_square, embed_grad, clip_factor, rate_value, fix_one
    )
    upper_new, upper_mean_new, upper_square_new = adamw_update(
        upper_weights, upper_mean, upper_square, upper_grad, clip_factor, rate_value, fix_one
    )
    return (
        block_out,
        input_grad,
        grad_norm.reshape(1),
        lower_grad,
        lower_new,
        lower_mean_new,
        lower_square_new,
        lower_new.astype(jnp.bfloat16),
        embed_grad,
        embed_new,
        embed_mean_new,
        embed_square_new,
        embed_new.astype(jnp.bfloat16),
        upper_grad,
        upper_new,
        upper_mean_new,
        upper_square_new,
        upper_new.astype(jnp.bfloat16),
    )


AXES = ("dp", "fsdp")
TOKENS = P(AXES, None, None)
FLAT = P(AXES)


def solution(mesh):
    return jax.shard_map(
        shards,
        mesh=mesh,
        in_specs=(
            TOKENS,
            FLAT,
            FLAT,
            TOKENS,
            FLAT,
            FLAT,
            FLAT,
            FLAT,
            FLAT,
            FLAT,
            FLAT,
            FLAT,
            FLAT,
            P(),
        ),
        out_specs=(
            TOKENS,
            TOKENS,
            P(),
            FLAT,
            FLAT,
            FLAT,
            FLAT,
            FLAT,
            FLAT,
            FLAT,
            FLAT,
            FLAT,
            FLAT,
            FLAT,
            FLAT,
            FLAT,
            FLAT,
            FLAT,
        ),
        check_vma=False,
    )
```

```python
import math

import jax
import jax.numpy as jnp
from jax import lax
from jax.experimental import pallas as pl
from jax.experimental.pallas import tpu as pltpu
from jax.sharding import PartitionSpec as P

D3 = 320
D4 = 512
HID3 = 1280
HID4 = 2048
HEAD = 64
GRID = 28
ADAM_STEP = 2
WIRE_TYPE = jnp.bfloat16


def block_layout(channels, units, has_reduction):
    row = (channels,)
    reduction = [(4 * channels, channels), row, row, row] if has_reduction else []
    return (
        [row, row, (channels, channels), row]
        + reduction
        + [(channels, 2 * channels), row, (channels, channels), row, row, row]
        + [(channels, units), (units,), (9, units), (units,), (units, channels), row]
    )


LOWER_LAYOUT = block_layout(D3, HID3, True)
UPPER_LAYOUT = block_layout(D4, HID4, False)
EMBED_LAYOUT = [(D3,), (D3,), (9 * D3, D4), (D4,), (D4,), (D4,)]


LANES = 128
PAIR_CHUNK = 64
ROW_CHUNK = 160


def layout_places(layout):
    places = []
    offset = 0
    for entry_shape in layout:
        places.append((entry_shape, offset))
        offset = offset + math.prod(entry_shape)
    return places


def is_narrow(entry_shape, offset):
    return entry_shape[-1] % LANES != 0 or offset % LANES != 0


def narrow_ranges(layout):
    ranges = []
    for entry_shape, offset in layout_places(layout):
        if not is_narrow(entry_shape, offset):
            continue
        first = offset // D3
        last = first + math.prod(entry_shape) // D3
        if ranges and ranges[-1][1] == first:
            ranges[-1] = (ranges[-1][0], last)
        else:
            ranges.append((first, last))
    return [(first // 2, (last + 1) // 2) for first, last in ranges]


def round_up(amount, unit):
    return (amount + unit - 1) // unit * unit


def for_chunks(first, last, chunk, step):
    full = (last - first) // chunk

    def body(index, carry):
        step(first + index * chunk, chunk)
        return carry

    if full > 0:
        lax.fori_loop(0, full, body, 0)
    rest = (last - first) - full * chunk
    if rest > 0:
        step(first + full * chunk, rest)


def unpack_group(layout, shard_rows, shard_count, spread, out_refs, dense_ref, narrow_ref):
    lax.fori_loop(0, shard_count, spread, 0)

    def narrow_step(start, amount):
        parts = [
            dense_ref[pl.ds(5 * start + part, amount, stride=5), :] for part in range(5)
        ]
        low_lanes = lax.broadcasted_iota(jnp.int32, (amount, LANES), 1) < LANES // 2
        turned = [pltpu.roll(part, LANES // 2, 1) for part in parts[2:]]
        even_rows = pl.ds(2 * start, amount, stride=2)
        odd_rows = pl.ds(2 * start + 1, amount, stride=2)
        for part in range(3):
            narrow_ref[part, even_rows, :] = parts[part]
        narrow_ref[0, odd_rows, :] = jnp.where(low_lanes, turned[0], turned[1])
        narrow_ref[1, odd_rows, :] = jnp.where(low_lanes, turned[1], turned[2])
        narrow_ref[2, odd_rows, :] = turned[2]

    for first, last in narrow_ranges(layout):
        for_chunks(first, last, PAIR_CHUNK, narrow_step)

    for out_ref, (entry_shape, offset) in zip(out_refs, layout_places(layout)):
        rows = math.prod(entry_shape[:-1])
        cols = entry_shape[-1]
        narrow = is_narrow(entry_shape, offset)

        def copy_rows(start, amount):
            for part in range(-(-cols // LANES)):
                lanes = min(LANES, cols - part * LANES)
                if narrow:
                    piece = narrow_ref[part, pl.ds(offset // D3 + start, amount), :]
                else:
                    stride = cols // LANES
                    base = offset // LANES + part + start * stride
                    piece = dense_ref[pl.ds(base, amount, stride=stride), :]
                out_ref[pl.ds(start, amount), part * LANES : part * LANES + lanes] = piece[
                    :, :lanes
                ].astype(out_ref.dtype)

        if rows < 32:
            copy_rows(0, rows)
        else:
            for_chunks(0, rows, ROW_CHUNK, copy_rows)


def dense_rows_of(layouts, row_counts, shard_count):
    return max(
        round_up(rows * shard_count + round_up(rows, 16), 16)
        for layout, rows in zip(layouts, row_counts)
    )


def narrow_rows_of(layouts):
    return max(
        [16] + [2 * last for layout in layouts for first, last in narrow_ranges(layout)]
    )


def work_scratch(layouts, row_counts, shard_count):
    return [
        pltpu.VMEM((dense_rows_of(layouts, row_counts, shard_count), LANES), jnp.float32),
        pltpu.VMEM((3, round_up(narrow_rows_of(layouts), 16), LANES), jnp.float32),
    ]


def local_rows(flat_shard):
    shard_rows = flat_shard.shape[0] // LANES
    return jnp.pad(
        flat_shard.reshape(shard_rows, LANES).astype(jnp.bfloat16),
        ((0, round_up(shard_rows, 16) - shard_rows), (0, 0)),
    )


def weight_shapes(layout):
    shapes = []
    for entry_shape in layout:
        is_matrix = len(entry_shape) == 2 and entry_shape[0] > 9
        kind = jnp.bfloat16 if is_matrix else jnp.float32
        shape = entry_shape if len(entry_shape) == 2 else (1,) + entry_shape
        shapes.append(shaped(shape, kind))
    return shapes


def unpack_joined(gathered, layouts, row_counts):
    shard_count = gathered.shape[0]

    def kernel(gathered_ref, *refs):
        dense_ref, narrow_ref = refs[-2:]
        first_row = 0
        first_out = 0
        for layout, shard_rows in zip(layouts, row_counts):
            padded_rows = round_up(shard_rows, 16)

            def spread(index, carry, shard_rows=shard_rows, first=first_row, rows=padded_rows):
                dense_ref[pl.ds(index * shard_rows, rows), :] = gathered_ref[
                    index, first : first + rows, :
                ].astype(jnp.float32)
                return carry

            out_refs = refs[first_out : first_out + len(layout)]
            unpack_group(
                layout, shard_rows, shard_count, spread, out_refs, dense_ref, narrow_ref
            )
            first_row += padded_rows
            first_out += len(layout)

    results = pl.pallas_call(
        kernel,
        out_shape=[shape for layout in layouts for shape in weight_shapes(layout)],
        scratch_shapes=work_scratch(layouts, row_counts, shard_count),
        compiler_params=PARAMS,
        name="unpack_joined",
    )(gathered)
    groups = []
    for layout in layouts:
        groups.append(results[: len(layout)])
        results = results[len(layout) :]
    return groups


def swap(values, axis, bit):
    return lax.ppermute(
        values, axis, [(place, place ^ bit) for place in range(lax.axis_size(axis))]
    )


def bit_orders(count):
    bits = [1 << place for place in range(count.bit_length() - 1)]
    return [bits, bits[1::-1] + bits[2:]]


def device_place():
    return jnp.stack([lax.axis_index("dp"), lax.axis_index("fsdp")]).astype(jnp.int32)


PLACE_SPEC = pl.BlockSpec(memory_space=pltpu.SMEM)


def gather_halves(rows, orders, beside):
    half = rows.shape[0] // 32 * 16
    held = []
    for piece, order in zip((rows[:half], rows[half:]), orders):
        piece = piece[None]
        for bit in order:
            piece = jnp.concatenate([piece, swap(piece, "fsdp", bit)], axis=0)
        held.append(piece)
    *held, beside = lax.optimization_barrier((*held, beside))
    gathered = []
    for piece in held:
        pieces = [piece]
        for bit in bit_orders(lax.axis_size("dp"))[0]:
            pieces += [swap(piece, "dp", bit) for piece in pieces]
        gathered += pieces
    return gathered, beside


def unpack_halves(halves, place, layout, shard_rows, orders):
    chips = lax.axis_size("fsdp")
    cores = lax.axis_size("dp")
    half = halves[0].shape[1]

    def kernel(place_ref, *refs):
        half_refs = refs[: 2 * cores]
        out_refs = refs[2 * cores : -2]
        dense_ref, narrow_ref = refs[-2:]

        def spread(apart, carry):
            for number in range(2):
                position = 0
                for step, bit in enumerate(orders[number]):
                    position = position + ((apart // bit) % 2) * (1 << step)
                rows = half if number == 0 else shard_rows - half
                for core in range(cores):
                    shard = (core ^ place_ref[0]) * chips + (apart ^ place_ref[1])
                    piece = half_refs[number * cores + core][position].astype(jnp.float32)
                    dense_ref[pl.ds(shard * shard_rows + number * half, rows), :] = piece[:rows]
            return carry

        unpack_group(layout, shard_rows, chips, spread, out_refs, dense_ref, narrow_ref)

    vmem_spec = pl.BlockSpec(memory_space=pltpu.VMEM)
    return pl.pallas_call(
        kernel,
        in_specs=[PLACE_SPEC] + [vmem_spec] * len(halves),
        out_shape=weight_shapes(layout),
        scratch_shapes=work_scratch([layout], [shard_rows], chips * cores),
        compiler_params=PARAMS,
        name="unpack_halves",
    )(place, *halves)


def pack_group(layout, sources, in_refs, dense_ref, narrow_ref):
    places = layout_places(layout)
    used_rows = (places[-1][1] + math.prod(places[-1][0])) // LANES
    tail = dense_ref.shape[0] - used_rows
    dense_ref[pl.ds(used_rows, tail), :] = jnp.zeros((tail, LANES), jnp.float32)

    for (operand, first_row), (entry_shape, offset) in zip(sources, places):
        in_ref = in_refs[operand]
        rows = math.prod(entry_shape[:-1])
        cols = entry_shape[-1]
        narrow = is_narrow(entry_shape, offset)

        def copy_rows(start, amount):
            for part in range(-(-cols // LANES)):
                lanes = min(LANES, cols - part * LANES)
                piece = in_ref[pl.ds(first_row + start, amount), part * LANES : part * LANES + lanes]
                if narrow:
                    narrow_ref[part, pl.ds(offset // D3 + start, amount), 0:lanes] = piece
                else:
                    stride = cols // LANES
                    base = offset // LANES + part + start * stride
                    dense_ref[pl.ds(base, amount, stride=stride), :] = piece

        if rows < 32:
            copy_rows(0, rows)
        else:
            for_chunks(0, rows, ROW_CHUNK, copy_rows)

    if narrow and (offset // D3 + rows) % 2 == 1:
        beyond = offset // D3 + rows
        narrow_ref[:, beyond : beyond + 1, :] = jnp.zeros((3, 1, LANES), jnp.float32)

    def narrow_step(start, amount):
        even_rows = pl.ds(2 * start, amount, stride=2)
        odd_rows = pl.ds(2 * start + 1, amount, stride=2)
        low_lanes = lax.broadcasted_iota(jnp.int32, (amount, LANES), 1) < LANES // 2
        even = [narrow_ref[part, even_rows, :] for part in range(3)]
        odd = [pltpu.roll(narrow_ref[part, odd_rows, :], LANES // 2, 1) for part in range(3)]
        joined = [
            even[0],
            even[1],
            jnp.where(low_lanes, even[2], odd[0]),
            jnp.where(low_lanes, odd[0], odd[1]),
            jnp.where(low_lanes, odd[1], odd[2]),
        ]
        for part in range(5):
            dense_ref[pl.ds(5 * start + part, amount, stride=5), :] = joined[part]

    for first, last in narrow_ranges(layout):
        for_chunks(first, last, PAIR_CHUNK, narrow_step)


def pack_grads(place, groups, parts):
    chips = lax.axis_size("fsdp")
    shard_count = lax.axis_size("dp") * chips
    layouts = [group[2] for group in groups]
    row_counts = [group[3] for group in groups]
    counts = [len(group[0]) for group in groups]

    def kernel(place_ref, *refs):
        out_refs = refs[sum(counts) : sum(counts) + len(parts)]
        dense_ref, narrow_ref = refs[-2:]
        first = 0
        for number, (operands, sources, layout, shard_rows) in enumerate(groups):
            in_refs = refs[first : first + len(operands)]
            first += len(operands)
            pack_group(layout, sources, in_refs, dense_ref, narrow_ref)

            def cut(index, carry, number=number, shard_rows=shard_rows):
                for out_ref, (pieces, core, turned) in zip(out_refs, parts):
                    out_row = 0
                    for group, first_row, rows in pieces:
                        if group == number:
                            chip = index ^ place_ref[1] if turned else index
                            shard = (place_ref[0] ^ core) * chips + chip
                            out_ref[index, out_row : out_row + rows, :] = dense_ref[
                                pl.ds(shard * shard_rows + first_row, rows), :
                            ].astype(out_ref.dtype)
                        out_row += rows
                return carry

            lax.fori_loop(0, chips, cut, 0)

    vmem_spec = pl.BlockSpec(memory_space=pltpu.VMEM)
    return pl.pallas_call(
        kernel,
        in_specs=[PLACE_SPEC] + [vmem_spec] * sum(counts),
        out_shape=[
            shaped((chips, sum(piece[2] for piece in pieces), LANES), WIRE_TYPE)
            for pieces, core, turned in parts
        ],
        scratch_shapes=work_scratch(layouts, row_counts, shard_count),
        compiler_params=PARAMS,
        name="pack_grads",
    )(place, *[operand for group in groups for operand in group[0]])


def add_rounded(kept, received):
    return (kept.astype(jnp.float32) + received.astype(jnp.float32)).astype(WIRE_TYPE)


def flat_rows(rows, shard_rows):
    return rows[:shard_rows].astype(jnp.float32).reshape(-1)


def sum_cores(parts):
    parts = list(parts)
    while len(parts) > 1:
        half = len(parts) // 2
        parts = [
            add_rounded(kept, swap(sent, "dp", half))
            for kept, sent in zip(parts[:half], parts[half:])
        ]
    return parts[0]


def scatter_half(parts, order):
    held = sum_cores(parts)
    left = sorted(order, reverse=True)
    held = held.reshape([2] * len(left) + list(held.shape[1:]))
    for bit in order:
        axis = left.index(bit)
        left.remove(bit)
        kept = lax.index_in_dim(held, 0, axis, keepdims=False)
        sent = lax.index_in_dim(held, 1, axis, keepdims=False)
        held = add_rounded(kept, swap(sent, "fsdp", bit))
    return held


def sum_devices(value):
    for axis in AXES:
        for bit in bit_orders(lax.axis_size(axis))[0]:
            value = value + swap(value, axis, bit)
    return value


def dot(left, right):
    return lax.dot_general(
        left, right, (((1,), (0,)), ((), ())), preferred_element_type=jnp.float32
    )


def dot_nt(left, right):
    return lax.dot_general(
        left, right, (((1,), (1,)), ((), ())), preferred_element_type=jnp.float32
    )


def dot_tn(left, right):
    return lax.dot_general(
        left, right, (((0,), (0,)), ((), ())), preferred_element_type=jnp.float32
    )


def rows_sum(values):
    return jnp.sum(values, axis=0, keepdims=True)


def norm_parts(values):
    centred = values - jnp.mean(values, axis=-1, keepdims=True)
    spread = jnp.mean(centred * centred, axis=-1, keepdims=True)
    scale = lax.rsqrt(spread + 1e-06)
    return centred * scale, scale


def norm_grad(unit, scale, gain_row, gradient):
    inner = gradient * gain_row
    first = jnp.mean(inner, axis=-1, keepdims=True)
    second = jnp.mean(inner * unit, axis=-1, keepdims=True)
    return scale * (inner - first - unit * second)


def column_mask(rows, lanes, side, width):
    places = lax.broadcasted_iota(jnp.int32, (rows, lanes), 0)
    return (places & (width - 1)) < side


def softmax_rows(query, key, valid):
    scores = jnp.where(valid, dot_nt(query, key) * 0.125, -1e30)
    powers = jnp.exp(scores - jnp.max(scores, axis=-1, keepdims=True))
    return powers * (1.0 / jnp.sum(powers, axis=-1, keepdims=True))


def split_lanes(values):
    rows, channels = values.shape
    pieces = []
    for first in range(0, channels, LANES):
        piece = values[:, first : min(first + LANES, channels)]
        if piece.shape[1] < LANES:
            rest = jnp.zeros((rows, LANES - piece.shape[1]), values.dtype)
            piece = jnp.concatenate([piece, rest], axis=1)
        pieces.append(piece)
    return pieces


def join_lanes(pieces, channels):
    return jnp.concatenate(pieces, axis=1)[:, :channels]


def softmax_columns(query, key, valid):
    scores = jnp.where(valid, dot_nt(key, query) * 0.125, -1e30)
    powers = jnp.exp(scores - jnp.max(scores, axis=0, keepdims=True))
    return powers * (1.0 / rows_sum(powers))


def pair_place(width, part):
    return pl.ds((part // 2) * width + part % 2, width // 2, stride=2)


def pair_part(grid_ref, width, part, channels):
    pieces = []
    for index in range(grid_ref.shape[0]):
        piece = grid_ref[index, :, pair_place(width, part), :]
        pieces.append(piece.reshape(piece.shape[0] * piece.shape[1], LANES))
    return join_lanes(pieces, channels).astype(jnp.bfloat16)


def attend_kernel(channels, side, width, has_reduction, *refs):
    if has_reduction:
        (
            x_ref, valid_ref, gain_ref, bias_ref, wq_ref, bq_ref, wr_ref, br_ref, rgain_ref,
            rbias_ref, wp_ref, bv_ref, wo_ref, bo_ref, gain2_ref, bias2_ref,
            query_ref, pair_ref, mixed_ref, middle_ref, normed_ref, reduced_ref, padded_ref,
            grid_ref, inputs_ref,
        ) = refs
    else:
        (
            x_ref, valid_ref, gain_ref, bias_ref, wq_ref, bq_ref,
            wp_ref, bv_ref, wo_ref, bo_ref, gain2_ref, bias2_ref,
            query_ref, pair_ref, mixed_ref, middle_ref, normed_ref,
        ) = refs
    inputs = x_ref[0].astype(jnp.float32)
    if has_reduction:
        for row in range(side):
            first = row * width
            inputs_ref[first : first + side, :] = inputs[row * side : (row + 1) * side]
            inputs_ref[first + side : first + width, :] = jnp.zeros(
                (width - side, channels), jnp.float32
            )
        inputs = inputs_ref[...]
        padded_ref[0] = inputs.astype(jnp.bfloat16)
    unit, _ = norm_parts(inputs)
    normed = (unit * gain_ref[...] + bias_ref[...]).astype(jnp.bfloat16)
    query_ref[0] = (dot(normed, wq_ref[...]) + bq_ref[...]).astype(jnp.bfloat16)
    if has_reduction:
        for index, piece in enumerate(split_lanes(normed.astype(jnp.float32))):
            grid_ref[index] = piece.reshape(grid_ref.shape[1:])
        reduced = br_ref[...]
        for part in range(4):
            reduced = reduced + dot(
                pair_part(grid_ref, width, part, channels),
                wr_ref[part * channels : (part + 1) * channels, :],
            )
        reduced_ref[0] = reduced
        unit, _ = norm_parts(reduced)
        source = (unit * rgain_ref[...] + rbias_ref[...]).astype(jnp.bfloat16)
    else:
        source = normed
    pair_ref[0, :, :channels] = dot(source, wp_ref[:, :channels]).astype(jnp.bfloat16)
    pair_ref[0, :, channels:] = (dot(source, wp_ref[:, channels:]) + bv_ref[...]).astype(
        jnp.bfloat16
    )
    valid = valid_ref[0] > 0.5
    for head in range(channels // HEAD):
        lanes = slice(head * HEAD, (head + 1) * HEAD)
        value_lanes = slice(channels + head * HEAD, channels + (head + 1) * HEAD)
        query = query_ref[0, :, lanes]
        key = pair_ref[0, :, lanes]
        value = pair_ref[0, :, value_lanes]
        if has_reduction:
            chances = softmax_columns(query, key, valid).astype(jnp.bfloat16)
            mixed = dot_tn(chances, value)
        else:
            chances = softmax_rows(query, key, valid).astype(jnp.bfloat16)
            mixed = dot(chances, value)
        mixed_ref[0, :, lanes] = mixed.astype(jnp.bfloat16)
    middle = inputs + (dot(mixed_ref[0], wo_ref[...]) + bo_ref[...])
    middle_ref[0] = middle
    unit, _ = norm_parts(middle)
    normed_ref[0] = (unit * gain2_ref[...] + bias2_ref[...]).astype(jnp.bfloat16)


def whole(shape):
    return pl.BlockSpec(shape, lambda *place: (0,) * len(shape))


def image_block(array):
    return pl.BlockSpec((1,) + array.shape[1:], lambda image: (image,) + (0,) * (len(array.shape) - 1))


def shaped(shape, kind):
    return jax.ShapeDtypeStruct(shape, kind)


PARAMS = pltpu.CompilerParams(vmem_limit_bytes=61000 * 1024)


def attend_block(inputs, valid, weights, side, width):
    images, _, channels = inputs.shape
    tokens = side * width
    has_reduction = len(weights) == 14
    keys = valid.shape[2]
    if has_reduction:
        valid = valid.swapaxes(1, 2)
    outs = [
        shaped((images, tokens, channels), jnp.bfloat16),
        shaped((images, keys, 2 * channels), jnp.bfloat16),
        shaped((images, tokens, channels), jnp.bfloat16),
        shaped((images, tokens, channels), jnp.float32),
        shaped((images, tokens, channels), jnp.bfloat16),
    ]
    scratch = []
    if has_reduction:
        outs.append(shaped((images, keys, channels), jnp.float32))
        outs.append(shaped((images, tokens, channels), jnp.bfloat16))
        grid_shape = (-(-channels // LANES), tokens // (2 * width), 2 * width, LANES)
        scratch.append(pltpu.VMEM(grid_shape, jnp.float32))
        scratch.append(pltpu.VMEM((tokens, channels), jnp.float32))
    return pl.pallas_call(
        lambda *refs: attend_kernel(channels, side, width, has_reduction, *refs),
        grid=(images,),
        in_specs=[image_block(inputs), image_block(valid)] + [whole(w.shape) for w in weights],
        out_specs=[image_block(out) for out in outs],
        out_shape=outs,
        scratch_shapes=scratch,
        compiler_params=PARAMS,
        name="attend",
    )(inputs, valid, *weights)


def zero_edges(ref, side, width, columns):
    tokens = side * width
    lanes = ref.shape[1]
    ref[0:width, :] = jnp.zeros((width, lanes), jnp.float32)
    ref[width + tokens : 2 * width + tokens, :] = jnp.zeros((width, lanes), jnp.float32)
    if columns:
        for row in range(1, side + 1):
            ref[row * width + side : (row + 1) * width, :] = jnp.zeros(
                (width - side, lanes), jnp.float32
            )


def store_cells(ref, values, side, width):
    for row in range(side):
        ref[0, row * side : (row + 1) * side, :] = values[row * width : row * width + side]


def mix_kernel(side, width, lanes, dense, *refs):
    (
        normed_ref, middle_ref, we_ref, be_ref, kd_ref, bd_ref, wc_ref, bc_ref,
        out_ref, mixed_ref, slope_ref, pad_ref,
    ) = refs
    tokens = side * width
    units = we_ref.shape[1]
    pad_ref[width : width + tokens, :] = dot(normed_ref[0], we_ref[...]) + be_ref[...]
    zero_edges(pad_ref, side, width, True)

    def step(row, carry):
        start = pl.multiple_of(row * width, width)
        for first in range(0, units, lanes):
            block = slice(first, first + lanes)
            rows = [pad_ref[pl.ds(start + up * width, width), block] for up in range(3)]
            sums = [
                kd_ref[col : col + 1, block] * rows[0]
                + kd_ref[3 + col : 4 + col, block] * rows[1]
                + kd_ref[6 + col : 7 + col, block] * rows[2]
                for col in range(3)
            ]
            value = (
                sums[1]
                + pltpu.roll(sums[0], 1, 0)
                + pltpu.roll(sums[2], width - 1, 0)
                + bd_ref[:, block]
            )
            share = 0.5 + 0.5 * lax.erf(value * math.sqrt(0.5))
            bell = jnp.exp(value * value * -0.5) * (1.0 / math.sqrt(2.0 * math.pi))
            mixed_ref[0, pl.ds(start, width), block] = (value * share).astype(jnp.bfloat16)
            slope_ref[0, pl.ds(start, width), block] = (share + value * bell).astype(jnp.bfloat16)
        return carry

    lax.fori_loop(0, side, step, 0)
    result = middle_ref[0] + bc_ref[...] + dot(mixed_ref[0], wc_ref[...])
    if dense:
        store_cells(out_ref, result, side, width)
    else:
        out_ref[0] = result


def mix_block(normed, middle, weights, side, width, lanes, dense):
    images, tokens, channels = middle.shape
    units = weights[0].shape[1]
    outs = [
        shaped((images, side * side if dense else tokens, channels), jnp.float32),
        shaped((images, tokens, units), jnp.bfloat16),
        shaped((images, tokens, units), jnp.bfloat16),
    ]
    return pl.pallas_call(
        lambda *refs: mix_kernel(side, width, lanes, dense, *refs),
        grid=(images,),
        in_specs=[image_block(normed), image_block(middle)] + [whole(w.shape) for w in weights],
        out_specs=[image_block(out) for out in outs],
        out_shape=outs,
        scratch_shapes=[pltpu.VMEM((tokens + 2 * width, units), jnp.float32)],
        compiler_params=PARAMS,
        name="mix",
    )(normed, middle, *weights)


def mix_back_kernel(side, width, lanes, *refs):
    (
        normed_ref, grad_ref, mixed_ref, slope_ref, we_ref, be_ref, kd_ref, wc_ref,
        dnormed_ref, dwe_ref, dwc_ref, drows_ref, pad_ref, dpad_ref, dhid_ref,
    ) = refs
    tokens = side * width
    units = we_ref.shape[1]
    gradient = grad_ref[0].astype(jnp.bfloat16)
    pad_ref[width : width + tokens, :] = dot(normed_ref[0], we_ref[...]) + be_ref[...]
    dpad_ref[width : width + tokens, :] = dot_nt(gradient, wc_ref[...]) * slope_ref[0].astype(
        jnp.float32
    )
    zero_edges(pad_ref, side, width, True)
    zero_edges(dpad_ref, side, width, False)

    @pl.when(pl.program_id(0) == 0)
    def _():
        for ref in (drows_ref, dwe_ref, dwc_ref):
            ref[...] = jnp.zeros(ref.shape, jnp.float32)

    inside = column_mask(width, lanes, side, width)

    def fold(values):
        total = values[0:8]
        for start in range(8, width, 8):
            total = total + values[start : start + 8]
        return total

    for first in range(0, units, lanes):
        block = slice(first, first + lanes)

        def step(row, sums, block=block):
            start = pl.multiple_of(row * width, width)
            rows = [pad_ref[pl.ds(start + up * width, width), block] for up in range(3)]
            drows = [dpad_ref[pl.ds(start + up * width, width), block] for up in range(3)]
            turned = [
                pltpu.roll(drows[1], width - 1, 0),
                drows[1],
                pltpu.roll(drows[1], 1, 0),
            ]
            found = []
            for up in range(3):
                for col in range(3):
                    found.append(sums[3 * up + col] + fold(turned[col] * rows[up]))
            found.append(sums[9] + fold(drows[1]))
            parts = [
                kd_ref[col : col + 1, block] * drows[2]
                + kd_ref[3 + col : 4 + col, block] * drows[1]
                + kd_ref[6 + col : 7 + col, block] * drows[0]
                for col in range(3)
            ]
            value = parts[1] + pltpu.roll(parts[0], width - 1, 0) + pltpu.roll(parts[2], 1, 0)
            value = jnp.where(inside, value, 0.0)
            dhid_ref[pl.ds(start, width), block] = value.astype(jnp.bfloat16)
            found.append(sums[10] + fold(value))
            return tuple(found)

        zero = jnp.zeros((8, lanes), jnp.float32)
        totals = lax.fori_loop(0, side, step, (zero,) * 11, unroll=2)
        for index in range(11):
            drows_ref[index : index + 1, block] += rows_sum(totals[index])
    dhidden = dhid_ref[...]
    dwe_ref[...] += dot_tn(normed_ref[0], dhidden)
    dwc_ref[...] += dot_tn(mixed_ref[0], gradient)
    dnormed_ref[0] = dot_nt(dhidden, we_ref[...])


def mix_back(normed, gradient, mixed, slope, weights, side, width, lanes):
    we, be, kd, bd, wc, bc = weights
    images, tokens, channels = normed.shape
    units = we.shape[1]
    operands = [normed, gradient, mixed, slope]
    used = [we, be, kd, wc]
    outs = [
        shaped((images, tokens, channels), jnp.float32),
        shaped((channels, units), jnp.float32),
        shaped((units, channels), jnp.float32),
        shaped((16, units), jnp.float32),
    ]
    return pl.pallas_call(
        lambda *refs: mix_back_kernel(side, width, lanes, *refs),
        grid=(images,),
        in_specs=[image_block(op) for op in operands] + [whole(u.shape) for u in used],
        out_specs=[image_block(outs[0])] + [whole(out.shape) for out in outs[1:]],
        out_shape=outs,
        scratch_shapes=[
            pltpu.VMEM((tokens + 2 * width, units), jnp.float32),
            pltpu.VMEM((tokens + 2 * width, units), jnp.float32),
            pltpu.VMEM((tokens, units), jnp.bfloat16),
        ],
        compiler_params=PARAMS,
        name="mix_back",
    )(*operands, *used)


def attend_back_kernel(channels, side, width, has_reduction, *refs):
    if has_reduction:
        (
            x_ref, valid_ref, grad_ref, dnormed_ref, middle_ref, query_ref, pair_ref, mixed_ref,
            reduced_ref, gain_ref, bias_ref, wq_ref, wr_ref, rgain_ref, rbias_ref, wp_ref, wo_ref,
            gain2_ref,
            dx_ref, dwq_ref, dwp_ref, dwo_ref, vec_ref, dwr_ref,
            dquery_ref, dpair_ref, dmiddle_ref, grid_ref, dgrid_ref,
        ) = refs
    else:
        (
            x_ref, valid_ref, grad_ref, dnormed_ref, middle_ref, query_ref, pair_ref, mixed_ref,
            gain_ref, bias_ref, wq_ref, wp_ref, wo_ref, gain2_ref,
            dx_ref, dwq_ref, dwp_ref, dwo_ref, vec_ref,
            dquery_ref, dpair_ref, dmiddle_ref,
        ) = refs

    @pl.when(pl.program_id(0) == 0)
    def _():
        sums = [dwq_ref, dwp_ref, dwo_ref, vec_ref] + ([dwr_ref] if has_reduction else [])
        for ref in sums:
            ref[...] = jnp.zeros(ref.shape, jnp.float32)

    def add_row(index, row):
        vec_ref[index : index + 1, :] += row

    gradient = grad_ref[0].astype(jnp.float32)
    add_row(0, rows_sum(gradient.astype(jnp.bfloat16).astype(jnp.float32)))
    dnormed = dnormed_ref[0]
    unit, scale = norm_parts(middle_ref[0])
    add_row(1, rows_sum(dnormed * unit))
    add_row(2, rows_sum(dnormed))
    dmiddle = gradient + norm_grad(unit, scale, gain2_ref[...], dnormed)
    dmiddle_ref[...] = dmiddle
    doutput = dmiddle.astype(jnp.bfloat16)
    add_row(3, rows_sum(doutput.astype(jnp.float32)))
    dwo_ref[...] += dot_tn(mixed_ref[0], doutput)
    dmixed = dot_nt(doutput, wo_ref[...]).astype(jnp.bfloat16)
    valid = valid_ref[0] > 0.5
    for head in range(channels // HEAD):
        lanes = slice(head * HEAD, (head + 1) * HEAD)
        value_lanes = slice(channels + head * HEAD, channels + (head + 1) * HEAD)
        query = query_ref[0, :, lanes]
        key = pair_ref[0, :, lanes]
        chances = softmax_columns(query, key, valid)
        dhead = dmixed[:, lanes]
        dchances = dot_nt(pair_ref[0, :, value_lanes], dhead)
        dpair_ref[:, value_lanes] = dot(chances.astype(jnp.bfloat16), dhead).astype(jnp.bfloat16)
        weighted = chances * dchances
        dscores = (weighted - chances * rows_sum(weighted)).astype(jnp.bfloat16)
        dquery_ref[:, lanes] = (dot_tn(dscores, key) * 0.125).astype(jnp.bfloat16)
        dpair_ref[:, lanes] = (dot(dscores, query) * 0.125).astype(jnp.bfloat16)
    dquery = dquery_ref[...]
    dpair = dpair_ref[...]
    unit, scale = norm_parts(x_ref[0].astype(jnp.float32))
    normed = (unit * gain_ref[...] + bias_ref[...]).astype(jnp.bfloat16)
    add_row(4, rows_sum(dquery.astype(jnp.float32)))
    add_row(5, rows_sum(dpair[:, channels:].astype(jnp.float32)))
    dwq_ref[...] += dot_tn(normed, dquery)
    total = dot_nt(dquery, wq_ref[...])
    dsource = dot_nt(dpair, wp_ref[...])
    if has_reduction:
        runit, rscale = norm_parts(reduced_ref[0])
        source = (runit * rgain_ref[...] + rbias_ref[...]).astype(jnp.bfloat16)
        dwp_ref[...] += dot_tn(source, dpair)
        add_row(8, rows_sum(dsource * runit))
        add_row(9, rows_sum(dsource))
        dreduced = norm_grad(runit, rscale, rgain_ref[...], dsource).astype(jnp.bfloat16)
        add_row(10, rows_sum(dreduced.astype(jnp.float32)))
        for index, piece in enumerate(split_lanes(normed.astype(jnp.float32))):
            grid_ref[index] = piece.reshape(grid_ref.shape[1:])
        for index, piece in enumerate(split_lanes(total)):
            dgrid_ref[index] = piece.reshape(dgrid_ref.shape[1:])
        for part in range(4):
            rows = slice(part * channels, (part + 1) * channels)
            dwr_ref[rows, :] += dot_tn(pair_part(grid_ref, width, part, channels), dreduced)
            for index, piece in enumerate(split_lanes(dot_nt(dreduced, wr_ref[rows, :]))):
                dgrid_ref[index, :, pair_place(width, part), :] += piece.reshape(
                    dgrid_ref.shape[1], width // 2, LANES
                )
        total = join_lanes(
            [dgrid_ref[index].reshape(total.shape[0], LANES) for index in range(dgrid_ref.shape[0])],
            channels,
        )
    else:
        dwp_ref[...] += dot_tn(normed, dpair)
        total = total + dsource
    add_row(6, rows_sum(total * unit))
    add_row(7, rows_sum(total))
    result = dmiddle_ref[...] + norm_grad(unit, scale, gain_ref[...], total)
    if has_reduction:
        store_cells(dx_ref, result, side, width)
    else:
        dx_ref[0] = result


def attend_back(inputs, valid, gradient, dnormed, saved, weights, side, width):
    query, pair, mixed, middle, normed = saved[:5]
    images, tokens, channels = middle.shape
    has_reduction = len(saved) > 5
    keys = valid.shape[2]
    operands = [inputs, valid.swapaxes(1, 2), gradient, dnormed, middle, query, pair, mixed]
    outs = [
        shaped((images, side * side if has_reduction else tokens, channels), jnp.float32),
        shaped((channels, channels), jnp.float32),
        shaped((channels, 2 * channels), jnp.float32),
        shaped((channels, channels), jnp.float32),
        shaped((16, channels), jnp.float32),
    ]
    scratch = [
        pltpu.VMEM((tokens, channels), jnp.bfloat16),
        pltpu.VMEM((keys, 2 * channels), jnp.bfloat16),
        pltpu.VMEM((tokens, channels), jnp.float32),
    ]
    if has_reduction:
        gain, bias, wq, bq, wr, br, rgain, rbias, wp, bv, wo, bo, gain2, bias2 = weights
        used = [gain, bias, wq, wr, rgain, rbias, wp, wo, gain2]
        operands.append(saved[5])
        outs.append(shaped((4 * channels, channels), jnp.float32))
        grid_shape = (-(-channels // LANES), tokens // (2 * width), 2 * width, LANES)
        scratch += [pltpu.VMEM(grid_shape, jnp.float32), pltpu.VMEM(grid_shape, jnp.float32)]
    else:
        gain, bias, wq, bq, wp, bv, wo, bo, gain2, bias2 = weights
        used = [gain, bias, wq, wp, wo, gain2]
    return pl.pallas_call(
        lambda *refs: attend_back_kernel(channels, side, width, has_reduction, *refs),
        grid=(images,),
        in_specs=[image_block(op) for op in operands] + [whole(w.shape) for w in used],
        out_specs=[image_block(outs[0])] + [whole(out.shape) for out in outs[1:]],
        out_shape=outs,
        scratch_shapes=scratch,
        compiler_params=PARAMS,
        name="attend_back",
    )(*operands, *used)


def tap_place(width, tap, row):
    first = LEAD + (tap // 3) * width + tap % 3 - 1
    return pl.ds(first + 2 * width * row, width // 2, stride=2)


def load_tap(grid_ref, side, width, tap, channels):
    pieces = []
    for index in range(grid_ref.shape[0]):
        rows = [grid_ref[index, tap_place(width, tap, row), :] for row in range(side // 2)]
        pieces.append(jnp.concatenate(rows, axis=0))
    return join_lanes(pieces, channels).astype(jnp.bfloat16)


def fill_grid(grid_ref, values, width):
    rows = grid_ref.shape[1]
    first = LEAD + width
    last = first + values.shape[0]
    for index, piece in enumerate(split_lanes(values)):
        grid_ref[index, 0:first, :] = jnp.zeros((first, LANES), jnp.float32)
        grid_ref[index, first:last, :] = piece
        grid_ref[index, last:rows, :] = jnp.zeros((rows - last, LANES), jnp.float32)


LEAD = 8


def embed_kernel(side, width, *refs):
    x_ref, gain_ref, bias_ref, w_ref, b_ref, pgain_ref, pbias_ref = refs[:7]
    out_ref, patch_ref, grid_ref = refs[7:]
    tokens, channels = x_ref.shape[1:]
    unit, _ = norm_parts(x_ref[0])
    normed = (unit * gain_ref[...] + bias_ref[...]).astype(jnp.bfloat16).astype(jnp.float32)
    inside = column_mask(tokens, channels, side, width)
    fill_grid(grid_ref, jnp.where(inside, normed, 0.0), width)
    patch = b_ref[...]
    for tap in range(9):
        patch = patch + dot(
            load_tap(grid_ref, side, width, tap, channels),
            w_ref[tap * channels : (tap + 1) * channels, :]
        )
    patch_ref[0] = patch
    unit, _ = norm_parts(patch)
    out_ref[0] = unit * pgain_ref[...] + pbias_ref[...]


def embed_block(inputs, weights, side, width):
    images, tokens, channels = inputs.shape
    units = weights[2].shape[1]
    outs = [shaped((images, tokens // 4, units), jnp.float32)] * 2
    return pl.pallas_call(
        lambda *refs: embed_kernel(side, width, *refs),
        grid=(images,),
        in_specs=[image_block(inputs)] + [whole(w.shape) for w in weights],
        out_specs=[image_block(out) for out in outs],
        out_shape=outs,
        scratch_shapes=[pltpu.VMEM((-(-channels // LANES), LEAD + (side + 3) * width, LANES), jnp.float32)],
        compiler_params=PARAMS,
        name="embed",
    )(inputs, *weights)


def embed_back_kernel(side, width, *refs):
    x_ref, grad_ref, patch_ref, gain_ref, bias_ref, w_ref, pgain_ref = refs[:7]
    dx_ref, dw_ref, vec_ref, pvec_ref, grid_ref, dgrid_ref = refs[7:]
    tokens, channels = x_ref.shape[1:]

    @pl.when(pl.program_id(0) == 0)
    def _():
        for ref in (dw_ref, vec_ref, pvec_ref):
            ref[...] = jnp.zeros(ref.shape, jnp.float32)

    gradient = grad_ref[0]
    punit, pscale = norm_parts(patch_ref[0])
    pvec_ref[0:1, :] += rows_sum(gradient * punit)
    pvec_ref[1:2, :] += rows_sum(gradient)
    dpatch = norm_grad(punit, pscale, pgain_ref[...], gradient).astype(jnp.bfloat16)
    pvec_ref[2:3, :] += rows_sum(dpatch.astype(jnp.float32))
    unit, scale = norm_parts(x_ref[0])
    normed = (unit * gain_ref[...] + bias_ref[...]).astype(jnp.bfloat16).astype(jnp.float32)
    inside = column_mask(tokens, channels, side, width)
    fill_grid(grid_ref, jnp.where(inside, normed, 0.0), width)
    dgrid_ref[...] = jnp.zeros(dgrid_ref.shape, jnp.float32)
    half = width // 2
    for tap in range(9):
        rows = slice(tap * channels, (tap + 1) * channels)
        dw_ref[rows, :] += dot_tn(load_tap(grid_ref, side, width, tap, channels), dpatch)
        for index, piece in enumerate(split_lanes(dot_nt(dpatch, w_ref[rows, :]))):
            for row in range(side // 2):
                dgrid_ref[index, tap_place(width, tap, row), :] += piece[
                    row * half : (row + 1) * half, :
                ]
    first = LEAD + width
    pieces = [dgrid_ref[index, first : first + tokens, :] for index in range(dgrid_ref.shape[0])]
    total = jnp.where(inside, join_lanes(pieces, channels), 0.0)
    vec_ref[0:1, :] += rows_sum(total * unit)
    vec_ref[1:2, :] += rows_sum(total)
    dx_ref[0] = norm_grad(unit, scale, gain_ref[...], total)


def embed_back(inputs, gradient, patch, weights, side, width):
    gain, bias, w, b, pgain, pbias = weights
    images, tokens, channels = inputs.shape
    units = w.shape[1]
    outs = [
        shaped(inputs.shape, jnp.float32),
        shaped(w.shape, jnp.float32),
        shaped((8, channels), jnp.float32),
        shaped((8, units), jnp.float32),
    ]
    operands = [inputs, gradient, patch]
    used = [gain, bias, w, pgain]
    grid_scratch = pltpu.VMEM((-(-channels // LANES), LEAD + (side + 3) * width, LANES), jnp.float32)
    return pl.pallas_call(
        lambda *refs: embed_back_kernel(side, width, *refs),
        grid=(images,),
        in_specs=[image_block(op) for op in operands] + [whole(u.shape) for u in used],
        out_specs=[image_block(outs[0])] + [whole(out.shape) for out in outs[1:]],
        out_shape=outs,
        scratch_shapes=[grid_scratch, grid_scratch],
        compiler_params=PARAMS,
        name="embed_back",
    )(*operands, *used)


def to_grid(values, side, width):
    images, tokens, channels = values.shape
    grid = values.reshape(images, side, side, channels)
    grid = jnp.pad(grid, ((0, 0), (0, 0), (0, width - side), (0, 0)))
    return grid.reshape(images, side * width, channels)


def key_mask(row_counts, col_counts, side, width):
    places = jnp.arange(side * width, dtype=jnp.int32)
    valid = ((places // width)[None, :] < row_counts[:, None]) & (
        (places % width)[None, :] < col_counts[:, None]
    )
    return valid.astype(jnp.float32)[:, None, :]


def block_sources(has_reduction):
    reduction = [(7, 0), (3, 10), (3, 8), (3, 9)] if has_reduction else []
    return (
        [(3, 6), (3, 7), (0, 0), (3, 4)]
        + reduction
        + [(1, 0), (3, 5), (2, 0), (3, 3), (3, 1), (3, 2)]
        + [(4, 0), (6, 10), (6, 0), (6, 9), (5, 0), (3, 0)]
    )


EMBED_SOURCES = [(1, 0), (1, 1), (0, 0), (2, 2), (2, 0), (2, 1)]


def adamw_update(weights, mean_old, square_old, gradient, clip_factor, rate_value, fix_one):
    clipped = gradient * clip_factor
    mean_new = 0.5 * mean_old + 0.5 * clipped
    square_new = 0.5 * square_old + 0.5 * clipped * clipped
    updated = weights * (1.0 - rate_value * 0.05) - rate_value * (mean_new / fix_one) / (
        jnp.sqrt(square_new / fix_one) + 1e-08
    )
    return (updated, mean_new, square_new)


def shards(
    features,
    key_rows,
    key_cols,
    out_grad,
    lower_weights,
    lower_mean,
    lower_square,
    embed_weights,
    embed_mean,
    embed_square,
    upper_weights,
    upper_mean,
    upper_square,
    learn_rate,
):
    side, half = GRID, GRID // 2
    width = round_up(side, 32)
    half_width = width // 2
    key_valid = key_mask(key_rows, key_cols, half, half_width)
    cores = lax.axis_size("dp")
    orders = bit_orders(lax.axis_size("fsdp"))
    place = device_place()
    lower_rows, embed_rows, upper_rows = (
        flat.shape[0] // LANES for flat in (lower_weights, embed_weights, upper_weights)
    )
    rest_local = jnp.concatenate([local_rows(embed_weights), local_rows(upper_weights)], axis=0)
    lower_halves, (rest_local, grad_in) = gather_halves(
        local_rows(lower_weights),
        [order[2:] + order[:2] for order in orders],
        (rest_local, to_grid(out_grad, half, half_width)),
    )
    rest = lax.all_gather(rest_local, AXES, axis=0, tiled=False)
    lower = unpack_halves(
        lower_halves, place, LOWER_LAYOUT, lower_rows, [order[2:] + order[:2] for order in orders]
    )
    embed, upper = unpack_joined(rest, [EMBED_LAYOUT, UPPER_LAYOUT], [embed_rows, upper_rows])

    lower_saved = attend_block(features, key_valid, lower[:14], side, width)
    three_in = lower_saved[6]
    section_three, lower_mixed, lower_slope = mix_block(
        lower_saved[4], lower_saved[3], lower[14:], side, width, 256, False
    )
    section_four, patch = embed_block(section_three, embed, side, width)
    upper_saved = attend_block(section_four, key_valid, upper[:10], half, half_width)
    block_out, upper_mixed, upper_slope = mix_block(
        upper_saved[4], upper_saved[3], upper[10:], half, half_width, 256, True
    )

    def back(inputs, gradient, saved, mixed, slope, weights, first, side, width, lanes):
        dnormed, dwe, dwc, drows = mix_back(
            saved[4], gradient, mixed, slope, weights[first:], side, width, lanes
        )
        dx, dwq, dwp, dwo, vec, *rest = attend_back(
            inputs, key_valid, gradient, dnormed, saved, weights[:first], side, width
        )
        return dx, [dwq, dwp, dwo, vec, dwe, dwc, drows] + rest

    four_grad, upper_found = back(
        section_four, grad_in, upper_saved, upper_mixed, upper_slope, upper, 10, half, half_width, 256
    )
    upper_wire = pack_grads(
        place,
        [(upper_found, block_sources(False), UPPER_LAYOUT, upper_rows)],
        [([(0, 0, round_up(upper_rows, 16))], core, False) for core in range(cores)],
    )
    *upper_wire, four_grad = lax.optimization_barrier((*upper_wire, four_grad))
    three_grad, *embed_found = embed_back(section_three, four_grad, patch, embed, side, width)
    embed_wire = pack_grads(
        place,
        [(embed_found, EMBED_SOURCES, EMBED_LAYOUT, embed_rows)],
        [([(0, 0, round_up(embed_rows, 16))], core, False) for core in range(cores)],
    )
    rest_sum = jnp.concatenate([sum_cores(embed_wire), sum_cores(upper_wire)], axis=1)
    rest_sum, three_grad = lax.optimization_barrier((rest_sum, three_grad))
    rest_grad = lax.psum_scatter(rest_sum, "fsdp", scatter_dimension=0, tiled=False)
    input_grad, lower_found = back(
        three_in, three_grad, lower_saved, lower_mixed, lower_slope, lower, 14, side, width, 256
    )
    padded_rows = round_up(lower_rows, 16)
    half_rows = padded_rows // 32 * 16
    parts = []
    for first, rows in ((0, half_rows), (half_rows, padded_rows - half_rows)):
        parts += [([(0, first, rows)], core, True) for core in range(cores)]
    wire = pack_grads(
        place, [(lower_found, block_sources(True), LOWER_LAYOUT, lower_rows)], parts
    )
    lower_sum = jnp.concatenate(
        [scatter_half(wire[:cores], orders[0]), scatter_half(wire[cores:], orders[1])], axis=0
    )
    lower_grad = flat_rows(lower_sum, lower_rows)
    embed_grad = flat_rows(rest_grad, embed_rows)
    upper_grad = flat_rows(rest_grad[round_up(embed_rows, 16) :], upper_rows)
    local_squares = (
        jnp.sum(lower_grad * lower_grad)
        + jnp.sum(embed_grad * embed_grad)
        + jnp.sum(upper_grad * upper_grad)
    )
    squares = sum_devices(local_squares.reshape(1, 1))[0, 0]
    grad_norm = jnp.sqrt(squares)
    clip_factor = jnp.minimum(1.0, 5.0 / (grad_norm + 1e-06))
    rate_value = learn_rate[0]
    fix_one = 1.0 - 0.5**ADAM_STEP
    lower_new, lower_mean_new, lower_square_new = adamw_update(
        lower_weights, lower_mean, lower_square, lower_grad, clip_factor, rate_value, fix_one
    )
    embed_new, embed_mean_new, embed_square_new = adamw_update(
        embed_weights, embed_mean, embed_square, embed_grad, clip_factor, rate_value, fix_one
    )
    upper_new, upper_mean_new, upper_square_new = adamw_update(
        upper_weights, upper_mean, upper_square, upper_grad, clip_factor, rate_value, fix_one
    )
    return (
        block_out,
        input_grad,
        grad_norm.reshape(1),
        lower_grad,
        lower_new,
        lower_mean_new,
        lower_square_new,
        lower_new.astype(jnp.bfloat16),
        embed_grad,
        embed_new,
        embed_mean_new,
        embed_square_new,
        embed_new.astype(jnp.bfloat16),
        upper_grad,
        upper_new,
        upper_mean_new,
        upper_square_new,
        upper_new.astype(jnp.bfloat16),
    )


AXES = ("dp", "fsdp")
TOKENS = P(AXES, None, None)
FLAT = P(AXES)


def solution(mesh):
    return jax.shard_map(
        shards,
        mesh=mesh,
        in_specs=(
            TOKENS,
            FLAT,
            FLAT,
            TOKENS,
            FLAT,
            FLAT,
            FLAT,
            FLAT,
            FLAT,
            FLAT,
            FLAT,
            FLAT,
            FLAT,
            P(),
        ),
        out_specs=(
            TOKENS,
            TOKENS,
            P(),
            FLAT,
            FLAT,
            FLAT,
            FLAT,
            FLAT,
            FLAT,
            FLAT,
            FLAT,
            FLAT,
            FLAT,
            FLAT,
            FLAT,
            FLAT,
            FLAT,
            FLAT,
        ),
        check_vma=False,
    )
```

```python
import math

import jax
import jax.numpy as jnp
from jax import lax
from jax.experimental import pallas as pl
from jax.experimental.pallas import tpu as pltpu
from jax.sharding import PartitionSpec as P

D3 = 320
D4 = 512
HID3 = 1280
HID4 = 2048
HEAD = 64
GRID = 28
ADAM_STEP = 2
WIRE_TYPE = jnp.bfloat16


def block_layout(channels, units, has_reduction):
    row = (channels,)
    reduction = [(4 * channels, channels), row, row, row] if has_reduction else []
    return (
        [row, row, (channels, channels), row]
        + reduction
        + [(channels, 2 * channels), row, (channels, channels), row, row, row]
        + [(channels, units), (units,), (9, units), (units,), (units, channels), row]
    )


LOWER_LAYOUT = block_layout(D3, HID3, True)
UPPER_LAYOUT = block_layout(D4, HID4, False)
EMBED_LAYOUT = [(D3,), (D3,), (9 * D3, D4), (D4,), (D4,), (D4,)]


LANES = 128
PAIR_CHUNK = 64
ROW_CHUNK = 160


def layout_places(layout):
    places = []
    offset = 0
    for entry_shape in layout:
        places.append((entry_shape, offset))
        offset = offset + math.prod(entry_shape)
    return places


def is_narrow(entry_shape, offset):
    return entry_shape[-1] % LANES != 0 or offset % LANES != 0


def narrow_ranges(layout):
    ranges = []
    for entry_shape, offset in layout_places(layout):
        if not is_narrow(entry_shape, offset):
            continue
        first = offset // D3
        last = first + math.prod(entry_shape) // D3
        if ranges and ranges[-1][1] == first:
            ranges[-1] = (ranges[-1][0], last)
        else:
            ranges.append((first, last))
    return [(first // 2, (last + 1) // 2) for first, last in ranges]


def round_up(amount, unit):
    return (amount + unit - 1) // unit * unit


def for_chunks(first, last, chunk, step):
    full = (last - first) // chunk

    def body(index, carry):
        step(first + index * chunk, chunk)
        return carry

    if full > 0:
        lax.fori_loop(0, full, body, 0)
    rest = (last - first) - full * chunk
    if rest > 0:
        step(first + full * chunk, rest)


def unpack_group(layout, shard_rows, shard_count, spread, out_refs, dense_ref, narrow_ref):
    lax.fori_loop(0, shard_count, spread, 0)

    def narrow_step(start, amount):
        parts = [
            dense_ref[pl.ds(5 * start + part, amount, stride=5), :] for part in range(5)
        ]
        low_lanes = lax.broadcasted_iota(jnp.int32, (amount, LANES), 1) < LANES // 2
        turned = [pltpu.roll(part, LANES // 2, 1) for part in parts[2:]]
        even_rows = pl.ds(2 * start, amount, stride=2)
        odd_rows = pl.ds(2 * start + 1, amount, stride=2)
        for part in range(3):
            narrow_ref[part, even_rows, :] = parts[part]
        narrow_ref[0, odd_rows, :] = jnp.where(low_lanes, turned[0], turned[1])
        narrow_ref[1, odd_rows, :] = jnp.where(low_lanes, turned[1], turned[2])
        narrow_ref[2, odd_rows, :] = turned[2]

    for first, last in narrow_ranges(layout):
        for_chunks(first, last, PAIR_CHUNK, narrow_step)

    for out_ref, (entry_shape, offset) in zip(out_refs, layout_places(layout)):
        rows = math.prod(entry_shape[:-1])
        cols = entry_shape[-1]
        narrow = is_narrow(entry_shape, offset)

        def copy_rows(start, amount):
            for part in range(-(-cols // LANES)):
                lanes = min(LANES, cols - part * LANES)
                if narrow:
                    piece = narrow_ref[part, pl.ds(offset // D3 + start, amount), :]
                else:
                    stride = cols // LANES
                    base = offset // LANES + part + start * stride
                    piece = dense_ref[pl.ds(base, amount, stride=stride), :]
                out_ref[pl.ds(start, amount), part * LANES : part * LANES + lanes] = piece[
                    :, :lanes
                ].astype(out_ref.dtype)

        if rows < 32:
            copy_rows(0, rows)
        else:
            for_chunks(0, rows, ROW_CHUNK, copy_rows)


def dense_rows_of(layouts, row_counts, shard_count):
    return max(
        round_up(rows * shard_count + round_up(rows, 16), 16)
        for layout, rows in zip(layouts, row_counts)
    )


def narrow_rows_of(layouts):
    return max(
        [16] + [2 * last for layout in layouts for first, last in narrow_ranges(layout)]
    )


def work_scratch(layouts, row_counts, shard_count):
    return [
        pltpu.VMEM((dense_rows_of(layouts, row_counts, shard_count), LANES), jnp.float32),
        pltpu.VMEM((3, round_up(narrow_rows_of(layouts), 16), LANES), jnp.float32),
    ]


def local_rows(flat_shard):
    shard_rows = flat_shard.shape[0] // LANES
    return jnp.pad(
        flat_shard.reshape(shard_rows, LANES).astype(jnp.bfloat16),
        ((0, round_up(shard_rows, 16) - shard_rows), (0, 0)),
    )


def weight_shapes(layout):
    shapes = []
    for entry_shape in layout:
        is_matrix = len(entry_shape) == 2 and entry_shape[0] > 9
        kind = jnp.bfloat16 if is_matrix else jnp.float32
        shape = entry_shape if len(entry_shape) == 2 else (1,) + entry_shape
        shapes.append(shaped(shape, kind))
    return shapes


def unpack_joined(gathered, layouts, row_counts):
    shard_count = gathered.shape[0]

    def kernel(gathered_ref, *refs):
        dense_ref, narrow_ref = refs[-2:]
        first_row = 0
        first_out = 0
        for layout, shard_rows in zip(layouts, row_counts):
            padded_rows = round_up(shard_rows, 16)

            def spread(index, carry, shard_rows=shard_rows, first=first_row, rows=padded_rows):
                dense_ref[pl.ds(index * shard_rows, rows), :] = gathered_ref[
                    index, first : first + rows, :
                ].astype(jnp.float32)
                return carry

            out_refs = refs[first_out : first_out + len(layout)]
            unpack_group(
                layout, shard_rows, shard_count, spread, out_refs, dense_ref, narrow_ref
            )
            first_row += padded_rows
            first_out += len(layout)

    results = pl.pallas_call(
        kernel,
        out_shape=[shape for layout in layouts for shape in weight_shapes(layout)],
        scratch_shapes=work_scratch(layouts, row_counts, shard_count),
        compiler_params=PARAMS,
        name="unpack_joined",
    )(gathered)
    groups = []
    for layout in layouts:
        groups.append(results[: len(layout)])
        results = results[len(layout) :]
    return groups


def swap(values, axis, bit):
    return lax.ppermute(
        values, axis, [(place, place ^ bit) for place in range(lax.axis_size(axis))]
    )


def bit_orders(count):
    bits = [1 << place for place in range(count.bit_length() - 1)]
    return [bits, bits[1::-1] + bits[2:]]


def device_place():
    return jnp.stack([lax.axis_index("dp"), lax.axis_index("fsdp")]).astype(jnp.int32)


PLACE_SPEC = pl.BlockSpec(memory_space=pltpu.SMEM)


def gather_halves(rows, orders, beside):
    half = rows.shape[0] // 32 * 16
    held = []
    for piece, order in zip((rows[:half], rows[half:]), orders):
        piece = piece[None]
        for bit in order:
            piece = jnp.concatenate([piece, swap(piece, "fsdp", bit)], axis=0)
        held.append(piece)
    *held, beside = lax.optimization_barrier((*held, beside))
    gathered = []
    for piece in held:
        pieces = [piece]
        for bit in bit_orders(lax.axis_size("dp"))[0]:
            pieces += [swap(piece, "dp", bit) for piece in pieces]
        gathered += pieces
    return gathered, beside


def unpack_halves(halves, place, layout, shard_rows, orders):
    chips = lax.axis_size("fsdp")
    cores = lax.axis_size("dp")
    half = halves[0].shape[1]

    def kernel(place_ref, *refs):
        half_refs = refs[: 2 * cores]
        out_refs = refs[2 * cores : -2]
        dense_ref, narrow_ref = refs[-2:]

        def spread(apart, carry):
            for number in range(2):
                position = 0
                for step, bit in enumerate(orders[number]):
                    position = position + ((apart // bit) % 2) * (1 << step)
                rows = half if number == 0 else shard_rows - half
                for core in range(cores):
                    shard = (core ^ place_ref[0]) * chips + (apart ^ place_ref[1])
                    piece = half_refs[number * cores + core][position].astype(jnp.float32)
                    dense_ref[pl.ds(shard * shard_rows + number * half, rows), :] = piece[:rows]
            return carry

        unpack_group(layout, shard_rows, chips, spread, out_refs, dense_ref, narrow_ref)

    vmem_spec = pl.BlockSpec(memory_space=pltpu.VMEM)
    return pl.pallas_call(
        kernel,
        in_specs=[PLACE_SPEC] + [vmem_spec] * len(halves),
        out_shape=weight_shapes(layout),
        scratch_shapes=work_scratch([layout], [shard_rows], chips * cores),
        compiler_params=PARAMS,
        name="unpack_halves",
    )(place, *halves)


def pack_group(layout, sources, in_refs, dense_ref, narrow_ref):
    places = layout_places(layout)
    used_rows = (places[-1][1] + math.prod(places[-1][0])) // LANES
    tail = dense_ref.shape[0] - used_rows
    dense_ref[pl.ds(used_rows, tail), :] = jnp.zeros((tail, LANES), jnp.float32)

    for (operand, first_row), (entry_shape, offset) in zip(sources, places):
        in_ref = in_refs[operand]
        rows = math.prod(entry_shape[:-1])
        cols = entry_shape[-1]
        narrow = is_narrow(entry_shape, offset)

        def copy_rows(start, amount):
            for part in range(-(-cols // LANES)):
                lanes = min(LANES, cols - part * LANES)
                piece = in_ref[pl.ds(first_row + start, amount), part * LANES : part * LANES + lanes]
                if narrow:
                    narrow_ref[part, pl.ds(offset // D3 + start, amount), 0:lanes] = piece
                else:
                    stride = cols // LANES
                    base = offset // LANES + part + start * stride
                    dense_ref[pl.ds(base, amount, stride=stride), :] = piece

        if rows < 32:
            copy_rows(0, rows)
        else:
            for_chunks(0, rows, ROW_CHUNK, copy_rows)

    if narrow and (offset // D3 + rows) % 2 == 1:
        beyond = offset // D3 + rows
        narrow_ref[:, beyond : beyond + 1, :] = jnp.zeros((3, 1, LANES), jnp.float32)

    def narrow_step(start, amount):
        even_rows = pl.ds(2 * start, amount, stride=2)
        odd_rows = pl.ds(2 * start + 1, amount, stride=2)
        low_lanes = lax.broadcasted_iota(jnp.int32, (amount, LANES), 1) < LANES // 2
        even = [narrow_ref[part, even_rows, :] for part in range(3)]
        odd = [pltpu.roll(narrow_ref[part, odd_rows, :], LANES // 2, 1) for part in range(3)]
        joined = [
            even[0],
            even[1],
            jnp.where(low_lanes, even[2], odd[0]),
            jnp.where(low_lanes, odd[0], odd[1]),
            jnp.where(low_lanes, odd[1], odd[2]),
        ]
        for part in range(5):
            dense_ref[pl.ds(5 * start + part, amount, stride=5), :] = joined[part]

    for first, last in narrow_ranges(layout):
        for_chunks(first, last, PAIR_CHUNK, narrow_step)


def pack_grads(place, groups, parts):
    chips = lax.axis_size("fsdp")
    shard_count = lax.axis_size("dp") * chips
    layouts = [group[2] for group in groups]
    row_counts = [group[3] for group in groups]
    counts = [len(group[0]) for group in groups]

    def kernel(place_ref, *refs):
        out_refs = refs[sum(counts) : sum(counts) + len(parts)]
        dense_ref, narrow_ref = refs[-2:]
        first = 0
        for number, (operands, sources, layout, shard_rows) in enumerate(groups):
            in_refs = refs[first : first + len(operands)]
            first += len(operands)
            pack_group(layout, sources, in_refs, dense_ref, narrow_ref)

            def cut(index, carry, number=number, shard_rows=shard_rows):
                for out_ref, (pieces, core, turned) in zip(out_refs, parts):
                    out_row = 0
                    for group, first_row, rows in pieces:
                        if group == number:
                            chip = index ^ place_ref[1] if turned else index
                            shard = (place_ref[0] ^ core) * chips + chip
                            out_ref[index, out_row : out_row + rows, :] = dense_ref[
                                pl.ds(shard * shard_rows + first_row, rows), :
                            ].astype(out_ref.dtype)
                        out_row += rows
                return carry

            lax.fori_loop(0, chips, cut, 0)

    vmem_spec = pl.BlockSpec(memory_space=pltpu.VMEM)
    return pl.pallas_call(
        kernel,
        in_specs=[PLACE_SPEC] + [vmem_spec] * sum(counts),
        out_shape=[
            shaped((chips, sum(piece[2] for piece in pieces), LANES), WIRE_TYPE)
            for pieces, core, turned in parts
        ],
        scratch_shapes=work_scratch(layouts, row_counts, shard_count),
        compiler_params=PARAMS,
        name="pack_grads",
    )(place, *[operand for group in groups for operand in group[0]])


def add_rounded(kept, received):
    return (kept.astype(jnp.float32) + received.astype(jnp.float32)).astype(WIRE_TYPE)


def flat_rows(rows, shard_rows):
    return rows[:shard_rows].astype(jnp.float32).reshape(-1)


def sum_cores(parts):
    parts = list(parts)
    while len(parts) > 1:
        half = len(parts) // 2
        parts = [
            add_rounded(kept, swap(sent, "dp", half))
            for kept, sent in zip(parts[:half], parts[half:])
        ]
    return parts[0]


def scatter_half(parts, order):
    held = sum_cores(parts)
    left = sorted(order, reverse=True)
    held = held.reshape([2] * len(left) + list(held.shape[1:]))
    for bit in order:
        axis = left.index(bit)
        left.remove(bit)
        kept = lax.index_in_dim(held, 0, axis, keepdims=False)
        sent = lax.index_in_dim(held, 1, axis, keepdims=False)
        held = add_rounded(kept, swap(sent, "fsdp", bit))
    return held


def sum_devices(value):
    for axis in AXES:
        for bit in bit_orders(lax.axis_size(axis))[0]:
            value = value + swap(value, axis, bit)
    return value


def dot(left, right):
    return lax.dot_general(
        left, right, (((1,), (0,)), ((), ())), preferred_element_type=jnp.float32
    )


def dot_nt(left, right):
    return lax.dot_general(
        left, right, (((1,), (1,)), ((), ())), preferred_element_type=jnp.float32
    )


def dot_tn(left, right):
    return lax.dot_general(
        left, right, (((0,), (0,)), ((), ())), preferred_element_type=jnp.float32
    )


def rows_sum(values):
    return jnp.sum(values, axis=0, keepdims=True)


def norm_parts(values):
    centred = values - jnp.mean(values, axis=-1, keepdims=True)
    spread = jnp.mean(centred * centred, axis=-1, keepdims=True)
    scale = lax.rsqrt(spread + 1e-06)
    return centred * scale, scale


def norm_grad(unit, scale, gain_row, gradient):
    inner = gradient * gain_row
    first = jnp.mean(inner, axis=-1, keepdims=True)
    second = jnp.mean(inner * unit, axis=-1, keepdims=True)
    return scale * (inner - first - unit * second)


def column_mask(rows, lanes, side, width):
    places = lax.broadcasted_iota(jnp.int32, (rows, lanes), 0)
    return (places & (width - 1)) < side


def softmax_rows(query, key, valid):
    scores = jnp.where(valid, dot_nt(query, key) * 0.125, -1e30)
    powers = jnp.exp(scores - jnp.max(scores, axis=-1, keepdims=True))
    return powers * (1.0 / jnp.sum(powers, axis=-1, keepdims=True))


def split_lanes(values):
    rows, channels = values.shape
    pieces = []
    for first in range(0, channels, LANES):
        piece = values[:, first : min(first + LANES, channels)]
        if piece.shape[1] < LANES:
            rest = jnp.zeros((rows, LANES - piece.shape[1]), values.dtype)
            piece = jnp.concatenate([piece, rest], axis=1)
        pieces.append(piece)
    return pieces


def join_lanes(pieces, channels):
    return jnp.concatenate(pieces, axis=1)[:, :channels]


def softmax_columns(query, key, valid):
    scores = jnp.where(valid, dot_nt(key, query) * 0.125, -1e30)
    powers = jnp.exp(scores - jnp.max(scores, axis=0, keepdims=True))
    return powers * (1.0 / rows_sum(powers))


def pair_place(width, part):
    return pl.ds((part // 2) * width + part % 2, width // 2, stride=2)


def pair_part(grid_ref, width, part, channels):
    pieces = []
    for index in range(grid_ref.shape[0]):
        piece = grid_ref[index, :, pair_place(width, part), :]
        pieces.append(piece.reshape(piece.shape[0] * piece.shape[1], LANES))
    return join_lanes(pieces, channels).astype(jnp.bfloat16)


def attend_kernel(channels, side, width, has_reduction, *refs):
    if has_reduction:
        (
            x_ref, valid_ref, gain_ref, bias_ref, wq_ref, bq_ref, wr_ref, br_ref, rgain_ref,
            rbias_ref, wp_ref, bv_ref, wo_ref, bo_ref, gain2_ref, bias2_ref,
            query_ref, pair_ref, mixed_ref, middle_ref, normed_ref, reduced_ref, padded_ref,
            grid_ref, inputs_ref,
        ) = refs
    else:
        (
            x_ref, valid_ref, gain_ref, bias_ref, wq_ref, bq_ref,
            wp_ref, bv_ref, wo_ref, bo_ref, gain2_ref, bias2_ref,
            query_ref, pair_ref, mixed_ref, middle_ref, normed_ref,
        ) = refs
    inputs = x_ref[0].astype(jnp.float32)
    if has_reduction:
        for row in range(side):
            first = row * width
            inputs_ref[first : first + side, :] = inputs[row * side : (row + 1) * side]
            inputs_ref[first + side : first + width, :] = jnp.zeros(
                (width - side, channels), jnp.float32
            )
        inputs = inputs_ref[...]
        padded_ref[0] = inputs.astype(jnp.bfloat16)
    unit, _ = norm_parts(inputs)
    normed = (unit * gain_ref[...] + bias_ref[...]).astype(jnp.bfloat16)
    query_ref[0] = (dot(normed, wq_ref[...]) + bq_ref[...]).astype(jnp.bfloat16)
    if has_reduction:
        for index, piece in enumerate(split_lanes(normed.astype(jnp.float32))):
            grid_ref[index] = piece.reshape(grid_ref.shape[1:])
        reduced = br_ref[...]
        for part in range(4):
            reduced = reduced + dot(
                pair_part(grid_ref, width, part, channels),
                wr_ref[part * channels : (part + 1) * channels, :],
            )
        reduced_ref[0] = reduced
        unit, _ = norm_parts(reduced)
        source = (unit * rgain_ref[...] + rbias_ref[...]).astype(jnp.bfloat16)
    else:
        source = normed
    pair_ref[0, :, :channels] = dot(source, wp_ref[:, :channels]).astype(jnp.bfloat16)
    pair_ref[0, :, channels:] = (dot(source, wp_ref[:, channels:]) + bv_ref[...]).astype(
        jnp.bfloat16
    )
    valid = valid_ref[0] > 0.5
    for head in range(channels // HEAD):
        lanes = slice(head * HEAD, (head + 1) * HEAD)
        value_lanes = slice(channels + head * HEAD, channels + (head + 1) * HEAD)
        query = query_ref[0, :, lanes]
        key = pair_ref[0, :, lanes]
        value = pair_ref[0, :, value_lanes]
        if has_reduction:
            chances = softmax_columns(query, key, valid).astype(jnp.bfloat16)
            mixed = dot_tn(chances, value)
        else:
            chances = softmax_rows(query, key, valid).astype(jnp.bfloat16)
            mixed = dot(chances, value)
        mixed_ref[0, :, lanes] = mixed.astype(jnp.bfloat16)
    middle = inputs + (dot(mixed_ref[0], wo_ref[...]) + bo_ref[...])
    middle_ref[0] = middle
    unit, _ = norm_parts(middle)
    normed_ref[0] = (unit * gain2_ref[...] + bias2_ref[...]).astype(jnp.bfloat16)


def whole(shape):
    return pl.BlockSpec(shape, lambda *place: (0,) * len(shape))


def image_block(array):
    return pl.BlockSpec((1,) + array.shape[1:], lambda image: (image,) + (0,) * (len(array.shape) - 1))


def shaped(shape, kind):
    return jax.ShapeDtypeStruct(shape, kind)


PARAMS = pltpu.CompilerParams(vmem_limit_bytes=61000 * 1024)


def attend_block(inputs, valid, weights, side, width):
    images, _, channels = inputs.shape
    tokens = side * width
    has_reduction = len(weights) == 14
    keys = valid.shape[2]
    if has_reduction:
        valid = valid.swapaxes(1, 2)
    outs = [
        shaped((images, tokens, channels), jnp.bfloat16),
        shaped((images, keys, 2 * channels), jnp.bfloat16),
        shaped((images, tokens, channels), jnp.bfloat16),
        shaped((images, tokens, channels), jnp.float32),
        shaped((images, tokens, channels), jnp.bfloat16),
    ]
    scratch = []
    if has_reduction:
        outs.append(shaped((images, keys, channels), jnp.float32))
        outs.append(shaped((images, tokens, channels), jnp.bfloat16))
        grid_shape = (-(-channels // LANES), tokens // (2 * width), 2 * width, LANES)
        scratch.append(pltpu.VMEM(grid_shape, jnp.float32))
        scratch.append(pltpu.VMEM((tokens, channels), jnp.float32))
    return pl.pallas_call(
        lambda *refs: attend_kernel(channels, side, width, has_reduction, *refs),
        grid=(images,),
        in_specs=[image_block(inputs), image_block(valid)] + [whole(w.shape) for w in weights],
        out_specs=[image_block(out) for out in outs],
        out_shape=outs,
        scratch_shapes=scratch,
        compiler_params=PARAMS,
        name="attend",
    )(inputs, valid, *weights)


def zero_edges(ref, side, width, columns):
    tokens = side * width
    lanes = ref.shape[1]
    ref[0:width, :] = jnp.zeros((width, lanes), jnp.float32)
    ref[width + tokens : 2 * width + tokens, :] = jnp.zeros((width, lanes), jnp.float32)
    if columns:
        for row in range(1, side + 1):
            ref[row * width + side : (row + 1) * width, :] = jnp.zeros(
                (width - side, lanes), jnp.float32
            )


def store_cells(ref, values, side, width):
    for row in range(side):
        ref[0, row * side : (row + 1) * side, :] = values[row * width : row * width + side]


def mix_kernel(side, width, lanes, dense, *refs):
    (
        normed_ref, middle_ref, we_ref, be_ref, kd_ref, bd_ref, wc_ref, bc_ref,
        out_ref, mixed_ref, slope_ref, pad_ref,
    ) = refs
    tokens = side * width
    units = we_ref.shape[1]
    pad_ref[width : width + tokens, :] = dot(normed_ref[0], we_ref[...]) + be_ref[...]
    zero_edges(pad_ref, side, width, True)

    def step(row, carry):
        start = pl.multiple_of(row * width, width)
        for first in range(0, units, lanes):
            block = slice(first, first + lanes)
            rows = [pad_ref[pl.ds(start + up * width, width), block] for up in range(3)]
            sums = [
                kd_ref[col : col + 1, block] * rows[0]
                + kd_ref[3 + col : 4 + col, block] * rows[1]
                + kd_ref[6 + col : 7 + col, block] * rows[2]
                for col in range(3)
            ]
            value = (
                sums[1]
                + pltpu.roll(sums[0], 1, 0)
                + pltpu.roll(sums[2], width - 1, 0)
                + bd_ref[:, block]
            )
            share = 0.5 + 0.5 * lax.erf(value * math.sqrt(0.5))
            bell = jnp.exp(value * value * -0.5) * (1.0 / math.sqrt(2.0 * math.pi))
            mixed_ref[0, pl.ds(start, width), block] = (value * share).astype(jnp.bfloat16)
            slope_ref[0, pl.ds(start, width), block] = (share + value * bell).astype(jnp.bfloat16)
        return carry

    lax.fori_loop(0, side, step, 0)
    result = middle_ref[0] + bc_ref[...] + dot(mixed_ref[0], wc_ref[...])
    if dense:
        store_cells(out_ref, result, side, width)
    else:
        out_ref[0] = result


def mix_block(normed, middle, weights, side, width, lanes, dense):
    images, tokens, channels = middle.shape
    units = weights[0].shape[1]
    outs = [
        shaped((images, side * side if dense else tokens, channels), jnp.float32),
        shaped((images, tokens, units), jnp.bfloat16),
        shaped((images, tokens, units), jnp.bfloat16),
    ]
    return pl.pallas_call(
        lambda *refs: mix_kernel(side, width, lanes, dense, *refs),
        grid=(images,),
        in_specs=[image_block(normed), image_block(middle)] + [whole(w.shape) for w in weights],
        out_specs=[image_block(out) for out in outs],
        out_shape=outs,
        scratch_shapes=[pltpu.VMEM((tokens + 2 * width, units), jnp.float32)],
        compiler_params=PARAMS,
        name="mix",
    )(normed, middle, *weights)


def mix_back_kernel(side, width, lanes, *refs):
    (
        normed_ref, grad_ref, mixed_ref, slope_ref, we_ref, be_ref, kd_ref, wc_ref,
        dnormed_ref, dwe_ref, dwc_ref, drows_ref, pad_ref, dpad_ref, dhid_ref,
    ) = refs
    tokens = side * width
    units = we_ref.shape[1]
    gradient = grad_ref[0].astype(jnp.bfloat16)
    pad_ref[width : width + tokens, :] = dot(normed_ref[0], we_ref[...]) + be_ref[...]
    dpad_ref[width : width + tokens, :] = dot_nt(gradient, wc_ref[...]) * slope_ref[0].astype(
        jnp.float32
    )
    zero_edges(pad_ref, side, width, True)
    zero_edges(dpad_ref, side, width, False)

    @pl.when(pl.program_id(0) == 0)
    def _():
        for ref in (drows_ref, dwe_ref, dwc_ref):
            ref[...] = jnp.zeros(ref.shape, jnp.float32)

    inside = column_mask(width, lanes, side, width)

    def fold(values):
        total = values[0:8]
        for start in range(8, width, 8):
            total = total + values[start : start + 8]
        return total

    for first in range(0, units, lanes):
        block = slice(first, first + lanes)

        def step(row, sums, block=block):
            start = pl.multiple_of(row * width, width)
            rows = [pad_ref[pl.ds(start + up * width, width), block] for up in range(3)]
            drows = [dpad_ref[pl.ds(start + up * width, width), block] for up in range(3)]
            turned = [
                pltpu.roll(drows[1], width - 1, 0),
                drows[1],
                pltpu.roll(drows[1], 1, 0),
            ]
            found = []
            for up in range(3):
                for col in range(3):
                    found.append(sums[3 * up + col] + fold(turned[col] * rows[up]))
            found.append(sums[9] + fold(drows[1]))
            parts = [
                kd_ref[col : col + 1, block] * drows[2]
                + kd_ref[3 + col : 4 + col, block] * drows[1]
                + kd_ref[6 + col : 7 + col, block] * drows[0]
                for col in range(3)
            ]
            value = parts[1] + pltpu.roll(parts[0], width - 1, 0) + pltpu.roll(parts[2], 1, 0)
            value = jnp.where(inside, value, 0.0)
            dhid_ref[pl.ds(start, width), block] = value.astype(jnp.bfloat16)
            found.append(sums[10] + fold(value))
            return tuple(found)

        zero = jnp.zeros((8, lanes), jnp.float32)
        totals = lax.fori_loop(0, side, step, (zero,) * 11, unroll=2)
        for index in range(11):
            drows_ref[index : index + 1, block] += rows_sum(totals[index])
    dhidden = dhid_ref[...]
    dwe_ref[...] += dot_tn(normed_ref[0], dhidden)
    dwc_ref[...] += dot_tn(mixed_ref[0], gradient)
    dnormed_ref[0] = dot_nt(dhidden, we_ref[...])


def mix_back(normed, gradient, mixed, slope, weights, side, width, lanes):
    we, be, kd, bd, wc, bc = weights
    images, tokens, channels = normed.shape
    units = we.shape[1]
    operands = [normed, gradient, mixed, slope]
    used = [we, be, kd, wc]
    outs = [
        shaped((images, tokens, channels), jnp.float32),
        shaped((channels, units), jnp.float32),
        shaped((units, channels), jnp.float32),
        shaped((16, units), jnp.float32),
    ]
    return pl.pallas_call(
        lambda *refs: mix_back_kernel(side, width, lanes, *refs),
        grid=(images,),
        in_specs=[image_block(op) for op in operands] + [whole(u.shape) for u in used],
        out_specs=[image_block(outs[0])] + [whole(out.shape) for out in outs[1:]],
        out_shape=outs,
        scratch_shapes=[
            pltpu.VMEM((tokens + 2 * width, units), jnp.float32),
            pltpu.VMEM((tokens + 2 * width, units), jnp.float32),
            pltpu.VMEM((tokens, units), jnp.bfloat16),
        ],
        compiler_params=PARAMS,
        name="mix_back",
    )(*operands, *used)


def attend_back_kernel(channels, side, width, has_reduction, *refs):
    if has_reduction:
        (
            x_ref, valid_ref, grad_ref, dnormed_ref, middle_ref, query_ref, pair_ref, mixed_ref,
            reduced_ref, gain_ref, bias_ref, wq_ref, wr_ref, rgain_ref, rbias_ref, wp_ref, wo_ref,
            gain2_ref,
            dx_ref, dwq_ref, dwp_ref, dwo_ref, vec_ref, dwr_ref,
            dquery_ref, dpair_ref, dmiddle_ref, grid_ref, dgrid_ref,
        ) = refs
    else:
        (
            x_ref, valid_ref, grad_ref, dnormed_ref, middle_ref, query_ref, pair_ref, mixed_ref,
            gain_ref, bias_ref, wq_ref, wp_ref, wo_ref, gain2_ref,
            dx_ref, dwq_ref, dwp_ref, dwo_ref, vec_ref,
            dquery_ref, dpair_ref, dmiddle_ref,
        ) = refs

    @pl.when(pl.program_id(0) == 0)
    def _():
        sums = [dwq_ref, dwp_ref, dwo_ref, vec_ref] + ([dwr_ref] if has_reduction else [])
        for ref in sums:
            ref[...] = jnp.zeros(ref.shape, jnp.float32)

    def add_row(index, row):
        vec_ref[index : index + 1, :] += row

    gradient = grad_ref[0].astype(jnp.float32)
    add_row(0, rows_sum(gradient.astype(jnp.bfloat16).astype(jnp.float32)))
    dnormed = dnormed_ref[0]
    unit, scale = norm_parts(middle_ref[0])
    add_row(1, rows_sum(dnormed * unit))
    add_row(2, rows_sum(dnormed))
    dmiddle = gradient + norm_grad(unit, scale, gain2_ref[...], dnormed)
    dmiddle_ref[...] = dmiddle
    doutput = dmiddle.astype(jnp.bfloat16)
    add_row(3, rows_sum(doutput.astype(jnp.float32)))
    dwo_ref[...] += dot_tn(mixed_ref[0], doutput)
    dmixed = dot_nt(doutput, wo_ref[...]).astype(jnp.bfloat16)
    valid = valid_ref[0] > 0.5
    for head in range(channels // HEAD):
        lanes = slice(head * HEAD, (head + 1) * HEAD)
        value_lanes = slice(channels + head * HEAD, channels + (head + 1) * HEAD)
        query = query_ref[0, :, lanes]
        key = pair_ref[0, :, lanes]
        chances = softmax_columns(query, key, valid)
        dhead = dmixed[:, lanes]
        dchances = dot_nt(pair_ref[0, :, value_lanes], dhead)
        dpair_ref[:, value_lanes] = dot(chances.astype(jnp.bfloat16), dhead).astype(jnp.bfloat16)
        weighted = chances * dchances
        dscores = (weighted - chances * rows_sum(weighted)).astype(jnp.bfloat16)
        dquery_ref[:, lanes] = (dot_tn(dscores, key) * 0.125).astype(jnp.bfloat16)
        dpair_ref[:, lanes] = (dot(dscores, query) * 0.125).astype(jnp.bfloat16)
    dquery = dquery_ref[...]
    dpair = dpair_ref[...]
    unit, scale = norm_parts(x_ref[0].astype(jnp.float32))
    normed = (unit * gain_ref[...] + bias_ref[...]).astype(jnp.bfloat16)
    add_row(4, rows_sum(dquery.astype(jnp.float32)))
    add_row(5, rows_sum(dpair[:, channels:].astype(jnp.float32)))
    dwq_ref[...] += dot_tn(normed, dquery)
    total = dot_nt(dquery, wq_ref[...])
    dsource = dot_nt(dpair, wp_ref[...])
    if has_reduction:
        runit, rscale = norm_parts(reduced_ref[0])
        source = (runit * rgain_ref[...] + rbias_ref[...]).astype(jnp.bfloat16)
        dwp_ref[...] += dot_tn(source, dpair)
        add_row(8, rows_sum(dsource * runit))
        add_row(9, rows_sum(dsource))
        dreduced = norm_grad(runit, rscale, rgain_ref[...], dsource).astype(jnp.bfloat16)
        add_row(10, rows_sum(dreduced.astype(jnp.float32)))
        for index, piece in enumerate(split_lanes(normed.astype(jnp.float32))):
            grid_ref[index] = piece.reshape(grid_ref.shape[1:])
        for index, piece in enumerate(split_lanes(total)):
            dgrid_ref[index] = piece.reshape(dgrid_ref.shape[1:])
        for part in range(4):
            rows = slice(part * channels, (part + 1) * channels)
            dwr_ref[rows, :] += dot_tn(pair_part(grid_ref, width, part, channels), dreduced)
            for index, piece in enumerate(split_lanes(dot_nt(dreduced, wr_ref[rows, :]))):
                dgrid_ref[index, :, pair_place(width, part), :] += piece.reshape(
                    dgrid_ref.shape[1], width // 2, LANES
                )
        total = join_lanes(
            [dgrid_ref[index].reshape(total.shape[0], LANES) for index in range(dgrid_ref.shape[0])],
            channels,
        )
    else:
        dwp_ref[...] += dot_tn(normed, dpair)
        total = total + dsource
    add_row(6, rows_sum(total * unit))
    add_row(7, rows_sum(total))
    result = dmiddle_ref[...] + norm_grad(unit, scale, gain_ref[...], total)
    if has_reduction:
        store_cells(dx_ref, result, side, width)
    else:
        dx_ref[0] = result


def attend_back(inputs, valid, gradient, dnormed, saved, weights, side, width):
    query, pair, mixed, middle, normed = saved[:5]
    images, tokens, channels = middle.shape
    has_reduction = len(saved) > 5
    keys = valid.shape[2]
    operands = [inputs, valid.swapaxes(1, 2), gradient, dnormed, middle, query, pair, mixed]
    outs = [
        shaped((images, side * side if has_reduction else tokens, channels), jnp.float32),
        shaped((channels, channels), jnp.float32),
        shaped((channels, 2 * channels), jnp.float32),
        shaped((channels, channels), jnp.float32),
        shaped((16, channels), jnp.float32),
    ]
    scratch = [
        pltpu.VMEM((tokens, channels), jnp.bfloat16),
        pltpu.VMEM((keys, 2 * channels), jnp.bfloat16),
        pltpu.VMEM((tokens, channels), jnp.float32),
    ]
    if has_reduction:
        gain, bias, wq, bq, wr, br, rgain, rbias, wp, bv, wo, bo, gain2, bias2 = weights
        used = [gain, bias, wq, wr, rgain, rbias, wp, wo, gain2]
        operands.append(saved[5])
        outs.append(shaped((4 * channels, channels), jnp.float32))
        grid_shape = (-(-channels // LANES), tokens // (2 * width), 2 * width, LANES)
        scratch += [pltpu.VMEM(grid_shape, jnp.float32), pltpu.VMEM(grid_shape, jnp.float32)]
    else:
        gain, bias, wq, bq, wp, bv, wo, bo, gain2, bias2 = weights
        used = [gain, bias, wq, wp, wo, gain2]
    return pl.pallas_call(
        lambda *refs: attend_back_kernel(channels, side, width, has_reduction, *refs),
        grid=(images,),
        in_specs=[image_block(op) for op in operands] + [whole(w.shape) for w in used],
        out_specs=[image_block(outs[0])] + [whole(out.shape) for out in outs[1:]],
        out_shape=outs,
        scratch_shapes=scratch,
        compiler_params=PARAMS,
        name="attend_back",
    )(*operands, *used)


def tap_place(width, tap, row):
    first = LEAD + (tap // 3) * width + tap % 3 - 1
    return pl.ds(first + 2 * width * row, width // 2, stride=2)


def load_tap(grid_ref, side, width, tap, channels):
    pieces = []
    for index in range(grid_ref.shape[0]):
        rows = [grid_ref[index, tap_place(width, tap, row), :] for row in range(side // 2)]
        pieces.append(jnp.concatenate(rows, axis=0))
    return join_lanes(pieces, channels).astype(jnp.bfloat16)


def fill_grid(grid_ref, values, width):
    rows = grid_ref.shape[1]
    first = LEAD + width
    last = first + values.shape[0]
    for index, piece in enumerate(split_lanes(values)):
        grid_ref[index, 0:first, :] = jnp.zeros((first, LANES), jnp.float32)
        grid_ref[index, first:last, :] = piece
        grid_ref[index, last:rows, :] = jnp.zeros((rows - last, LANES), jnp.float32)


LEAD = 8


def embed_kernel(side, width, *refs):
    x_ref, gain_ref, bias_ref, w_ref, b_ref, pgain_ref, pbias_ref = refs[:7]
    out_ref, patch_ref, grid_ref = refs[7:]
    tokens, channels = x_ref.shape[1:]
    unit, _ = norm_parts(x_ref[0])
    normed = (unit * gain_ref[...] + bias_ref[...]).astype(jnp.bfloat16).astype(jnp.float32)
    inside = column_mask(tokens, channels, side, width)
    fill_grid(grid_ref, jnp.where(inside, normed, 0.0), width)
    patch = b_ref[...]
    for tap in range(9):
        patch = patch + dot(
            load_tap(grid_ref, side, width, tap, channels),
            w_ref[tap * channels : (tap + 1) * channels, :]
        )
    patch_ref[0] = patch
    unit, _ = norm_parts(patch)
    out_ref[0] = unit * pgain_ref[...] + pbias_ref[...]


def embed_block(inputs, weights, side, width):
    images, tokens, channels = inputs.shape
    units = weights[2].shape[1]
    outs = [shaped((images, tokens // 4, units), jnp.float32)] * 2
    return pl.pallas_call(
        lambda *refs: embed_kernel(side, width, *refs),
        grid=(images,),
        in_specs=[image_block(inputs)] + [whole(w.shape) for w in weights],
        out_specs=[image_block(out) for out in outs],
        out_shape=outs,
        scratch_shapes=[pltpu.VMEM((-(-channels // LANES), LEAD + (side + 3) * width, LANES), jnp.float32)],
        compiler_params=PARAMS,
        name="embed",
    )(inputs, *weights)


def embed_back_kernel(side, width, *refs):
    x_ref, grad_ref, patch_ref, gain_ref, bias_ref, w_ref, pgain_ref = refs[:7]
    dx_ref, dw_ref, vec_ref, pvec_ref, grid_ref, dgrid_ref = refs[7:]
    tokens, channels = x_ref.shape[1:]

    @pl.when(pl.program_id(0) == 0)
    def _():
        for ref in (dw_ref, vec_ref, pvec_ref):
            ref[...] = jnp.zeros(ref.shape, jnp.float32)

    gradient = grad_ref[0]
    punit, pscale = norm_parts(patch_ref[0])
    pvec_ref[0:1, :] += rows_sum(gradient * punit)
    pvec_ref[1:2, :] += rows_sum(gradient)
    dpatch = norm_grad(punit, pscale, pgain_ref[...], gradient).astype(jnp.bfloat16)
    pvec_ref[2:3, :] += rows_sum(dpatch.astype(jnp.float32))
    unit, scale = norm_parts(x_ref[0])
    normed = (unit * gain_ref[...] + bias_ref[...]).astype(jnp.bfloat16).astype(jnp.float32)
    inside = column_mask(tokens, channels, side, width)
    fill_grid(grid_ref, jnp.where(inside, normed, 0.0), width)
    dgrid_ref[...] = jnp.zeros(dgrid_ref.shape, jnp.float32)
    half = width // 2
    for tap in range(9):
        rows = slice(tap * channels, (tap + 1) * channels)
        dw_ref[rows, :] += dot_tn(load_tap(grid_ref, side, width, tap, channels), dpatch)
        for index, piece in enumerate(split_lanes(dot_nt(dpatch, w_ref[rows, :]))):
            for row in range(side // 2):
                dgrid_ref[index, tap_place(width, tap, row), :] += piece[
                    row * half : (row + 1) * half, :
                ]
    first = LEAD + width
    pieces = [dgrid_ref[index, first : first + tokens, :] for index in range(dgrid_ref.shape[0])]
    total = jnp.where(inside, join_lanes(pieces, channels), 0.0)
    vec_ref[0:1, :] += rows_sum(total * unit)
    vec_ref[1:2, :] += rows_sum(total)
    dx_ref[0] = norm_grad(unit, scale, gain_ref[...], total)


def embed_back(inputs, gradient, patch, weights, side, width):
    gain, bias, w, b, pgain, pbias = weights
    images, tokens, channels = inputs.shape
    units = w.shape[1]
    outs = [
        shaped(inputs.shape, jnp.float32),
        shaped(w.shape, jnp.float32),
        shaped((8, channels), jnp.float32),
        shaped((8, units), jnp.float32),
    ]
    operands = [inputs, gradient, patch]
    used = [gain, bias, w, pgain]
    grid_scratch = pltpu.VMEM((-(-channels // LANES), LEAD + (side + 3) * width, LANES), jnp.float32)
    return pl.pallas_call(
        lambda *refs: embed_back_kernel(side, width, *refs),
        grid=(images,),
        in_specs=[image_block(op) for op in operands] + [whole(u.shape) for u in used],
        out_specs=[image_block(outs[0])] + [whole(out.shape) for out in outs[1:]],
        out_shape=outs,
        scratch_shapes=[grid_scratch, grid_scratch],
        compiler_params=PARAMS,
        name="embed_back",
    )(*operands, *used)


def to_grid(values, side, width):
    images, tokens, channels = values.shape
    grid = values.reshape(images, side, side, channels)
    grid = jnp.pad(grid, ((0, 0), (0, 0), (0, width - side), (0, 0)))
    return grid.reshape(images, side * width, channels)


def key_mask(row_counts, col_counts, side, width):
    places = jnp.arange(side * width, dtype=jnp.int32)
    valid = ((places // width)[None, :] < row_counts[:, None]) & (
        (places % width)[None, :] < col_counts[:, None]
    )
    return valid.astype(jnp.float32)[:, None, :]


def block_sources(has_reduction):
    reduction = [(7, 0), (3, 10), (3, 8), (3, 9)] if has_reduction else []
    return (
        [(3, 6), (3, 7), (0, 0), (3, 4)]
        + reduction
        + [(1, 0), (3, 5), (2, 0), (3, 3), (3, 1), (3, 2)]
        + [(4, 0), (6, 10), (6, 0), (6, 9), (5, 0), (3, 0)]
    )


EMBED_SOURCES = [(1, 0), (1, 1), (0, 0), (2, 2), (2, 0), (2, 1)]


def adamw_update(weights, mean_old, square_old, gradient, clip_factor, rate_value, fix_one):
    clipped = gradient * clip_factor
    mean_new = 0.5 * mean_old + 0.5 * clipped
    square_new = 0.5 * square_old + 0.5 * clipped * clipped
    updated = weights * (1.0 - rate_value * 0.05) - rate_value * (mean_new / fix_one) / (
        jnp.sqrt(square_new / fix_one) + 1e-08
    )
    return (updated, mean_new, square_new)


def shards(
    features,
    key_rows,
    key_cols,
    out_grad,
    lower_weights,
    lower_mean,
    lower_square,
    embed_weights,
    embed_mean,
    embed_square,
    upper_weights,
    upper_mean,
    upper_square,
    learn_rate,
):
    side, half = GRID, GRID // 2
    width = round_up(side, 32)
    half_width = width // 2
    key_valid = key_mask(key_rows, key_cols, half, half_width)
    cores = lax.axis_size("dp")
    orders = bit_orders(lax.axis_size("fsdp"))
    place = device_place()
    lower_rows, embed_rows, upper_rows = (
        flat.shape[0] // LANES for flat in (lower_weights, embed_weights, upper_weights)
    )
    rest_local = jnp.concatenate([local_rows(embed_weights), local_rows(upper_weights)], axis=0)
    lower_halves, grad_in = gather_halves(
        local_rows(lower_weights),
        [order[2:] + order[:2] for order in orders],
        to_grid(out_grad, half, half_width),
    )
    *lower_halves, rest_local = lax.optimization_barrier((*lower_halves, rest_local))
    rest = lax.all_gather(rest_local, AXES, axis=0, tiled=False)
    lower = unpack_halves(
        lower_halves, place, LOWER_LAYOUT, lower_rows, [order[2:] + order[:2] for order in orders]
    )
    embed, upper = unpack_joined(rest, [EMBED_LAYOUT, UPPER_LAYOUT], [embed_rows, upper_rows])

    lower_saved = attend_block(features, key_valid, lower[:14], side, width)
    three_in = lower_saved[6]
    section_three, lower_mixed, lower_slope = mix_block(
        lower_saved[4], lower_saved[3], lower[14:], side, width, 256, False
    )
    section_four, patch = embed_block(section_three, embed, side, width)
    upper_saved = attend_block(section_four, key_valid, upper[:10], half, half_width)
    block_out, upper_mixed, upper_slope = mix_block(
        upper_saved[4], upper_saved[3], upper[10:], half, half_width, 256, True
    )

    def back(inputs, gradient, saved, mixed, slope, weights, first, side, width, lanes):
        dnormed, dwe, dwc, drows = mix_back(
            saved[4], gradient, mixed, slope, weights[first:], side, width, lanes
        )
        dx, dwq, dwp, dwo, vec, *rest = attend_back(
            inputs, key_valid, gradient, dnormed, saved, weights[:first], side, width
        )
        return dx, [dwq, dwp, dwo, vec, dwe, dwc, drows] + rest

    four_grad, upper_found = back(
        section_four, grad_in, upper_saved, upper_mixed, upper_slope, upper, 10, half, half_width, 256
    )
    upper_wire = pack_grads(
        place,
        [(upper_found, block_sources(False), UPPER_LAYOUT, upper_rows)],
        [([(0, 0, round_up(upper_rows, 16))], core, False) for core in range(cores)],
    )
    *upper_wire, four_grad = lax.optimization_barrier((*upper_wire, four_grad))
    three_grad, *embed_found = embed_back(section_three, four_grad, patch, embed, side, width)
    embed_wire = pack_grads(
        place,
        [(embed_found, EMBED_SOURCES, EMBED_LAYOUT, embed_rows)],
        [([(0, 0, round_up(embed_rows, 16))], core, False) for core in range(cores)],
    )
    rest_sum = jnp.concatenate([sum_cores(embed_wire), sum_cores(upper_wire)], axis=1)
    rest_sum, three_grad = lax.optimization_barrier((rest_sum, three_grad))
    rest_grad = lax.psum_scatter(rest_sum, "fsdp", scatter_dimension=0, tiled=False)
    input_grad, lower_found = back(
        three_in, three_grad, lower_saved, lower_mixed, lower_slope, lower, 14, side, width, 256
    )
    padded_rows = round_up(lower_rows, 16)
    half_rows = padded_rows // 32 * 16
    parts = []
    for first, rows in ((0, half_rows), (half_rows, padded_rows - half_rows)):
        parts += [([(0, first, rows)], core, True) for core in range(cores)]
    wire = pack_grads(
        place, [(lower_found, block_sources(True), LOWER_LAYOUT, lower_rows)], parts
    )
    lower_sum = jnp.concatenate(
        [scatter_half(wire[:cores], orders[0]), scatter_half(wire[cores:], orders[1])], axis=0
    )
    lower_grad = flat_rows(lower_sum, lower_rows)
    embed_grad = flat_rows(rest_grad, embed_rows)
    upper_grad = flat_rows(rest_grad[round_up(embed_rows, 16) :], upper_rows)
    local_squares = (
        jnp.sum(lower_grad * lower_grad)
        + jnp.sum(embed_grad * embed_grad)
        + jnp.sum(upper_grad * upper_grad)
    )
    squares = sum_devices(local_squares.reshape(1, 1))[0, 0]
    grad_norm = jnp.sqrt(squares)
    clip_factor = jnp.minimum(1.0, 5.0 / (grad_norm + 1e-06))
    rate_value = learn_rate[0]
    fix_one = 1.0 - 0.5**ADAM_STEP
    lower_new, lower_mean_new, lower_square_new = adamw_update(
        lower_weights, lower_mean, lower_square, lower_grad, clip_factor, rate_value, fix_one
    )
    embed_new, embed_mean_new, embed_square_new = adamw_update(
        embed_weights, embed_mean, embed_square, embed_grad, clip_factor, rate_value, fix_one
    )
    upper_new, upper_mean_new, upper_square_new = adamw_update(
        upper_weights, upper_mean, upper_square, upper_grad, clip_factor, rate_value, fix_one
    )
    return (
        block_out,
        input_grad,
        grad_norm.reshape(1),
        lower_grad,
        lower_new,
        lower_mean_new,
        lower_square_new,
        lower_new.astype(jnp.bfloat16),
        embed_grad,
        embed_new,
        embed_mean_new,
        embed_square_new,
        embed_new.astype(jnp.bfloat16),
        upper_grad,
        upper_new,
        upper_mean_new,
        upper_square_new,
        upper_new.astype(jnp.bfloat16),
    )


AXES = ("dp", "fsdp")
TOKENS = P(AXES, None, None)
FLAT = P(AXES)


def solution(mesh):
    return jax.shard_map(
        shards,
        mesh=mesh,
        in_specs=(
            TOKENS,
            FLAT,
            FLAT,
            TOKENS,
            FLAT,
            FLAT,
            FLAT,
            FLAT,
            FLAT,
            FLAT,
            FLAT,
            FLAT,
            FLAT,
            P(),
        ),
        out_specs=(
            TOKENS,
            TOKENS,
            P(),
            FLAT,
            FLAT,
            FLAT,
            FLAT,
            FLAT,
            FLAT,
            FLAT,
            FLAT,
            FLAT,
            FLAT,
            FLAT,
            FLAT,
            FLAT,
            FLAT,
            FLAT,
        ),
        check_vma=False,
    )
```
